32 devices in a mesh: prompt: 2 (over y), tensor: 4 (over z), ctx: 4 (over x, core).
Axes of the slice: x: 2, y: 2, z: 4, core: 2. Of those that a mesh axis runs over, the one named last changes fastest.
Arguments:
- hidden_in: bfloat16 [2048, 8192], P(('prompt', 'ctx', 'tensor')), parts along dimension 0, may hold values from -6 to 6
- norm_gain: float32 [8192], replicated, may hold values from 0.1 to 1.9
- weight_in: bfloat16 [8192, 3, 4096], P('ctx', None, 'tensor'), may hold values from -0.0625 to 0.0625
- filter_taps: float32 [256, 128], P('tensor'), may hold values from -0.6 to 0.6
- filter_decay: float32 [256], P('tensor'), may hold values from 0.003 to 0.3
- skip_gain: float32 [4096], P('tensor'), may hold values from -1 to 1
- tail_cache: bfloat16 [254, 4096], P('prompt', 'tensor'), parts along dimension 0, may hold values from -6 to 6
- output_weight: bfloat16 [4096, 8192], P(None, 'tensor'), may hold values from -0.09375 to 0.09375
Outputs:
- mixer_output: bfloat16 [2048, 8192], P(('prompt', 'ctx'), 'tensor'), parts along dimension 0
The draws below stay inside these ranges and needn't reach their ends.
There are 2 independent parts, one for each index of `prompt`. The reference program is written for one: setup_inputs(seed, part) draws one part's arguments, and reference() takes and returns one part's arrays. A program takes and returns all parts, laid end to end along the dimension named above; an argument that names none is the same for every part. Nothing has to cross between parts.
All inputs are finite; a program needn't handle non-finite values.
Results may differ from the reference program's by a relative error of at most 0.0095.
Values may be sent and summed in bfloat16 or wider, within the bound.
A program may use at most 256 MiB of HBM per device.

```python
import math
import jax
import jax.numpy as jnp
from jax import lax

D = 8192
C = 4096
GROUP = 16
TAPS = 128
GROUPS = 256
TOKENS = 1024


def levels(rng, extent, pieces, low, high):
    factor_of = 1.0
    for dim, blocks in pieces:
        heights = jax.random.uniform(jax.random.fold_in(jax.random.fold_in(rng, 6), dim), (blocks,), jnp.float32, low / len(pieces), high / len(pieces))
        factor_of = factor_of * jnp.repeat(jnp.exp(heights), extent[dim] // blocks).reshape((-1,) + (1,) * (len(extent) - 1 - dim))
    return factor_of


def bell_draw(stream_key, shape, scale, most, cuts=(), held_as=jnp.bfloat16):
    array = jax.random.normal(stream_key, shape, jnp.float32) * scale
    if len(cuts) > 0:
        array = levels(stream_key, shape, cuts, -0.22, 0.18) * array
    return jnp.clip(array, min=-most, max=most).astype(held_as)


def setup_inputs(seed: int = 0, part: int = 0) -> dict:
    key_list = jax.random.split(jax.random.key(seed), 9)
    part_splits = jax.random.split(jax.random.fold_in(key_list[8], part), 9)
    hidden_in = bell_draw(part_splits[0], (TOKENS, D), 1.0, 6.0, ((0, 16),))
    norm_gain = jnp.clip(1.0 + 0.18 * jax.random.normal(key_list[1], (D,), jnp.float32), 0.1, 1.9)
    weight_in = bell_draw(key_list[2], (D, 3, C), D ** -0.5, 0.0625, ((0, 4), (2, 4)))
    filter_taps = bell_draw(key_list[3], (GROUPS, TAPS), 0.1, 0.6, ((0, 4),), jnp.float32)
    filter_decay = jnp.clip(jnp.exp(math.log(0.3) - 4.6051702 * jax.random.uniform(key_list[4], (GROUPS,), jnp.float32) ** levels(key_list[4], (GROUPS,), ((0, 4),), -0.2, 0.2)), 0.003, 0.3)
    skip_gain = jnp.clip(jax.random.uniform(key_list[5], (C,), jnp.float32, -1.0, 1.0) * levels(key_list[5], (C,), ((0, 4),), -0.4, 0.0), -1.0, 1.0)
    tail_cache = bell_draw(part_splits[6], (TAPS - 1, C), 1.0, 6.0, ((1, 4),))
    output_weight = bell_draw(key_list[7], (C, D), C ** -0.5, 0.09375, ((1, 4),))
    return dict(hidden_in=hidden_in, norm_gain=norm_gain, weight_in=weight_in, filter_taps=filter_taps, filter_decay=filter_decay, skip_gain=skip_gain, tail_cache=tail_cache, output_weight=output_weight)


def normalize_rows(hidden_in, norm_gain):
    values = hidden_in.astype(jnp.float32)
    scaled = lax.rsqrt(lax.optimization_barrier(jnp.mean(values * values, axis=-1, keepdims=True)) + 1e-06)
    return (values * scaled * norm_gain[None, :]).astype(jnp.bfloat16)

def reference(hidden_in, norm_gain, weight_in, filter_taps, filter_decay, skip_gain, tail_cache, output_weight):
    normed = normalize_rows(hidden_in, norm_gain)
    qkv = jnp.dot(normed, weight_in.reshape(D, 3 * C), preferred_element_type=jnp.float32).reshape(TOKENS, 3, C)
    query = qkv[:, 0]
    product = (qkv[:, 1] * qkv[:, 2]).astype(jnp.bfloat16)
    lags = jnp.arange(TAPS).astype(jnp.float32)
    taps_full = filter_taps * jnp.exp(-filter_decay[:, None] * lags[None, :])
    channel_taps = jnp.repeat(taps_full, GROUP, axis=0)
    extended = jnp.concatenate([tail_cache, product], axis=0).astype(jnp.float32)

    def add_tap(position, running):
        weights = lax.dynamic_index_in_dim(channel_taps, position, 1, keepdims=False)
        shifted = lax.dynamic_slice_in_dim(extended, (TAPS - 1 - position).astype(jnp.int32), TOKENS, 0)
        return running + weights[None, :] * shifted
    filtered = lax.fori_loop(0, TAPS, add_tap, jnp.zeros((TOKENS, C), jnp.float32))
    gated = (query * (filtered + skip_gain[None, :] * product.astype(jnp.float32))).astype(jnp.bfloat16)
    return jnp.dot(gated, output_weight, preferred_element_type=jnp.float32).astype(jnp.bfloat16)
```

```python
import functools

import jax
import jax.numpy as jnp
from jax import lax
from jax.experimental import pallas as pl
from jax.experimental.pallas import tpu as pltpu
from jax.sharding import PartitionSpec as P

GROUP = 16
LANES = 128
MESH = pl.DeviceIdType.MESH


def span(index, size):
    return pl.ds(pl.multiple_of(index * size, size), size)


def greet(peers):
    barrier = pltpu.get_barrier_semaphore()
    for axis, peer, there in peers:

        @pl.when(there)
        def _(axis=axis, peer=peer):
            pl.semaphore_signal(barrier, inc=1, device_id={axis: peer}, device_id_type=MESH)

    return sum(jnp.where(there, 1, 0) for _, _, there in peers)


def normalize_rows(hidden_ref, gain_ref, normed):
    rows, width = hidden_ref.shape
    few, part = min(16, rows), 1024

    def step(index, carry):
        where = span(index, few)

        def values(start):
            return hidden_ref[where, pl.ds(start, part)].astype(jnp.float32)

        squares = jnp.zeros((few, part), jnp.float32)
        for start in range(0, width, part):
            squares = squares + values(start) * values(start)
        scaled = lax.rsqrt(jnp.sum(squares, axis=-1, keepdims=True) / width + 1e-06)
        for start in range(0, width, part):
            inner = pl.ds(start, part)
            normed[where, inner] = (values(start) * scaled * gain_ref[:, inner]).astype(
                jnp.bfloat16
            )
        return carry

    lax.fori_loop(0, rows // few, step, 0)


def first_rows(taps_ref, decay_ref):
    groups, taps = taps_ref.shape
    lags = lax.broadcasted_iota(jnp.int32, (groups, taps), 1).astype(jnp.float32)
    across = lax.broadcasted_iota(jnp.int32, (groups, groups), 1)
    down = lax.broadcasted_iota(jnp.int32, (groups, groups), 0)
    decay = jnp.sum(jnp.where(across == down, decay_ref[...], 0.0), axis=1, keepdims=True)
    taps_full = (taps_ref[...] * jnp.exp(-decay * lags)).astype(jnp.bfloat16)
    lag = lax.broadcasted_iota(jnp.int32, (taps, 2 * taps), 0)
    column = lax.broadcasted_iota(jnp.int32, (taps, 2 * taps), 1)
    turned = jnp.where(lag + column == taps, 1.0, 0.0).astype(jnp.bfloat16)
    return jnp.dot(taps_full, turned, preferred_element_type=jnp.float32)


class Line:
    def __init__(self, count, pieces, view, send_sem, recv_sem):
        self.count, self.pieces, self.view = count, pieces, view
        self.send_sem, self.recv_sem = send_sem, recv_sem
        self.place = lax.axis_index("tensor")

    def inside(self, position):
        return (position >= 0) & (position < self.count)

    def hop(self, origin, piece, up, source=None):
        ref = self.view(origin, piece)
        return pltpu.make_async_remote_copy(
            src_ref=ref if source is None else source,
            dst_ref=ref,
            send_sem=self.send_sem.at[up, origin, piece],
            recv_sem=self.recv_sem.at[origin, piece],
            device_id={"tensor": jnp.clip(self.place + 2 * up - 1, 0, self.count - 1)},
            device_id_type=MESH,
        )

    def send(self, origin, piece, up, source=None):
        @pl.when(self.inside(self.place + 2 * up - 1))
        def _():
            self.hop(origin, piece, up, source).start()

    def pass_on(self, distance, piece, up):
        origin = self.place - distance * (2 * up - 1)

        @pl.when(self.inside(origin))
        def _():
            source = jnp.clip(origin, 0, self.count - 1)
            self.hop(source, piece, up).wait_recv()
            self.send(source, piece, up)

    def sent(self):
        def step(index, carry):
            origin, piece = index // self.pieces, lax.rem(index, self.pieces)

            @pl.when((origin <= self.place) & (self.place + 1 < self.count))
            def _():
                self.hop(origin, piece, 1).wait_send()

            @pl.when((origin >= self.place) & (self.place > 0))
            def _():
                self.hop(origin, piece, 0).wait_send()

            return carry

        lax.fori_loop(0, self.count * self.pieces, step, 0)


def mixer_kernel(
    shards,
    parts,
    hidden_ref,
    gain_ref,
    planes_ref,
    taps_ref,
    decay_ref,
    skip_ref,
    tail_ref,
    weight_ref,
    out_ref,
    normed,
    first,
    planes,
    slots,
    partial,
    arrived,
    filtered,
    product,
    before,
    bands,
    weight,
    gated,
    total,
    load_sem,
    own_sem,
    swap_send,
    swap_recv,
    line_send,
    line_recv,
    sum_send,
    sum_recv,
    tail_send,
    tail_recv,
    gated_send,
    gated_recv,
):
    rows = hidden_ref.shape[0]
    _, depth, channels = planes.shape
    groups, taps, _ = bands.shape
    chunks, all_rows, chunk = gated.shape[1:]
    columns = out_ref.shape[1]
    tile = min(256, channels)
    me, place = lax.axis_index("ctx"), lax.axis_index("tensor")
    others = [lax.rem(me + 1 + k, parts) for k in range(parts - 1)]

    loads = [
        pltpu.make_async_copy(planes_ref.at[g], planes.at[g], load_sem.at[g]) for g in (1, 2, 0)
    ]
    for load in loads:
        load.start()
    last_load = pltpu.make_async_copy(weight_ref, weight, load_sem.at[3])
    last_load.start()
    neighbours = [
        ("tensor", jnp.maximum(place - 1, 0), place > 0),
        ("tensor", jnp.minimum(place + 1, shards - 1), place < shards - 1),
    ]
    greeted = greet([("ctx", other, me >= 0) for other in others] + neighbours)
    normalize_rows(hidden_ref, gain_ref, normed)
    own = pltpu.make_async_copy(
        normed.at[:, span(me, depth)], slots.at[place, span(me, rows)], own_sem
    )
    own.start()
    pl.semaphore_wait(pltpu.get_barrier_semaphore(), greeted)

    swaps = [
        pltpu.make_async_remote_copy(
            src_ref=normed.at[:, span(other, depth)],
            dst_ref=slots.at[place, span(me, rows)],
            send_sem=swap_send.at[k],
            recv_sem=swap_recv.at[parts - 2 - k],
            device_id={"ctx": other},
            device_id_type=MESH,
        )
        for k, other in enumerate(others)
    ]
    for swap in swaps:
        swap.start()
    line = Line(
        shards, parts, lambda origin, c: slots.at[origin, span(c, rows)], line_send, line_recv
    )
    own.wait()
    line.send(place, me, 0)
    line.send(place, me, 1)

    first[...] = first_rows(taps_ref, decay_ref)

    @pl.when(me == 0)
    def _():
        padding = jnp.zeros((taps - tail_ref.shape[0], channels), jnp.float32)
        before[...] = jnp.concatenate(
            [padding, tail_ref[...].astype(jnp.float32)], axis=0
        ).astype(jnp.bfloat16)

    for k in range(parts - 1):
        swaps[parts - 2 - k].wait_recv()
        line.send(place, others[k], 0)
        line.send(place, others[k], 1)

    def write_band(group, carry):
        row = jnp.broadcast_to(first[pl.ds(group, 1), :], (taps, 2 * taps))
        bands[group] = pltpu.roll(row, 0, 1, stride=1, stride_axis=0).astype(jnp.bfloat16)
        return carry

    lax.fori_loop(0, groups, write_band, 0)
    for load in loads:
        load.wait()

    tiles = channels // tile

    def project(origin, k):
        def step(index, carry):
            g, column = lax.rem(index // tiles + 1, 3), lax.rem(index, tiles)
            where = span(column, tile)
            partial[g, origin, :, where] = jnp.dot(
                slots[origin], planes[g, :, where], preferred_element_type=jnp.float32
            ).astype(jnp.bfloat16)

            @pl.when(column == tiles - 1)
            def _():
                for k, other in enumerate(others):
                    pltpu.make_async_remote_copy(
                        src_ref=partial.at[g, origin, span(other, rows)],
                        dst_ref=arrived.at[g, parts - 2 - k, span(origin, rows)],
                        send_sem=sum_send,
                        recv_sem=sum_recv.at[g],
                        device_id={"ctx": other},
                        device_id_type=MESH,
                    ).start()

            return carry

        steps = 3 * tiles
        lax.fori_loop(k * steps // parts, (k + 1) * steps // parts, step, 0)

    def project_from(distance, k):
        below, above = place - distance, place + distance

        @pl.when(line.inside(below))
        def _():
            project(jnp.maximum(below, 0), k)

        @pl.when(line.inside(above) & (distance > 0))
        def _():
            project(jnp.minimum(above, shards - 1), k)

    def project_piece(origin, piece):
        mine = span(piece, rows)

        def plane(step, carry):
            g = lax.rem(step + 1, 3)

            def columns(column, inner):
                where = span(column, tile)
                partial[g, origin, mine, where] = jnp.dot(
                    slots[origin, mine], planes[g, :, where], preferred_element_type=jnp.float32
                ).astype(jnp.bfloat16)
                return inner

            lax.fori_loop(0, tiles, columns, 0)

            @pl.when(piece != me)
            def _():
                slot = jnp.clip(lax.rem(me - piece - 1 + parts, parts), 0, parts - 2)
                pltpu.make_async_remote_copy(
                    src_ref=partial.at[g, origin, mine],
                    dst_ref=arrived.at[g, slot, span(origin, rows)],
                    send_sem=sum_send,
                    recv_sem=sum_recv.at[g],
                    device_id={"ctx": piece},
                    device_id_type=MESH,
                ).start()

            return carry

        lax.fori_loop(0, 3, plane, 0)

    def stage(index, carry):
        distance, k = index // parts, lax.rem(index, parts)
        project_from(distance, k)
        piece = lax.rem(me + k, parts)
        line.pass_on(distance + 1, piece, 1)
        line.pass_on(distance + 1, piece, 0)

        @pl.when((distance == shards - 2) & ((place == 0) | (place == shards - 1)))
        def _():
            project_piece(shards - 1 - place, piece)

        return carry

    lax.fori_loop(0, (shards - 1) * parts, stage, 0)

    def summed(g, origin, where=slice(None)):
        value = partial[g, origin, span(me, rows), where].astype(jnp.float32)
        for k in range(parts - 1):
            value = value + arrived[g, k, span(origin, rows), where].astype(jnp.float32)
        return value

    for g in (1, 2):
        pltpu.make_async_copy(arrived.at[g], arrived.at[g], sum_recv.at[g]).wait()

    def write_product(step, carry):
        origin = shards - 1 - step
        product[span(origin, rows), :] = (summed(1, origin) * summed(2, origin)).astype(
            jnp.bfloat16
        )
        return carry

    tail_steps = -(-taps // rows)
    lax.fori_loop(0, tail_steps, write_product, 0)
    tail = pltpu.make_async_remote_copy(
        src_ref=product.at[pl.ds(all_rows - taps, taps)],
        dst_ref=before,
        send_sem=tail_send,
        recv_sem=tail_recv,
        device_id={"ctx": jnp.minimum(me + 1, parts - 1)},
        device_id_type=MESH,
    )

    @pl.when(me + 1 < parts)
    def _():
        tail.start()

    lax.fori_loop(tail_steps, shards, write_product, 0)
    @pl.when(me > 0)
    def _():
        tail.wait_recv()

    per, windows_count = LANES // GROUP, all_rows // taps

    def filter_lanes(block, carry):
        where = span(block, LANES)
        extended = jnp.concatenate([before[:, where], product[:, where]], axis=0)
        windows = jnp.concatenate(
            [extended[b * taps : (b + 2) * taps] for b in range(windows_count)], axis=1
        )
        lane = lax.broadcasted_iota(jnp.int32, windows.shape, 1)
        owner = lax.rem(lane, LANES) // GROUP
        sums = jnp.zeros((taps, windows_count * LANES), jnp.float32)
        for group in range(per):
            mine = jnp.where(owner == group, windows, jnp.zeros_like(windows))
            sums = sums + jnp.dot(
                bands[block * per + group], mine, preferred_element_type=jnp.float32
            )
        for b in range(windows_count):
            inner = pl.ds(b * taps, taps)
            direct = skip_ref[:, where] * product[inner, where].astype(jnp.float32)
            filtered[inner, where] = sums[:, b * LANES : (b + 1) * LANES] + direct
        return carry

    lax.fori_loop(0, channels // LANES, filter_lanes, 0)
    pltpu.make_async_copy(arrived.at[0], arrived.at[0], sum_recv.at[0]).wait()

    gated_line = Line(
        shards, chunks, lambda origin, c: gated.at[origin, c], gated_send, gated_recv
    )

    def gate_chunk(c, carry):
        where = span(c, chunk)

        def gate(origin, inner):
            mine = span(origin, rows)
            gated[place, c, mine, :] = (
                summed(0, origin, where) * filtered[mine, where]
            ).astype(jnp.bfloat16)
            return inner

        lax.fori_loop(0, shards, gate, 0)
        gated_line.send(place, c, 0)
        gated_line.send(place, c, 1)
        return carry

    lax.fori_loop(0, chunks, gate_chunk, 0)
    last_load.wait()
    wide = min(512, columns)

    def multiply(origin, c, fresh):
        deep = span(origin * chunks + c, chunk)

        def column(index, carry):
            where = span(index, wide)
            value = jnp.dot(
                gated[origin, c], weight[deep, where], preferred_element_type=jnp.float32
            )
            total[:, where] = value if fresh else total[:, where] + value
            return carry

        lax.fori_loop(0, columns // wide, column, 0)

    multiply(place, 0, True)

    def multiply_own(c, carry):
        multiply(place, c, False)
        return carry

    lax.fori_loop(1, chunks, multiply_own, 0)
    first_up = jnp.where(2 * place >= shards, 1, 0)

    def collect(index, carry):
        distance, side = index // (2 * chunks) + 1, lax.rem(index // chunks, 2)
        c = lax.rem(index, chunks)
        up = lax.rem(first_up + side, 2)
        gated_line.pass_on(distance, c, up)
        origin = place - distance * (2 * up - 1)

        @pl.when(gated_line.inside(origin))
        def _():
            multiply(jnp.clip(origin, 0, shards - 1), c, False)

        return carry

    lax.fori_loop(0, 2 * chunks * (shards - 1), collect, 0)
    out_ref[...] = total[...].astype(jnp.bfloat16)

    for swap in swaps:
        swap.wait_send()

    @pl.when(me + 1 < parts)
    def _():
        tail.wait_send()

    line.sent()
    gated_line.sent()
    pltpu.make_async_copy(arrived, arrived, sum_send).wait()


def paired_kernel(
    shards,
    hidden_ref,
    gain_ref,
    planes_ref,
    taps_ref,
    decay_ref,
    skip_ref,
    tail_ref,
    weight_ref,
    out_ref,
    normed,
    first,
    planes,
    slots,
    mine,
    outgoing,
    arrived,
    extended,
    filtered,
    bands,
    weight,
    gated,
    handed,
    total,
    load_sem,
    own_sem,
    planes_send,
    planes_recv,
    swap_send,
    line_send,
    line_recv,
    pair_send,
    pair_recv,
    sum_send,
    sum_recv,
    tail_send,
    tail_recv,
    hand_send,
    hand_recv,
    gated_send,
    gated_recv,
):
    rows = hidden_ref.shape[0]
    parts = slots.shape[1] // rows
    _, both_depths, half = planes.shape
    depth = both_depths // 2
    _, taps, _ = bands.shape
    chunks, all_rows, chunk = gated.shape[1:]
    columns = out_ref.shape[1]
    tile = min(256, half)
    tiles = half // tile
    me, place = lax.axis_index("ctx"), lax.axis_index("tensor")
    pair, core = me // 2, lax.rem(me, 2)
    across = 1 - pair
    sibling, peer = 2 * pair + 1 - core, 2 * across + core

    loads = [
        pltpu.make_async_copy(
            planes_ref.at[g, :, span(core, half)], planes.at[g, span(core, depth)], load_sem.at[g]
        )
        for g in (1, 2, 0)
    ]
    for load in loads:
        load.start()
    last_load = pltpu.make_async_copy(weight_ref, weight, load_sem.at[3])
    others = [lax.rem(me + 1 + k, parts) for k in range(parts - 1)]
    neighbours = [
        ("tensor", jnp.maximum(place - 1, 0), place > 0),
        ("tensor", jnp.minimum(place + 1, shards - 1), place < shards - 1),
    ]
    greeted = greet([("ctx", other, me >= 0) for other in others] + neighbours)
    normalize_rows(hidden_ref, gain_ref, normed)
    mine_in = normed.at[:, span(pair, both_depths)]
    own = pltpu.make_async_copy(mine_in, slots.at[place, span(me, rows)], own_sem)
    own.start()
    pl.semaphore_wait(pltpu.get_barrier_semaphore(), greeted)

    def remote(source, target, send, recv, **device):
        return pltpu.make_async_remote_copy(
            src_ref=source,
            dst_ref=target,
            send_sem=send,
            recv_sem=recv,
            device_id=device,
            device_id_type=MESH,
        )

    line = Line(
        shards,
        parts,
        lambda origin, c: slots.at[origin, span(c, rows), span(core, depth)],
        line_send,
        line_recv,
    )
    line.send(place, me, 0, normed.at[:, span(me, depth)])
    line.send(place, me, 1, normed.at[:, span(me, depth)])
    to_sibling = remote(
        mine_in, slots.at[place, span(me, rows)], pair_send, pair_recv.at[place, me], ctx=sibling
    )
    to_sibling.start()
    swaps = [
        remote(
            normed.at[:, span(2 * across + k, depth)],
            slots.at[place, span(me, rows), pl.ds(k * depth, depth)],
            swap_send.at[k],
            line_recv.at[place, me],
            ctx=2 * across + k,
        )
        for k in range(2)
    ]
    for swap in swaps:
        swap.start()
    shares = [
        remote(
            planes_ref.at[g, :, span(1 - core, half)],
            planes.at[g, span(core, depth)],
            planes_send,
            planes_recv.at[g],
            ctx=sibling,
        )
        for g in (1, 2, 0)
    ]
    for share in shares:
        share.start()

    def share_piece(origin, c):
        ref = slots.at[origin, span(c, rows), span(core, depth)]
        return remote(ref, ref, pair_send, pair_recv.at[origin, c], ctx=sibling)

    def from_sibling(origin, c):
        ref = slots.at[origin, span(c, rows), span(1 - core, depth)]
        return remote(ref, ref, pair_send, pair_recv.at[origin, c], ctx=sibling)

    first[...] = first_rows(taps_ref, decay_ref)

    @pl.when(pair == 0)
    def _():
        padding = jnp.zeros((taps - tail_ref.shape[0], half), jnp.float32)
        extended[pl.ds(0, taps), :] = jnp.concatenate(
            [padding, tail_ref[:, span(core, half)].astype(jnp.float32)], axis=0
        ).astype(jnp.bfloat16)

    remote(
        mine_in,
        slots.at[place, span(sibling, rows)],
        pair_send,
        pair_recv.at[place, sibling],
        ctx=sibling,
    ).wait_recv()
    line.send(place, sibling, 0)
    line.send(place, sibling, 1)

    def write_band(group, carry):
        row = jnp.broadcast_to(first[pl.ds(core * (half // GROUP) + group, 1), :], (taps, 2 * taps))
        bands[group] = pltpu.roll(row, 0, 1, stride=1, stride_axis=0).astype(jnp.bfloat16)
        return carry

    for k in range(2):
        c = 2 * across + k
        line.hop(place, c, 1).wait_recv()
        line.send(place, c, 0)
        line.send(place, c, 1)
        share_piece(place, c).start()
    lax.fori_loop(0, half // GROUP, write_band, 0)
    own.wait()
    for load in loads:
        load.wait()
    for share in shares:
        share.wait_recv()
    last_load.start()

    def sum_piece(g, origin):
        where = span(origin, rows)
        return remote(
            outgoing.at[g, :, where],
            arrived.at[g, :, where],
            sum_send,
            sum_recv.at[g, origin],
            ctx=peer,
        )

    def project(origin, far):
        tokens = span(across if far else pair, 2 * rows)
        target = outgoing if far else mine

        def step(index, carry):
            g, column = lax.rem(index // tiles + 1, 3), lax.rem(index, tiles)
            where = span(column, tile)
            value = jnp.dot(
                slots[origin, tokens], planes[g, :, where], preferred_element_type=jnp.float32
            ).astype(target.dtype)
            for k in range(2):
                target[g, k, span(origin, rows), where] = value[k * rows : (k + 1) * rows]
            if far:

                @pl.when(column == tiles - 1)
                def _():
                    sum_piece(g, origin).start()

            return carry

        lax.fori_loop(0, 3 * tiles, step, 0)

    def combine(origin):
        where = span(origin, rows)
        for g in (1, 2, 0):
            sum_piece(g, origin).wait_recv()
        for k in range(2):
            q, key, value = [
                mine[g, k, where] + arrived[g, k, where].astype(jnp.float32) for g in range(3)
            ]
            mine[0, k, where] = q
            start = pl.multiple_of(taps + k * all_rows + origin * rows, rows)
            extended[pl.ds(start, rows), :] = (key * value).astype(jnp.bfloat16)

    def beside(distance, work):
        for origin in (place - distance, place + distance):

            @pl.when(line.inside(origin))
            def _(origin=origin):
                work(jnp.clip(origin, 0, shards - 1))

    project(place, False)
    for k in range(2):
        from_sibling(place, 2 * across + k).wait_recv()
    project(place, True)

    def stage(distance, carry):
        for far in (False, True):
            group = across if far else pair
            for k in range(2):
                c = 2 * group + k
                line.pass_on(distance, c, 1)
                line.pass_on(distance, c, 0)
                beside(distance, lambda origin, c=c: share_piece(origin, c).start())

            def both(origin, far=far, group=group):
                for k in range(2):
                    from_sibling(origin, 2 * group + k).wait_recv()
                project(origin, far)

            beside(distance, both)

        @pl.when(distance == 1)
        def _():
            combine(place)

        @pl.when(distance > 1)
        def _():
            beside(distance - 1, combine)

        return carry

    lax.fori_loop(1, shards, stage, 0)
    beside(shards - 1, combine)
    before = extended.at[pl.ds(0, taps)]
    tail = remote(
        extended.at[pl.ds(2 * all_rows, taps)], before, tail_send, tail_recv, ctx=peer
    )

    @pl.when(pair == 0)
    def _():
        tail.start()

    @pl.when(pair == 1)
    def _():
        tail.wait_recv()

    per, windows_count = LANES // GROUP, 2 * all_rows // taps

    def filter_lanes(block, carry):
        where = span(block, LANES)
        values = extended[:, where]
        windows = jnp.concatenate(
            [values[b * taps : (b + 2) * taps] for b in range(windows_count)], axis=1
        )
        lane = lax.broadcasted_iota(jnp.int32, windows.shape, 1)
        owner = lax.rem(lane, LANES) // GROUP
        sums = jnp.zeros((taps, windows_count * LANES), jnp.float32)
        for group in range(per):
            some = jnp.where(owner == group, windows, jnp.zeros_like(windows))
            sums = sums + jnp.dot(
                bands[block * per + group], some, preferred_element_type=jnp.float32
            )
        skip = skip_ref[:, pl.ds(pl.multiple_of(core * half + block * LANES, LANES), LANES)]
        for b in range(windows_count):
            direct = skip * values[(b + 1) * taps : (b + 2) * taps].astype(jnp.float32)
            filtered[pl.ds(b * taps, taps), where] = sums[:, b * LANES : (b + 1) * LANES] + direct
        return carry

    gated_line = Line(
        shards, chunks, lambda origin, c: gated.at[origin, c], gated_send, gated_recv
    )
    mine_chunks = half // chunk

    def hand(i, owner):
        c = owner * mine_chunks + i
        return remote(handed.at[i], gated.at[place, c], hand_send, hand_recv.at[i], ctx=sibling)

    def gate_chunk(i, carry):
        per_chunk = chunk // LANES
        lax.fori_loop(i * per_chunk, (i + 1) * per_chunk, filter_lanes, 0)
        where = span(i, chunk)

        def gate(k):
            return (mine[0, k, :, where] * filtered[span(k, all_rows), where]).astype(jnp.bfloat16)

        handed[i] = gate(1 - core)
        hand(i, core).start()
        c = core * mine_chunks + i
        gated[place, c] = gate(core)
        gated_line.send(place, c, 0)
        gated_line.send(place, c, 1)
        return carry

    lax.fori_loop(0, mine_chunks, gate_chunk, 0)

    def take(i, carry):
        hand(i, 1 - core).wait_recv()
        c = (1 - core) * mine_chunks + i
        gated_line.send(place, c, 0)
        gated_line.send(place, c, 1)
        return carry

    lax.fori_loop(0, mine_chunks, take, 0)
    last_load.wait()
    wide = min(512, columns)

    def multiply(origin, c, fresh):
        deep = span(origin * chunks + c, chunk)

        def column(index, carry):
            where = span(index, wide)
            value = jnp.dot(
                gated[origin, c], weight[deep, where], preferred_element_type=jnp.float32
            )
            total[:, where] = value if fresh else total[:, where] + value
            return carry

        lax.fori_loop(0, columns // wide, column, 0)

    multiply(place, 0, True)

    def multiply_own(c, carry):
        multiply(place, c, False)
        return carry

    lax.fori_loop(1, chunks, multiply_own, 0)
    first_up = jnp.where(2 * place >= shards, 1, 0)

    def collect(index, carry):
        distance, side = index // (2 * chunks) + 1, lax.rem(index // chunks, 2)
        step = lax.rem(index, chunks)
        c = lax.rem(step + core * mine_chunks, chunks)
        up = lax.rem(first_up + side, 2)
        gated_line.pass_on(distance, c, up)
        origin = place - distance * (2 * up - 1)

        @pl.when(gated_line.inside(origin))
        def _():
            multiply(jnp.clip(origin, 0, shards - 1), c, False)

        return carry

    lax.fori_loop(0, 2 * chunks * (shards - 1), collect, 0)
    out_ref[...] = total[...].astype(jnp.bfloat16)

    for swap in swaps:
        swap.wait_send()

    @pl.when(pair == 0)
    def _():
        tail.wait_send()

    line.sent()
    gated_line.sent()
    slices = slots.at[:, :, pl.ds(0, depth)]
    pltpu.make_async_copy(slices, slices, pair_send).wait()
    pltpu.make_async_copy(handed, handed, hand_send).wait()
    pltpu.make_async_copy(outgoing, outgoing, sum_send).wait()
    sent_planes = planes.at[:, pl.ds(0, depth)]
    pltpu.make_async_copy(sent_planes, sent_planes, planes_send).wait()


def on_paired_device(
    hidden_in, norm_gain, weight_in, filter_taps, filter_decay, skip_gain, tail_cache, output_weight
):
    shards, parts = lax.axis_size("tensor"), lax.axis_size("ctx")
    rows = hidden_in.shape[0]
    depth, _, channels = weight_in.shape
    groups, taps = filter_taps.shape
    columns = output_weight.shape[1]
    all_rows = shards * rows
    half = channels // 2
    chunk = min(256, half)
    chunks = channels // chunk
    vmem, anywhere = pl.BlockSpec(memory_space=pltpu.VMEM), pl.BlockSpec(memory_space=pl.ANY)
    dma = pltpu.SemaphoreType.DMA
    bf16, f32 = jnp.bfloat16, jnp.float32
    return pl.pallas_call(
        functools.partial(paired_kernel, shards),
        out_shape=jax.ShapeDtypeStruct((all_rows, columns), bf16),
        in_specs=[vmem, vmem, anywhere, vmem, vmem, vmem, vmem, anywhere],
        out_specs=vmem,
        scratch_shapes=[
            pltpu.VMEM((rows, hidden_in.shape[1]), bf16),
            pltpu.VMEM((groups, 2 * taps), f32),
            pltpu.VMEM((3, 2 * depth, half), bf16),
            pltpu.VMEM((shards, parts * rows, 2 * depth), bf16),
            pltpu.VMEM((3, 2, all_rows, half), f32),
            pltpu.VMEM((3, 2, all_rows, half), bf16),
            pltpu.VMEM((3, 2, all_rows, half), bf16),
            pltpu.VMEM((taps + 2 * all_rows, half), bf16),
            pltpu.VMEM((2 * all_rows, half), f32),
            pltpu.VMEM((groups // 2, taps, 2 * taps), bf16),
            pltpu.VMEM(output_weight.shape, bf16),
            pltpu.VMEM((shards, chunks, all_rows, chunk), bf16),
            pltpu.VMEM((chunks // 2, all_rows, chunk), bf16),
            pltpu.VMEM((all_rows, columns), f32),
            dma((4,)),
            dma,
            dma,
            dma((3,)),
            dma((2,)),
            dma((2, shards, parts)),
            dma((shards, parts)),
            dma,
            dma((shards, parts)),
            dma,
            dma((3, shards)),
            dma,
            dma,
            dma,
            dma((chunks // 2,)),
            dma((2, shards, chunks)),
            dma((shards, chunks)),
        ],
        compiler_params=pltpu.CompilerParams(
            collective_id=0, has_side_effects=True, vmem_limit_bytes=58 << 20
        ),
    )(
        hidden_in,
        norm_gain.reshape(1, norm_gain.shape[0]),
        weight_in.transpose(1, 0, 2),
        filter_taps,
        filter_decay.reshape(1, groups),
        skip_gain.reshape(1, channels),
        tail_cache,
        output_weight,
    )


def on_device(
    hidden_in, norm_gain, weight_in, filter_taps, filter_decay, skip_gain, tail_cache, output_weight
):
    shards, parts = lax.axis_size("tensor"), lax.axis_size("ctx")
    rows = hidden_in.shape[0]
    depth, _, channels = weight_in.shape
    groups, taps = filter_taps.shape
    columns = output_weight.shape[1]
    all_rows = shards * rows
    chunk = min(256, channels)
    chunks = channels // chunk
    vmem, anywhere = pl.BlockSpec(memory_space=pltpu.VMEM), pl.BlockSpec(memory_space=pl.ANY)
    dma = pltpu.SemaphoreType.DMA
    bf16, f32 = jnp.bfloat16, jnp.float32
    return pl.pallas_call(
        functools.partial(mixer_kernel, shards, parts),
        out_shape=jax.ShapeDtypeStruct((all_rows, columns), bf16),
        in_specs=[vmem, vmem, anywhere, vmem, vmem, vmem, vmem, anywhere],
        out_specs=vmem,
        scratch_shapes=[
            pltpu.VMEM((rows, hidden_in.shape[1]), bf16),
            pltpu.VMEM((groups, 2 * taps), f32),
            pltpu.VMEM((3, depth, channels), bf16),
            pltpu.VMEM((shards, parts * rows, depth), bf16),
            pltpu.VMEM((3, shards, parts * rows, channels), bf16),
            pltpu.VMEM((3, parts - 1, all_rows, channels), bf16),
            pltpu.VMEM((all_rows, channels), f32),
            pltpu.VMEM((all_rows, channels), bf16),
            pltpu.VMEM((taps, channels), bf16),
            pltpu.VMEM((groups, taps, 2 * taps), bf16),
            pltpu.VMEM(output_weight.shape, bf16),
            pltpu.VMEM((shards, chunks, all_rows, chunk), bf16),
            pltpu.VMEM((all_rows, columns), f32),
            dma((4,)),
            dma,
            dma((parts - 1,)),
            dma((parts - 1,)),
            dma((2, shards, parts)),
            dma((shards, parts)),
            dma,
            dma((3,)),
            dma,
            dma,
            dma((2, shards, chunks)),
            dma((shards, chunks)),
        ],
        compiler_params=pltpu.CompilerParams(
            collective_id=0, has_side_effects=True, vmem_limit_bytes=56 << 20
        ),
    )(
        hidden_in,
        norm_gain.reshape(1, norm_gain.shape[0]),
        weight_in.transpose(1, 0, 2),
        filter_taps,
        filter_decay.reshape(1, groups),
        skip_gain.reshape(1, channels),
        tail_cache,
        output_weight,
    )


def solution(mesh):
    in_specs = (
        P(("prompt", "ctx", "tensor"), None),
        P(),
        P("ctx", None, "tensor"),
        P("tensor", None),
        P("tensor"),
        P("tensor"),
        P("prompt", "tensor"),
        P(None, "tensor"),
    )
    out_specs = P(("prompt", "ctx"), "tensor")
    paired = mesh.shape["ctx"] == 4
    return jax.shard_map(
        on_paired_device if paired else on_device, mesh=mesh, in_specs=in_specs, out_specs=out_specs, check_vma=False
    )
```

```python
import functools

import jax
import jax.numpy as jnp
from jax import lax
from jax.experimental import pallas as pl
from jax.experimental.pallas import tpu as pltpu
from jax.sharding import PartitionSpec as P

GROUP = 16
LANES = 128
MESH = pl.DeviceIdType.MESH


def span(index, size):
    return pl.ds(pl.multiple_of(index * size, size), size)


def greet(peers):
    barrier = pltpu.get_barrier_semaphore()
    for axis, peer, there in peers:

        @pl.when(there)
        def _(axis=axis, peer=peer):
            pl.semaphore_signal(barrier, inc=1, device_id={axis: peer}, device_id_type=MESH)

    return sum(jnp.where(there, 1, 0) for _, _, there in peers)


def normalize_rows(hidden_ref, gain_ref, normed):
    rows, width = hidden_ref.shape
    few, part = min(16, rows), 1024

    def step(index, carry):
        where = span(index, few)

        def values(start):
            return hidden_ref[where, pl.ds(start, part)].astype(jnp.float32)

        squares = jnp.zeros((few, part), jnp.float32)
        for start in range(0, width, part):
            squares = squares + values(start) * values(start)
        scaled = lax.rsqrt(jnp.sum(squares, axis=-1, keepdims=True) / width + 1e-06)
        for start in range(0, width, part):
            inner = pl.ds(start, part)
            normed[where, inner] = (values(start) * scaled * gain_ref[:, inner]).astype(
                jnp.bfloat16
            )
        return carry

    lax.fori_loop(0, rows // few, step, 0)


def first_rows(taps_ref, decay_ref):
    groups, taps = taps_ref.shape
    lags = lax.broadcasted_iota(jnp.int32, (groups, taps), 1).astype(jnp.float32)
    across = lax.broadcasted_iota(jnp.int32, (groups, groups), 1)
    down = lax.broadcasted_iota(jnp.int32, (groups, groups), 0)
    decay = jnp.sum(jnp.where(across == down, decay_ref[...], 0.0), axis=1, keepdims=True)
    taps_full = (taps_ref[...] * jnp.exp(-decay * lags)).astype(jnp.bfloat16)
    lag = lax.broadcasted_iota(jnp.int32, (taps, 2 * taps), 0)
    column = lax.broadcasted_iota(jnp.int32, (taps, 2 * taps), 1)
    turned = jnp.where(lag + column == taps, 1.0, 0.0).astype(jnp.bfloat16)
    return jnp.dot(taps_full, turned, preferred_element_type=jnp.float32)


class Line:
    def __init__(self, count, pieces, view, send_sem, recv_sem):
        self.count, self.pieces, self.view = count, pieces, view
        self.send_sem, self.recv_sem = send_sem, recv_sem
        self.place = lax.axis_index("tensor")

    def inside(self, position):
        return (position >= 0) & (position < self.count)

    def hop(self, origin, piece, up, source=None):
        ref = self.view(origin, piece)
        return pltpu.make_async_remote_copy(
            src_ref=ref if source is None else source,
            dst_ref=ref,
            send_sem=self.send_sem.at[up, origin, piece],
            recv_sem=self.recv_sem.at[origin, piece],
            device_id={"tensor": jnp.clip(self.place + 2 * up - 1, 0, self.count - 1)},
            device_id_type=MESH,
        )

    def send(self, origin, piece, up, source=None):
        @pl.when(self.inside(self.place + 2 * up - 1))
        def _():
            self.hop(origin, piece, up, source).start()

    def pass_on(self, distance, piece, up):
        origin = self.place - distance * (2 * up - 1)

        @pl.when(self.inside(origin))
        def _():
            source = jnp.clip(origin, 0, self.count - 1)
            self.hop(source, piece, up).wait_recv()
            self.send(source, piece, up)

    def sent(self):
        def step(index, carry):
            origin, piece = index // self.pieces, lax.rem(index, self.pieces)

            @pl.when((origin <= self.place) & (self.place + 1 < self.count))
            def _():
                self.hop(origin, piece, 1).wait_send()

            @pl.when((origin >= self.place) & (self.place > 0))
            def _():
                self.hop(origin, piece, 0).wait_send()

            return carry

        lax.fori_loop(0, self.count * self.pieces, step, 0)


def mixer_kernel(
    shards,
    parts,
    hidden_ref,
    gain_ref,
    planes_ref,
    taps_ref,
    decay_ref,
    skip_ref,
    tail_ref,
    weight_ref,
    out_ref,
    normed,
    first,
    planes,
    slots,
    partial,
    arrived,
    filtered,
    product,
    before,
    bands,
    weight,
    gated,
    total,
    load_sem,
    own_sem,
    swap_send,
    swap_recv,
    line_send,
    line_recv,
    sum_send,
    sum_recv,
    tail_send,
    tail_recv,
    gated_send,
    gated_recv,
):
    rows = hidden_ref.shape[0]
    _, depth, channels = planes.shape
    groups, taps, _ = bands.shape
    chunks, all_rows, chunk = gated.shape[1:]
    columns = out_ref.shape[1]
    tile = min(256, channels)
    me, place = lax.axis_index("ctx"), lax.axis_index("tensor")
    others = [lax.rem(me + 1 + k, parts) for k in range(parts - 1)]

    loads = [
        pltpu.make_async_copy(planes_ref.at[g], planes.at[g], load_sem.at[g]) for g in (1, 2, 0)
    ]
    for load in loads:
        load.start()
    last_load = pltpu.make_async_copy(weight_ref, weight, load_sem.at[3])
    last_load.start()
    neighbours = [
        ("tensor", jnp.maximum(place - 1, 0), place > 0),
        ("tensor", jnp.minimum(place + 1, shards - 1), place < shards - 1),
    ]
    greeted = greet([("ctx", other, me >= 0) for other in others] + neighbours)
    normalize_rows(hidden_ref, gain_ref, normed)
    own = pltpu.make_async_copy(
        normed.at[:, span(me, depth)], slots.at[place, span(me, rows)], own_sem
    )
    own.start()
    pl.semaphore_wait(pltpu.get_barrier_semaphore(), greeted)

    swaps = [
        pltpu.make_async_remote_copy(
            src_ref=normed.at[:, span(other, depth)],
            dst_ref=slots.at[place, span(me, rows)],
            send_sem=swap_send.at[k],
            recv_sem=swap_recv.at[parts - 2 - k],
            device_id={"ctx": other},
            device_id_type=MESH,
        )
        for k, other in enumerate(others)
    ]
    for swap in swaps:
        swap.start()
    line = Line(
        shards, parts, lambda origin, c: slots.at[origin, span(c, rows)], line_send, line_recv
    )
    own.wait()
    line.send(place, me, 0)
    line.send(place, me, 1)

    first[...] = first_rows(taps_ref, decay_ref)

    @pl.when(me == 0)
    def _():
        padding = jnp.zeros((taps - tail_ref.shape[0], channels), jnp.float32)
        before[...] = jnp.concatenate(
            [padding, tail_ref[...].astype(jnp.float32)], axis=0
        ).astype(jnp.bfloat16)

    for k in range(parts - 1):
        swaps[parts - 2 - k].wait_recv()
        line.send(place, others[k], 0)
        line.send(place, others[k], 1)

    def write_band(group, carry):
        row = jnp.broadcast_to(first[pl.ds(group, 1), :], (taps, 2 * taps))
        bands[group] = pltpu.roll(row, 0, 1, stride=1, stride_axis=0).astype(jnp.bfloat16)
        return carry

    lax.fori_loop(0, groups, write_band, 0)
    for load in loads:
        load.wait()

    tiles = channels // tile

    def project(origin, k):
        def step(index, carry):
            g, column = lax.rem(index // tiles + 1, 3), lax.rem(index, tiles)
            where = span(column, tile)
            partial[g, origin, :, where] = jnp.dot(
                slots[origin], planes[g, :, where], preferred_element_type=jnp.float32
            ).astype(jnp.bfloat16)

            @pl.when(column == tiles - 1)
            def _():
                for k, other in enumerate(others):
                    pltpu.make_async_remote_copy(
                        src_ref=partial.at[g, origin, span(other, rows)],
                        dst_ref=arrived.at[g, parts - 2 - k, span(origin, rows)],
                        send_sem=sum_send,
                        recv_sem=sum_recv.at[g],
                        device_id={"ctx": other},
                        device_id_type=MESH,
                    ).start()

            return carry

        steps = 3 * tiles
        lax.fori_loop(k * steps // parts, (k + 1) * steps // parts, step, 0)

    def project_from(distance, k):
        below, above = place - distance, place + distance

        @pl.when(line.inside(below))
        def _():
            project(jnp.maximum(below, 0), k)

        @pl.when(line.inside(above) & (distance > 0))
        def _():
            project(jnp.minimum(above, shards - 1), k)

    def project_piece(origin, piece):
        mine = span(piece, rows)

        def plane(step, carry):
            g = lax.rem(step + 1, 3)

            def columns(column, inner):
                where = span(column, tile)
                partial[g, origin, mine, where] = jnp.dot(
                    slots[origin, mine], planes[g, :, where], preferred_element_type=jnp.float32
                ).astype(jnp.bfloat16)
                return inner

            lax.fori_loop(0, tiles, columns, 0)

            @pl.when(piece != me)
            def _():
                slot = jnp.clip(lax.rem(me - piece - 1 + parts, parts), 0, parts - 2)
                pltpu.make_async_remote_copy(
                    src_ref=partial.at[g, origin, mine],
                    dst_ref=arrived.at[g, slot, span(origin, rows)],
                    send_sem=sum_send,
                    recv_sem=sum_recv.at[g],
                    device_id={"ctx": piece},
                    device_id_type=MESH,
                ).start()

            return carry

        lax.fori_loop(0, 3, plane, 0)

    def stage(index, carry):
        distance, k = index // parts, lax.rem(index, parts)
        project_from(distance, k)
        piece = lax.rem(me + k, parts)
        line.pass_on(distance + 1, piece, 1)
        line.pass_on(distance + 1, piece, 0)

        @pl.when((distance == shards - 2) & ((place == 0) | (place == shards - 1)))
        def _():
            project_piece(shards - 1 - place, piece)

        return carry

    lax.fori_loop(0, (shards - 1) * parts, stage, 0)

    def summed(g, origin, where=slice(None)):
        value = partial[g, origin, span(me, rows), where].astype(jnp.float32)
        for k in range(parts - 1):
            value = value + arrived[g, k, span(origin, rows), where].astype(jnp.float32)
        return value

    for g in (1, 2):
        pltpu.make_async_copy(arrived.at[g], arrived.at[g], sum_recv.at[g]).wait()

    def write_product(step, carry):
        origin = shards - 1 - step
        product[span(origin, rows), :] = (summed(1, origin) * summed(2, origin)).astype(
            jnp.bfloat16
        )
        return carry

    tail_steps = -(-taps // rows)
    lax.fori_loop(0, tail_steps, write_product, 0)
    tail = pltpu.make_async_remote_copy(
        src_ref=product.at[pl.ds(all_rows - taps, taps)],
        dst_ref=before,
        send_sem=tail_send,
        recv_sem=tail_recv,
        device_id={"ctx": jnp.minimum(me + 1, parts - 1)},
        device_id_type=MESH,
    )

    @pl.when(me + 1 < parts)
    def _():
        tail.start()

    lax.fori_loop(tail_steps, shards, write_product, 0)
    @pl.when(me > 0)
    def _():
        tail.wait_recv()

    per, windows_count = LANES // GROUP, all_rows // taps

    def filter_lanes(block, carry):
        where = span(block, LANES)
        extended = jnp.concatenate([before[:, where], product[:, where]], axis=0)
        windows = jnp.concatenate(
            [extended[b * taps : (b + 2) * taps] for b in range(windows_count)], axis=1
        )
        lane = lax.broadcasted_iota(jnp.int32, windows.shape, 1)
        owner = lax.rem(lane, LANES) // GROUP
        sums = jnp.zeros((taps, windows_count * LANES), jnp.float32)
        for group in range(per):
            mine = jnp.where(owner == group, windows, jnp.zeros_like(windows))
            sums = sums + jnp.dot(
                bands[block * per + group], mine, preferred_element_type=jnp.float32
            )
        for b in range(windows_count):
            inner = pl.ds(b * taps, taps)
            direct = skip_ref[:, where] * product[inner, where].astype(jnp.float32)
            filtered[inner, where] = sums[:, b * LANES : (b + 1) * LANES] + direct
        return carry

    lax.fori_loop(0, channels // LANES, filter_lanes, 0)
    pltpu.make_async_copy(arrived.at[0], arrived.at[0], sum_recv.at[0]).wait()

    gated_line = Line(
        shards, chunks, lambda origin, c: gated.at[origin, c], gated_send, gated_recv
    )

    def gate_chunk(c, carry):
        where = span(c, chunk)

        def gate(origin, inner):
            mine = span(origin, rows)
            gated[place, c, mine, :] = (
                summed(0, origin, where) * filtered[mine, where]
            ).astype(jnp.bfloat16)
            return inner

        lax.fori_loop(0, shards, gate, 0)
        gated_line.send(place, c, 0)
        gated_line.send(place, c, 1)
        return carry

    lax.fori_loop(0, chunks, gate_chunk, 0)
    last_load.wait()
    wide = min(512, columns)

    def multiply(origin, c, fresh):
        deep = span(origin * chunks + c, chunk)

        def column(index, carry):
            where = span(index, wide)
            value = jnp.dot(
                gated[origin, c], weight[deep, where], preferred_element_type=jnp.float32
            )
            total[:, where] = value if fresh else total[:, where] + value
            return carry

        lax.fori_loop(0, columns // wide, column, 0)

    multiply(place, 0, True)

    def multiply_own(c, carry):
        multiply(place, c, False)
        return carry

    lax.fori_loop(1, chunks, multiply_own, 0)
    first_up = jnp.where(2 * place >= shards, 1, 0)

    def collect(index, carry):
        distance, side = index // (2 * chunks) + 1, lax.rem(index // chunks, 2)
        c = lax.rem(index, chunks)
        up = lax.rem(first_up + side, 2)
        gated_line.pass_on(distance, c, up)
        origin = place - distance * (2 * up - 1)

        @pl.when(gated_line.inside(origin))
        def _():
            multiply(jnp.clip(origin, 0, shards - 1), c, False)

        return carry

    lax.fori_loop(0, 2 * chunks * (shards - 1), collect, 0)
    out_ref[...] = total[...].astype(jnp.bfloat16)

    for swap in swaps:
        swap.wait_send()

    @pl.when(me + 1 < parts)
    def _():
        tail.wait_send()

    line.sent()
    gated_line.sent()
    pltpu.make_async_copy(arrived, arrived, sum_send).wait()


def paired_kernel(
    shards,
    hidden_in,
    gain_in,
    planes_ref,
    taps_in,
    decay_in,
    skip_in,
    tail_in,
    weight_ref,
    out_ref,
    hidden_ref,
    gain_ref,
    taps_ref,
    decay_ref,
    skip_ref,
    tail_ref,
    normed,
    first,
    planes,
    slots,
    mine,
    outgoing,
    arrived,
    extended,
    filtered,
    bands,
    weight,
    gated,
    handed,
    total,
    result,
    input_sem,
    out_sem,
    load_sem,
    own_sem,
    planes_send,
    planes_recv,
    swap_send,
    line_send,
    line_recv,
    pair_send,
    pair_recv,
    sum_send,
    sum_recv,
    tail_send,
    tail_recv,
    hand_send,
    hand_recv,
    gated_send,
    gated_recv,
):
    rows = hidden_ref.shape[0]
    parts = slots.shape[1] // rows
    _, both_depths, half = planes.shape
    depth = both_depths // 2
    _, taps, _ = bands.shape
    chunks, all_rows, chunk = gated.shape[1:]
    columns = out_ref.shape[1]
    tile = min(256, half)
    tiles = half // tile
    me, place = lax.axis_index("ctx"), lax.axis_index("tensor")
    pair, core = me // 2, lax.rem(me, 2)
    across = 1 - pair
    sibling, peer = 2 * pair + 1 - core, 2 * across + core

    others = [lax.rem(me + 1 + k, parts) for k in range(parts - 1)]
    neighbours = [
        ("tensor", jnp.maximum(place - 1, 0), place > 0),
        ("tensor", jnp.minimum(place + 1, shards - 1), place < shards - 1),
    ]
    greeted = greet([("ctx", other, me >= 0) for other in others] + neighbours)
    inputs = [
        pltpu.make_async_copy(source, target, input_sem.at[k])
        for k, (source, target) in enumerate(
            [
                (hidden_in, hidden_ref),
                (gain_in, gain_ref),
                (taps_in, taps_ref),
                (decay_in, decay_ref),
                (skip_in, skip_ref),
                (tail_in, tail_ref),
            ]
        )
    ]
    for load in inputs:
        load.start()
    loads = [
        pltpu.make_async_copy(
            planes_ref.at[g, :, span(core, half)], planes.at[g, span(core, depth)], load_sem.at[g]
        )
        for g in (1, 2, 0)
    ]
    for load in loads:
        load.start()
    last_load = pltpu.make_async_copy(weight_ref, weight, load_sem.at[3])
    for load in inputs[:2]:
        load.wait()
    normalize_rows(hidden_ref, gain_ref, normed)
    mine_in = normed.at[:, span(pair, both_depths)]
    own = pltpu.make_async_copy(mine_in, slots.at[place, span(me, rows)], own_sem)
    own.start()
    pl.semaphore_wait(pltpu.get_barrier_semaphore(), greeted)

    def remote(source, target, send, recv, **device):
        return pltpu.make_async_remote_copy(
            src_ref=source,
            dst_ref=target,
            send_sem=send,
            recv_sem=recv,
            device_id=device,
            device_id_type=MESH,
        )

    line = Line(
        shards,
        parts,
        lambda origin, c: slots.at[origin, span(c, rows), span(core, depth)],
        line_send,
        line_recv,
    )
    line.send(place, me, 0, normed.at[:, span(me, depth)])
    line.send(place, me, 1, normed.at[:, span(me, depth)])
    to_sibling = remote(
        mine_in, slots.at[place, span(me, rows)], pair_send, pair_recv.at[place, me], ctx=sibling
    )
    to_sibling.start()
    swaps = [
        remote(
            normed.at[:, span(2 * across + k, depth)],
            slots.at[place, span(me, rows), pl.ds(k * depth, depth)],
            swap_send.at[k],
            line_recv.at[place, me],
            ctx=2 * across + k,
        )
        for k in range(2)
    ]
    for swap in swaps:
        swap.start()
    shares = [
        remote(
            planes_ref.at[g, :, span(1 - core, half)],
            planes.at[g, span(core, depth)],
            planes_send,
            planes_recv.at[g],
            ctx=sibling,
        )
        for g in (1, 2, 0)
    ]
    for share in shares:
        share.start()

    def share_piece(origin, c):
        ref = slots.at[origin, span(c, rows), span(core, depth)]
        return remote(ref, ref, pair_send, pair_recv.at[origin, c], ctx=sibling)

    def from_sibling(origin, c):
        ref = slots.at[origin, span(c, rows), span(1 - core, depth)]
        return remote(ref, ref, pair_send, pair_recv.at[origin, c], ctx=sibling)

    for load in inputs[2:]:
        load.wait()
    first[...] = first_rows(taps_ref, decay_ref)

    @pl.when(pair == 0)
    def _():
        padding = jnp.zeros((taps - tail_ref.shape[0], half), jnp.float32)
        extended[pl.ds(0, taps), :] = jnp.concatenate(
            [padding, tail_ref[:, span(core, half)].astype(jnp.float32)], axis=0
        ).astype(jnp.bfloat16)

    remote(
        mine_in,
        slots.at[place, span(sibling, rows)],
        pair_send,
        pair_recv.at[place, sibling],
        ctx=sibling,
    ).wait_recv()
    line.send(place, sibling, 0)
    line.send(place, sibling, 1)

    def write_band(group, carry):
        row = jnp.broadcast_to(first[pl.ds(core * (half // GROUP) + group, 1), :], (taps, 2 * taps))
        bands[group] = pltpu.roll(row, 0, 1, stride=1, stride_axis=0).astype(jnp.bfloat16)
        return carry

    for k in range(2):
        c = 2 * across + k
        line.hop(place, c, 1).wait_recv()
        line.send(place, c, 0)
        line.send(place, c, 1)
        share_piece(place, c).start()
    lax.fori_loop(0, half // GROUP, write_band, 0)
    own.wait()
    for load in loads:
        load.wait()
    for share in shares:
        share.wait_recv()
    last_load.start()

    def sum_piece(g, origin):
        where = span(origin, rows)
        return remote(
            outgoing.at[g, :, where],
            arrived.at[g, :, where],
            sum_send,
            sum_recv.at[g, origin],
            ctx=peer,
        )

    def group_of(far):
        return jnp.where(far == 1, across, pair)

    def project(origin, far):
        tokens = span(group_of(far), 2 * rows)

        def step(index, carry):
            g, column = lax.rem(index // tiles + 1, 3), lax.rem(index, tiles)
            where = span(column, tile)
            value = jnp.dot(
                slots[origin, tokens], planes[g, :, where], preferred_element_type=jnp.float32
            )

            def keep(target):
                for k in range(2):
                    target[g, k, span(origin, rows), where] = value[
                        k * rows : (k + 1) * rows
                    ].astype(target.dtype)

            @pl.when(far == 0)
            def _():
                keep(mine)

            @pl.when(far == 1)
            def _():
                keep(outgoing)

            @pl.when((far == 1) & (column == tiles - 1))
            def _():
                sum_piece(g, origin).start()

            return carry

        lax.fori_loop(0, 3 * tiles, step, 0)

    def combine(origin):
        where = span(origin, rows)
        for g in (1, 2, 0):
            sum_piece(g, origin).wait_recv()
        for k in range(2):
            q, key, value = [
                mine[g, k, where] + arrived[g, k, where].astype(jnp.float32) for g in range(3)
            ]
            mine[0, k, where] = q
            start = pl.multiple_of(taps + k * all_rows + origin * rows, rows)
            extended[pl.ds(start, rows), :] = (key * value).astype(jnp.bfloat16)

    def beside(distance, work):
        for origin in (place - distance, place + distance):

            @pl.when(line.inside(origin))
            def _(origin=origin):
                work(jnp.clip(origin, 0, shards - 1))

    def project_own(far, carry):
        @pl.when(far == 1)
        def _():
            for k in range(2):
                from_sibling(place, 2 * across + k).wait_recv()

        project(place, far)
        return carry

    lax.fori_loop(0, 2, project_own, 0)

    def from_side(distance, up):
        origin = place - distance * (2 * up - 1)
        return line.inside(origin), jnp.clip(origin, 0, shards - 1), origin == (1 - up) * (shards - 1)

    def far_at(distance, turn, last):
        return jnp.where(last & (distance > 1), 1 - turn, turn)

    def flow(distance, turn, up):
        there, origin, last = from_side(distance, up)
        held = last & (distance == 1)

        @pl.when(there)
        def _():
            group = group_of(far_at(distance, turn, last))
            for k in range(2):
                line.hop(origin, 2 * group + k, up).wait_recv()

                @pl.when(~held | (turn == 1))
                def _(k=k):
                    line.send(origin, 2 * group + k, up)

                share_piece(origin, 2 * group + k).start()

            @pl.when(held & (turn == 1))
            def _():
                for k in range(2):
                    line.send(origin, 2 * pair + k, up)

    def project_side(distance, turn, up):
        there, origin, last = from_side(distance, up)

        @pl.when(there)
        def _():
            far = far_at(distance, turn, last)
            for k in range(2):
                from_sibling(origin, 2 * group_of(far) + k).wait_recv()
            project(origin, far)

    def stage(distance, carry):
        def half_stage(turn, inner):
            flow(distance, turn, 1)
            flow(distance, turn, 0)

            def side(up, nothing):
                project_side(distance, turn, up)
                return nothing

            lax.fori_loop(0, 2, side, 0)
            return inner

        lax.fori_loop(0, 2, half_stage, 0)

        @pl.when(distance == 1)
        def _():
            combine(place)

        @pl.when(distance > 1)
        def _():
            beside(distance - 1, combine)

        return carry

    lax.fori_loop(1, shards, stage, 0)
    beside(shards - 1, combine)
    before = extended.at[pl.ds(0, taps)]
    tail = remote(
        extended.at[pl.ds(2 * all_rows, taps)], before, tail_send, tail_recv, ctx=peer
    )

    @pl.when(pair == 0)
    def _():
        tail.start()

    per, windows_count = LANES // GROUP, all_rows // taps

    def filter_lanes(k, block):
        where = span(block, LANES)
        values = extended[pl.ds(k * all_rows, taps + all_rows), where]
        windows = jnp.concatenate(
            [values[b * taps : (b + 2) * taps] for b in range(windows_count)], axis=1
        )
        lane = lax.broadcasted_iota(jnp.int32, windows.shape, 1)
        owner = lax.rem(lane, LANES) // GROUP
        sums = jnp.zeros((taps, windows_count * LANES), jnp.float32)
        for group in range(per):
            some = jnp.where(owner == group, windows, jnp.zeros_like(windows))
            sums = sums + jnp.dot(
                bands[block * per + group], some, preferred_element_type=jnp.float32
            )
        skip = skip_ref[:, pl.ds(pl.multiple_of(core * half + block * LANES, LANES), LANES)]
        for b in range(windows_count):
            direct = skip * values[(b + 1) * taps : (b + 2) * taps].astype(jnp.float32)
            filtered[pl.ds(b * taps, taps), where] = sums[:, b * LANES : (b + 1) * LANES] + direct

    gated_line = Line(
        shards, chunks, lambda origin, c: gated.at[origin, c], gated_send, gated_recv
    )
    mine_chunks = half // chunk

    def hand(i, owner):
        c = owner * mine_chunks + i
        return remote(handed.at[i], gated.at[place, c], hand_send, hand_recv.at[i], ctx=sibling)

    def gate_half(step, carry):
        k = 1 - step

        @pl.when((k == 0) & (pair == 1))
        def _():
            tail.wait_recv()

        def gate_chunk(i, inner):
            def lanes(block, nothing):
                filter_lanes(k, block)
                return nothing

            per_chunk = chunk // LANES
            lax.fori_loop(i * per_chunk, (i + 1) * per_chunk, lanes, 0)
            where, c = span(i, chunk), core * mine_chunks + i
            value = (mine[0, k, :, where] * filtered[:, where]).astype(jnp.bfloat16)

            @pl.when(k == core)
            def _():
                gated[place, c] = value
                gated_line.send(place, c, 0)
                gated_line.send(place, c, 1)

            @pl.when(k != core)
            def _():
                handed[i] = value
                hand(i, core).start()

            return inner

        lax.fori_loop(0, mine_chunks, gate_chunk, 0)
        return carry

    lax.fori_loop(0, 2, gate_half, 0)

    def take(i, carry):
        hand(i, 1 - core).wait_recv()
        c = (1 - core) * mine_chunks + i
        gated_line.send(place, c, 0)
        gated_line.send(place, c, 1)
        return carry

    lax.fori_loop(0, mine_chunks, take, 0)
    last_load.wait()
    wide = min(512, columns)

    def multiply(origin, c, fresh):
        deep = span(origin * chunks + c, chunk)

        def column(index, carry):
            where = span(index, wide)
            value = jnp.dot(
                gated[origin, c], weight[deep, where], preferred_element_type=jnp.float32
            )
            total[:, where] = value if fresh else total[:, where] + value
            return carry

        lax.fori_loop(0, columns // wide, column, 0)

    multiply(place, 0, True)

    def multiply_own(c, carry):
        multiply(place, c, False)
        return carry

    lax.fori_loop(1, chunks, multiply_own, 0)
    first_up = jnp.where(2 * place >= shards, 1, 0)

    def collect(index, carry):
        distance, side = index // (2 * chunks) + 1, lax.rem(index // chunks, 2)
        step = lax.rem(index, chunks)
        c = lax.rem(step + core * mine_chunks, chunks)
        up = lax.rem(first_up + side, 2)
        gated_line.pass_on(distance, c, up)
        origin = place - distance * (2 * up - 1)

        @pl.when(gated_line.inside(origin))
        def _():
            multiply(jnp.clip(origin, 0, shards - 1), c, False)

        return carry

    lax.fori_loop(0, 2 * chunks * (shards - 1), collect, 0)
    outs = []
    for index in range(columns // wide):
        where = pl.ds(index * wide, wide)
        result[:, where] = total[:, where].astype(jnp.bfloat16)
        outs.append(
            pltpu.make_async_copy(result.at[:, where], out_ref.at[:, where], out_sem.at[index])
        )
        outs[-1].start()
    for out in outs:
        out.wait()
    for swap in swaps:
        swap.wait_send()

    @pl.when(pair == 0)
    def _():
        tail.wait_send()

    line.sent()
    gated_line.sent()
    slices = slots.at[:, :, pl.ds(0, depth)]
    pltpu.make_async_copy(slices, slices, pair_send).wait()
    pltpu.make_async_copy(handed, handed, hand_send).wait()
    pltpu.make_async_copy(outgoing, outgoing, sum_send).wait()
    sent_planes = planes.at[:, pl.ds(0, depth)]
    pltpu.make_async_copy(sent_planes, sent_planes, planes_send).wait()


def on_paired_device(
    hidden_in, norm_gain, weight_in, filter_taps, filter_decay, skip_gain, tail_cache, output_weight
):
    shards, parts = lax.axis_size("tensor"), lax.axis_size("ctx")
    rows = hidden_in.shape[0]
    depth, _, channels = weight_in.shape
    groups, taps = filter_taps.shape
    columns = output_weight.shape[1]
    all_rows = shards * rows
    half = channels // 2
    chunk = min(256, half)
    chunks = channels // chunk
    anywhere = pl.BlockSpec(memory_space=pl.ANY)
    dma = pltpu.SemaphoreType.DMA
    bf16, f32 = jnp.bfloat16, jnp.float32
    return pl.pallas_call(
        functools.partial(paired_kernel, shards),
        out_shape=jax.ShapeDtypeStruct((all_rows, columns), bf16),
        in_specs=[anywhere] * 8,
        out_specs=anywhere,
        scratch_shapes=[
            pltpu.VMEM(hidden_in.shape, bf16),
            pltpu.VMEM((1, norm_gain.shape[0]), f32),
            pltpu.VMEM(filter_taps.shape, f32),
            pltpu.VMEM((1, groups), f32),
            pltpu.VMEM((1, channels), f32),
            pltpu.VMEM(tail_cache.shape, bf16),
            pltpu.VMEM((rows, hidden_in.shape[1]), bf16),
            pltpu.VMEM((groups, 2 * taps), f32),
            pltpu.VMEM((3, 2 * depth, half), bf16),
            pltpu.VMEM((shards, parts * rows, 2 * depth), bf16),
            pltpu.VMEM((3, 2, all_rows, half), f32),
            pltpu.VMEM((3, 2, all_rows, half), bf16),
            pltpu.VMEM((3, 2, all_rows, half), bf16),
            pltpu.VMEM((taps + 2 * all_rows, half), bf16),
            pltpu.VMEM((all_rows, half), f32),
            pltpu.VMEM((groups // 2, taps, 2 * taps), bf16),
            pltpu.VMEM(output_weight.shape, bf16),
            pltpu.VMEM((shards, chunks, all_rows, chunk), bf16),
            pltpu.VMEM((chunks // 2, all_rows, chunk), bf16),
            pltpu.VMEM((all_rows, columns), f32),
            pltpu.VMEM((all_rows, columns), bf16),
            dma((6,)),
            dma((columns // min(512, columns),)),
            dma((4,)),
            dma,
            dma,
            dma((3,)),
            dma((2,)),
            dma((2, shards, parts)),
            dma((shards, parts)),
            dma,
            dma((shards, parts)),
            dma,
            dma((3, shards)),
            dma,
            dma,
            dma,
            dma((chunks // 2,)),
            dma((2, shards, chunks)),
            dma((shards, chunks)),
        ],
        compiler_params=pltpu.CompilerParams(
            collective_id=0, has_side_effects=True, vmem_limit_bytes=58 << 20
        ),
    )(
        hidden_in,
        norm_gain.reshape(1, norm_gain.shape[0]),
        weight_in.transpose(1, 0, 2),
        filter_taps,
        filter_decay.reshape(1, groups),
        skip_gain.reshape(1, channels),
        tail_cache,
        output_weight,
    )


def on_device(
    hidden_in, norm_gain, weight_in, filter_taps, filter_decay, skip_gain, tail_cache, output_weight
):
    shards, parts = lax.axis_size("tensor"), lax.axis_size("ctx")
    rows = hidden_in.shape[0]
    depth, _, channels = weight_in.shape
    groups, taps = filter_taps.shape
    columns = output_weight.shape[1]
    all_rows = shards * rows
    chunk = min(256, channels)
    chunks = channels // chunk
    vmem, anywhere = pl.BlockSpec(memory_space=pltpu.VMEM), pl.BlockSpec(memory_space=pl.ANY)
    dma = pltpu.SemaphoreType.DMA
    bf16, f32 = jnp.bfloat16, jnp.float32
    return pl.pallas_call(
        functools.partial(mixer_kernel, shards, parts),
        out_shape=jax.ShapeDtypeStruct((all_rows, columns), bf16),
        in_specs=[vmem, vmem, anywhere, vmem, vmem, vmem, vmem, anywhere],
        out_specs=vmem,
        scratch_shapes=[
            pltpu.VMEM((rows, hidden_in.shape[1]), bf16),
            pltpu.VMEM((groups, 2 * taps), f32),
            pltpu.VMEM((3, depth, channels), bf16),
            pltpu.VMEM((shards, parts * rows, depth), bf16),
            pltpu.VMEM((3, shards, parts * rows, channels), bf16),
            pltpu.VMEM((3, parts - 1, all_rows, channels), bf16),
            pltpu.VMEM((all_rows, channels), f32),
            pltpu.VMEM((all_rows, channels), bf16),
            pltpu.VMEM((taps, channels), bf16),
            pltpu.VMEM((groups, taps, 2 * taps), bf16),
            pltpu.VMEM(output_weight.shape, bf16),
            pltpu.VMEM((shards, chunks, all_rows, chunk), bf16),
            pltpu.VMEM((all_rows, columns), f32),
            dma((4,)),
            dma,
            dma((parts - 1,)),
            dma((parts - 1,)),
            dma((2, shards, parts)),
            dma((shards, parts)),
            dma,
            dma((3,)),
            dma,
            dma,
            dma((2, shards, chunks)),
            dma((shards, chunks)),
        ],
        compiler_params=pltpu.CompilerParams(
            collective_id=0, has_side_effects=True, vmem_limit_bytes=56 << 20
        ),
    )(
        hidden_in,
        norm_gain.reshape(1, norm_gain.shape[0]),
        weight_in.transpose(1, 0, 2),
        filter_taps,
        filter_decay.reshape(1, groups),
        skip_gain.reshape(1, channels),
        tail_cache,
        output_weight,
    )


def solution(mesh):
    in_specs = (
        P(("prompt", "ctx", "tensor"), None),
        P(),
        P("ctx", None, "tensor"),
        P("tensor", None),
        P("tensor"),
        P("tensor"),
        P("prompt", "tensor"),
        P(None, "tensor"),
    )
    out_specs = P(("prompt", "ctx"), "tensor")
    paired = mesh.shape["ctx"] == 4
    return jax.shard_map(
        on_paired_device if paired else on_device, mesh=mesh, in_specs=in_specs, out_specs=out_specs, check_vma=False
    )
```

```python
import functools

import jax
import jax.numpy as jnp
from jax import lax
from jax.experimental import pallas as pl
from jax.experimental.pallas import tpu as pltpu
from jax.sharding import PartitionSpec as P

GROUP = 16
LANES = 128
MESH = pl.DeviceIdType.MESH


def span(index, size):
    return pl.ds(pl.multiple_of(index * size, size), size)


def greet(peers):
    barrier = pltpu.get_barrier_semaphore()
    for axis, peer, there in peers:

        @pl.when(there)
        def _(axis=axis, peer=peer):
            pl.semaphore_signal(barrier, inc=1, device_id={axis: peer}, device_id_type=MESH)

    return sum(jnp.where(there, 1, 0) for _, _, there in peers)


def normalize_rows(hidden_ref, gain_ref, normed):
    rows, width = hidden_ref.shape
    few, part = min(16, rows), 1024

    def step(index, carry):
        where = span(index, few)

        def values(start):
            return hidden_ref[where, pl.ds(start, part)].astype(jnp.float32)

        squares = jnp.zeros((few, part), jnp.float32)
        for start in range(0, width, part):
            squares = squares + values(start) * values(start)
        scaled = lax.rsqrt(jnp.sum(squares, axis=-1, keepdims=True) / width + 1e-06)
        for start in range(0, width, part):
            inner = pl.ds(start, part)
            normed[where, inner] = (values(start) * scaled * gain_ref[:, inner]).astype(
                jnp.bfloat16
            )
        return carry

    lax.fori_loop(0, rows // few, step, 0)


def first_rows(taps_ref, decay_ref):
    groups, taps = taps_ref.shape
    lags = lax.broadcasted_iota(jnp.int32, (groups, taps), 1).astype(jnp.float32)
    across = lax.broadcasted_iota(jnp.int32, (groups, groups), 1)
    down = lax.broadcasted_iota(jnp.int32, (groups, groups), 0)
    decay = jnp.sum(jnp.where(across == down, decay_ref[...], 0.0), axis=1, keepdims=True)
    taps_full = (taps_ref[...] * jnp.exp(-decay * lags)).astype(jnp.bfloat16)
    lag = lax.broadcasted_iota(jnp.int32, (taps, 2 * taps), 0)
    column = lax.broadcasted_iota(jnp.int32, (taps, 2 * taps), 1)
    turned = jnp.where(lag + column == taps, 1.0, 0.0).astype(jnp.bfloat16)
    return jnp.dot(taps_full, turned, preferred_element_type=jnp.float32)


class Line:
    def __init__(self, count, pieces, view, send_sem, recv_sem):
        self.count, self.pieces, self.view = count, pieces, view
        self.send_sem, self.recv_sem = send_sem, recv_sem
        self.place = lax.axis_index("tensor")

    def inside(self, position):
        return (position >= 0) & (position < self.count)

    def hop(self, origin, piece, up, source=None):
        ref = self.view(origin, piece)
        return pltpu.make_async_remote_copy(
            src_ref=ref if source is None else source,
            dst_ref=ref,
            send_sem=self.send_sem.at[up, origin, piece],
            recv_sem=self.recv_sem.at[origin, piece],
            device_id={"tensor": jnp.clip(self.place + 2 * up - 1, 0, self.count - 1)},
            device_id_type=MESH,
        )

    def send(self, origin, piece, up, source=None):
        @pl.when(self.inside(self.place + 2 * up - 1))
        def _():
            self.hop(origin, piece, up, source).start()

    def pass_on(self, distance, piece, up):
        origin = self.place - distance * (2 * up - 1)

        @pl.when(self.inside(origin))
        def _():
            source = jnp.clip(origin, 0, self.count - 1)
            self.hop(source, piece, up).wait_recv()
            self.send(source, piece, up)

    def sent(self):
        def step(index, carry):
            origin, piece = index // self.pieces, lax.rem(index, self.pieces)

            @pl.when((origin <= self.place) & (self.place + 1 < self.count))
            def _():
                self.hop(origin, piece, 1).wait_send()

            @pl.when((origin >= self.place) & (self.place > 0))
            def _():
                self.hop(origin, piece, 0).wait_send()

            return carry

        lax.fori_loop(0, self.count * self.pieces, step, 0)


def mixer_kernel(
    shards,
    parts,
    hidden_ref,
    gain_ref,
    planes_ref,
    taps_ref,
    decay_ref,
    skip_ref,
    tail_ref,
    weight_ref,
    out_ref,
    normed,
    first,
    planes,
    slots,
    partial,
    arrived,
    filtered,
    product,
    before,
    bands,
    weight,
    gated,
    total,
    load_sem,
    own_sem,
    swap_send,
    swap_recv,
    line_send,
    line_recv,
    sum_send,
    sum_recv,
    tail_send,
    tail_recv,
    gated_send,
    gated_recv,
):
    rows = hidden_ref.shape[0]
    _, depth, channels = planes.shape
    groups, taps, _ = bands.shape
    chunks, all_rows, chunk = gated.shape[1:]
    columns = out_ref.shape[1]
    tile = min(256, channels)
    me, place = lax.axis_index("ctx"), lax.axis_index("tensor")
    others = [lax.rem(me + 1 + k, parts) for k in range(parts - 1)]

    loads = [
        pltpu.make_async_copy(planes_ref.at[g], planes.at[g], load_sem.at[g]) for g in (1, 2, 0)
    ]
    for load in loads:
        load.start()
    last_load = pltpu.make_async_copy(weight_ref, weight, load_sem.at[3])
    last_load.start()
    neighbours = [
        ("tensor", jnp.maximum(place - 1, 0), place > 0),
        ("tensor", jnp.minimum(place + 1, shards - 1), place < shards - 1),
    ]
    greeted = greet([("ctx", other, me >= 0) for other in others] + neighbours)
    normalize_rows(hidden_ref, gain_ref, normed)
    own = pltpu.make_async_copy(
        normed.at[:, span(me, depth)], slots.at[place, span(me, rows)], own_sem
    )
    own.start()
    pl.semaphore_wait(pltpu.get_barrier_semaphore(), greeted)

    swaps = [
        pltpu.make_async_remote_copy(
            src_ref=normed.at[:, span(other, depth)],
            dst_ref=slots.at[place, span(me, rows)],
            send_sem=swap_send.at[k],
            recv_sem=swap_recv.at[parts - 2 - k],
            device_id={"ctx": other},
            device_id_type=MESH,
        )
        for k, other in enumerate(others)
    ]
    for swap in swaps:
        swap.start()
    line = Line(
        shards, parts, lambda origin, c: slots.at[origin, span(c, rows)], line_send, line_recv
    )
    own.wait()
    line.send(place, me, 0)
    line.send(place, me, 1)

    first[...] = first_rows(taps_ref, decay_ref)

    @pl.when(me == 0)
    def _():
        padding = jnp.zeros((taps - tail_ref.shape[0], channels), jnp.float32)
        before[...] = jnp.concatenate(
            [padding, tail_ref[...].astype(jnp.float32)], axis=0
        ).astype(jnp.bfloat16)

    for k in range(parts - 1):
        swaps[parts - 2 - k].wait_recv()
        line.send(place, others[k], 0)
        line.send(place, others[k], 1)

    def write_band(group, carry):
        row = jnp.broadcast_to(first[pl.ds(group, 1), :], (taps, 2 * taps))
        bands[group] = pltpu.roll(row, 0, 1, stride=1, stride_axis=0).astype(jnp.bfloat16)
        return carry

    lax.fori_loop(0, groups, write_band, 0)
    for load in loads:
        load.wait()

    tiles = channels // tile

    def project(origin, k):
        def step(index, carry):
            g, column = lax.rem(index // tiles + 1, 3), lax.rem(index, tiles)
            where = span(column, tile)
            partial[g, origin, :, where] = jnp.dot(
                slots[origin], planes[g, :, where], preferred_element_type=jnp.float32
            ).astype(jnp.bfloat16)

            @pl.when(column == tiles - 1)
            def _():
                for k, other in enumerate(others):
                    pltpu.make_async_remote_copy(
                        src_ref=partial.at[g, origin, span(other, rows)],
                        dst_ref=arrived.at[g, parts - 2 - k, span(origin, rows)],
                        send_sem=sum_send,
                        recv_sem=sum_recv.at[g],
                        device_id={"ctx": other},
                        device_id_type=MESH,
                    ).start()

            return carry

        steps = 3 * tiles
        lax.fori_loop(k * steps // parts, (k + 1) * steps // parts, step, 0)

    def project_from(distance, k):
        below, above = place - distance, place + distance

        @pl.when(line.inside(below))
        def _():
            project(jnp.maximum(below, 0), k)

        @pl.when(line.inside(above) & (distance > 0))
        def _():
            project(jnp.minimum(above, shards - 1), k)

    def project_piece(origin, piece):
        mine = span(piece, rows)

        def plane(step, carry):
            g = lax.rem(step + 1, 3)

            def columns(column, inner):
                where = span(column, tile)
                partial[g, origin, mine, where] = jnp.dot(
                    slots[origin, mine], planes[g, :, where], preferred_element_type=jnp.float32
                ).astype(jnp.bfloat16)
                return inner

            lax.fori_loop(0, tiles, columns, 0)

            @pl.when(piece != me)
            def _():
                slot = jnp.clip(lax.rem(me - piece - 1 + parts, parts), 0, parts - 2)
                pltpu.make_async_remote_copy(
                    src_ref=partial.at[g, origin, mine],
                    dst_ref=arrived.at[g, slot, span(origin, rows)],
                    send_sem=sum_send,
                    recv_sem=sum_recv.at[g],
                    device_id={"ctx": piece},
                    device_id_type=MESH,
                ).start()

            return carry

        lax.fori_loop(0, 3, plane, 0)

    def stage(index, carry):
        distance, k = index // parts, lax.rem(index, parts)
        project_from(distance, k)
        piece = lax.rem(me + k, parts)
        line.pass_on(distance + 1, piece, 1)
        line.pass_on(distance + 1, piece, 0)

        @pl.when((distance == shards - 2) & ((place == 0) | (place == shards - 1)))
        def _():
            project_piece(shards - 1 - place, piece)

        return carry

    lax.fori_loop(0, (shards - 1) * parts, stage, 0)

    def summed(g, origin, where=slice(None)):
        value = partial[g, origin, span(me, rows), where].astype(jnp.float32)
        for k in range(parts - 1):
            value = value + arrived[g, k, span(origin, rows), where].astype(jnp.float32)
        return value

    for g in (1, 2):
        pltpu.make_async_copy(arrived.at[g], arrived.at[g], sum_recv.at[g]).wait()

    def write_product(step, carry):
        origin = shards - 1 - step
        product[span(origin, rows), :] = (summed(1, origin) * summed(2, origin)).astype(
            jnp.bfloat16
        )
        return carry

    tail_steps = -(-taps // rows)
    lax.fori_loop(0, tail_steps, write_product, 0)
    tail = pltpu.make_async_remote_copy(
        src_ref=product.at[pl.ds(all_rows - taps, taps)],
        dst_ref=before,
        send_sem=tail_send,
        recv_sem=tail_recv,
        device_id={"ctx": jnp.minimum(me + 1, parts - 1)},
        device_id_type=MESH,
    )

    @pl.when(me + 1 < parts)
    def _():
        tail.start()

    lax.fori_loop(tail_steps, shards, write_product, 0)
    @pl.when(me > 0)
    def _():
        tail.wait_recv()

    per, windows_count = LANES // GROUP, all_rows // taps

    def filter_lanes(block, carry):
        where = span(block, LANES)
        extended = jnp.concatenate([before[:, where], product[:, where]], axis=0)
        windows = jnp.concatenate(
            [extended[b * taps : (b + 2) * taps] for b in range(windows_count)], axis=1
        )
        lane = lax.broadcasted_iota(jnp.int32, windows.shape, 1)
        owner = lax.rem(lane, LANES) // GROUP
        sums = jnp.zeros((taps, windows_count * LANES), jnp.float32)
        for group in range(per):
            mine = jnp.where(owner == group, windows, jnp.zeros_like(windows))
            sums = sums + jnp.dot(
                bands[block * per + group], mine, preferred_element_type=jnp.float32
            )
        for b in range(windows_count):
            inner = pl.ds(b * taps, taps)
            direct = skip_ref[:, where] * product[inner, where].astype(jnp.float32)
            filtered[inner, where] = sums[:, b * LANES : (b + 1) * LANES] + direct
        return carry

    lax.fori_loop(0, channels // LANES, filter_lanes, 0)
    pltpu.make_async_copy(arrived.at[0], arrived.at[0], sum_recv.at[0]).wait()

    gated_line = Line(
        shards, chunks, lambda origin, c: gated.at[origin, c], gated_send, gated_recv
    )

    def gate_chunk(c, carry):
        where = span(c, chunk)

        def gate(origin, inner):
            mine = span(origin, rows)
            gated[place, c, mine, :] = (
                summed(0, origin, where) * filtered[mine, where]
            ).astype(jnp.bfloat16)
            return inner

        lax.fori_loop(0, shards, gate, 0)
        gated_line.send(place, c, 0)
        gated_line.send(place, c, 1)
        return carry

    lax.fori_loop(0, chunks, gate_chunk, 0)
    last_load.wait()
    wide = min(512, columns)

    def multiply(origin, c, fresh):
        deep = span(origin * chunks + c, chunk)

        def column(index, carry):
            where = span(index, wide)
            value = jnp.dot(
                gated[origin, c], weight[deep, where], preferred_element_type=jnp.float32
            )
            total[:, where] = value if fresh else total[:, where] + value
            return carry

        lax.fori_loop(0, columns // wide, column, 0)

    multiply(place, 0, True)

    def multiply_own(c, carry):
        multiply(place, c, False)
        return carry

    lax.fori_loop(1, chunks, multiply_own, 0)
    first_up = jnp.where(2 * place >= shards, 1, 0)

    def collect(index, carry):
        distance, side = index // (2 * chunks) + 1, lax.rem(index // chunks, 2)
        c = lax.rem(index, chunks)
        up = lax.rem(first_up + side, 2)
        gated_line.pass_on(distance, c, up)
        origin = place - distance * (2 * up - 1)

        @pl.when(gated_line.inside(origin))
        def _():
            multiply(jnp.clip(origin, 0, shards - 1), c, False)

        return carry

    lax.fori_loop(0, 2 * chunks * (shards - 1), collect, 0)
    out_ref[...] = total[...].astype(jnp.bfloat16)

    for swap in swaps:
        swap.wait_send()

    @pl.when(me + 1 < parts)
    def _():
        tail.wait_send()

    line.sent()
    gated_line.sent()
    pltpu.make_async_copy(arrived, arrived, sum_send).wait()


def paired_kernel(
    shards,
    hidden_in,
    gain_in,
    planes_ref,
    taps_in,
    decay_in,
    skip_in,
    tail_in,
    weight_ref,
    out_ref,
    hidden_ref,
    gain_ref,
    taps_ref,
    decay_ref,
    skip_ref,
    tail_ref,
    normed,
    first,
    planes,
    slots,
    mine,
    outgoing,
    arrived,
    extended,
    filtered,
    bands,
    weight,
    gated,
    handed,
    total,
    input_sem,
    load_sem,
    own_sem,
    planes_send,
    planes_recv,
    swap_send,
    line_send,
    line_recv,
    pair_send,
    pair_recv,
    sum_send,
    sum_recv,
    tail_send,
    tail_recv,
    hand_send,
    hand_recv,
    gated_send,
    gated_recv,
):
    rows = hidden_ref.shape[0]
    parts = slots.shape[1] // rows
    _, both_depths, half = planes.shape
    depth = both_depths // 2
    _, taps, _ = bands.shape
    chunks, all_rows, chunk = gated.shape[1:]
    columns = out_ref.shape[1]
    tile = min(256, half)
    tiles = half // tile
    me, place = lax.axis_index("ctx"), lax.axis_index("tensor")
    pair, core = me // 2, lax.rem(me, 2)
    across = 1 - pair
    sibling, peer = 2 * pair + 1 - core, 2 * across + core

    others = [lax.rem(me + 1 + k, parts) for k in range(parts - 1)]
    neighbours = [
        ("tensor", jnp.maximum(place - 1, 0), place > 0),
        ("tensor", jnp.minimum(place + 1, shards - 1), place < shards - 1),
    ]
    greeted = greet([("ctx", other, me >= 0) for other in others] + neighbours)
    inputs = [
        pltpu.make_async_copy(source, target, input_sem.at[k])
        for k, (source, target) in enumerate(
            [
                (hidden_in, hidden_ref),
                (gain_in, gain_ref),
                (taps_in, taps_ref),
                (decay_in, decay_ref),
                (skip_in, skip_ref),
                (tail_in, tail_ref),
            ]
        )
    ]
    for load in inputs:
        load.start()
    loads = [
        pltpu.make_async_copy(
            planes_ref.at[g, :, span(core, half)], planes.at[g, span(core, depth)], load_sem.at[g]
        )
        for g in (1, 2, 0)
    ]
    for load in loads:
        load.start()
    last_load = pltpu.make_async_copy(weight_ref, weight, load_sem.at[3])
    for load in inputs[:2]:
        load.wait()
    normalize_rows(hidden_ref, gain_ref, normed)
    mine_in = normed.at[:, span(pair, both_depths)]
    own = pltpu.make_async_copy(mine_in, slots.at[place, span(me, rows)], own_sem)
    own.start()
    pl.semaphore_wait(pltpu.get_barrier_semaphore(), greeted)

    def remote(source, target, send, recv, **device):
        return pltpu.make_async_remote_copy(
            src_ref=source,
            dst_ref=target,
            send_sem=send,
            recv_sem=recv,
            device_id=device,
            device_id_type=MESH,
        )

    line = Line(
        shards,
        parts,
        lambda origin, c: slots.at[origin, span(c, rows), span(core, depth)],
        line_send,
        line_recv,
    )
    line.send(place, me, 0, normed.at[:, span(me, depth)])
    line.send(place, me, 1, normed.at[:, span(me, depth)])
    to_sibling = remote(
        mine_in, slots.at[place, span(me, rows)], pair_send, pair_recv.at[place, me], ctx=sibling
    )
    to_sibling.start()
    swaps = [
        remote(
            normed.at[:, span(2 * across + k, depth)],
            slots.at[place, span(me, rows), pl.ds(k * depth, depth)],
            swap_send.at[k],
            line_recv.at[place, me],
            ctx=2 * across + k,
        )
        for k in range(2)
    ]
    for swap in swaps:
        swap.start()
    shares = [
        remote(
            planes_ref.at[g, :, span(1 - core, half)],
            planes.at[g, span(core, depth)],
            planes_send,
            planes_recv.at[g],
            ctx=sibling,
        )
        for g in (1, 2, 0)
    ]
    for share in shares:
        share.start()

    def share_piece(origin, c):
        ref = slots.at[origin, span(c, rows), span(core, depth)]
        return remote(ref, ref, pair_send, pair_recv.at[origin, c], ctx=sibling)

    def from_sibling(origin, c):
        ref = slots.at[origin, span(c, rows), span(1 - core, depth)]
        return remote(ref, ref, pair_send, pair_recv.at[origin, c], ctx=sibling)

    for load in inputs[2:]:
        load.wait()
    first[...] = first_rows(taps_ref, decay_ref)

    @pl.when(pair == 0)
    def _():
        padding = jnp.zeros((taps - tail_ref.shape[0], half), jnp.float32)
        extended[pl.ds(0, taps), :] = jnp.concatenate(
            [padding, tail_ref[:, span(core, half)].astype(jnp.float32)], axis=0
        ).astype(jnp.bfloat16)

    remote(
        mine_in,
        slots.at[place, span(sibling, rows)],
        pair_send,
        pair_recv.at[place, sibling],
        ctx=sibling,
    ).wait_recv()
    line.send(place, sibling, 0)
    line.send(place, sibling, 1)

    def write_band(group, carry):
        row = jnp.broadcast_to(first[pl.ds(core * (half // GROUP) + group, 1), :], (taps, 2 * taps))
        bands[group] = pltpu.roll(row, 0, 1, stride=1, stride_axis=0).astype(jnp.bfloat16)
        return carry

    for k in range(2):
        c = 2 * across + k
        line.hop(place, c, 1).wait_recv()
        line.send(place, c, 0)
        line.send(place, c, 1)
        share_piece(place, c).start()
    lax.fori_loop(0, half // GROUP, write_band, 0)
    own.wait()
    for load in loads:
        load.wait()
    for share in shares:
        share.wait_recv()
    last_load.start()

    def sum_piece(g, origin):
        where = span(origin, rows)
        return remote(
            outgoing.at[g, :, where],
            arrived.at[g, :, where],
            sum_send,
            sum_recv.at[g, origin],
            ctx=peer,
        )

    def group_of(far):
        return jnp.where(far == 1, across, pair)

    def project(origin, far):
        tokens = span(group_of(far), 2 * rows)

        def step(index, carry):
            g, column = lax.rem(index // tiles + 1, 3), lax.rem(index, tiles)
            where = span(column, tile)
            value = jnp.dot(
                slots[origin, tokens], planes[g, :, where], preferred_element_type=jnp.float32
            )

            def keep(target):
                for k in range(2):
                    target[g, k, span(origin, rows), where] = value[
                        k * rows : (k + 1) * rows
                    ].astype(target.dtype)

            @pl.when(far == 0)
            def _():
                keep(mine)

            @pl.when(far == 1)
            def _():
                keep(outgoing)

            @pl.when((far == 1) & (column == tiles - 1))
            def _():
                sum_piece(g, origin).start()

            return carry

        lax.fori_loop(0, 3 * tiles, step, 0)

    def combine(origin):
        where = span(origin, rows)
        for g in (1, 2, 0):
            sum_piece(g, origin).wait_recv()
        for k in range(2):
            q, key, value = [
                mine[g, k, where] + arrived[g, k, where].astype(jnp.float32) for g in range(3)
            ]
            mine[0, k, where] = q
            start = pl.multiple_of(taps + k * all_rows + origin * rows, rows)
            extended[pl.ds(start, rows), :] = (key * value).astype(jnp.bfloat16)

    def beside(distance, work):
        for origin in (place - distance, place + distance):

            @pl.when(line.inside(origin))
            def _(origin=origin):
                work(jnp.clip(origin, 0, shards - 1))

    def project_own(far, carry):
        @pl.when(far == 1)
        def _():
            for k in range(2):
                from_sibling(place, 2 * across + k).wait_recv()

        project(place, far)
        return carry

    lax.fori_loop(0, 2, project_own, 0)

    def from_side(distance, up):
        origin = place - distance * (2 * up - 1)
        return line.inside(origin), jnp.clip(origin, 0, shards - 1), origin == (1 - up) * (shards - 1)

    def far_at(distance, turn, last):
        return jnp.where(last & (distance > 1), 1 - turn, turn)

    def flow(distance, turn, up):
        there, origin, last = from_side(distance, up)
        held = last & (distance == 1)

        @pl.when(there)
        def _():
            group = group_of(far_at(distance, turn, last))
            for k in range(2):
                line.hop(origin, 2 * group + k, up).wait_recv()

                @pl.when(~held | (turn == 1))
                def _(k=k):
                    line.send(origin, 2 * group + k, up)

                share_piece(origin, 2 * group + k).start()

            @pl.when(held & (turn == 1))
            def _():
                for k in range(2):
                    line.send(origin, 2 * pair + k, up)

    def project_side(distance, turn, up):
        there, origin, last = from_side(distance, up)

        @pl.when(there)
        def _():
            far = far_at(distance, turn, last)
            for k in range(2):
                from_sibling(origin, 2 * group_of(far) + k).wait_recv()
            project(origin, far)

    def stage(distance, carry):
        def half_stage(turn, inner):
            flow(distance, turn, 1)
            flow(distance, turn, 0)

            def side(up, nothing):
                project_side(distance, turn, up)
                return nothing

            lax.fori_loop(0, 2, side, 0)
            return inner

        lax.fori_loop(0, 2, half_stage, 0)

        @pl.when(distance == 1)
        def _():
            combine(place)

        @pl.when(distance > 1)
        def _():
            beside(distance - 1, combine)

        return carry

    lax.fori_loop(1, shards, stage, 0)
    beside(shards - 1, combine)
    before = extended.at[pl.ds(0, taps)]
    tail = remote(
        extended.at[pl.ds(2 * all_rows, taps)], before, tail_send, tail_recv, ctx=peer
    )

    @pl.when(pair == 0)
    def _():
        tail.start()

    per, windows_count = LANES // GROUP, all_rows // taps

    def filter_lanes(k, block):
        where = span(block, LANES)
        values = extended[pl.ds(k * all_rows, taps + all_rows), where]
        windows = jnp.concatenate(
            [values[b * taps : (b + 2) * taps] for b in range(windows_count)], axis=1
        )
        lane = lax.broadcasted_iota(jnp.int32, windows.shape, 1)
        owner = lax.rem(lane, LANES) // GROUP
        sums = jnp.zeros((taps, windows_count * LANES), jnp.float32)
        for group in range(per):
            some = jnp.where(owner == group, windows, jnp.zeros_like(windows))
            sums = sums + jnp.dot(
                bands[block * per + group], some, preferred_element_type=jnp.float32
            )
        skip = skip_ref[:, pl.ds(pl.multiple_of(core * half + block * LANES, LANES), LANES)]
        for b in range(windows_count):
            direct = skip * values[(b + 1) * taps : (b + 2) * taps].astype(jnp.float32)
            filtered[pl.ds(b * taps, taps), where] = sums[:, b * LANES : (b + 1) * LANES] + direct

    gated_line = Line(
        shards, chunks, lambda origin, c: gated.at[origin, c], gated_send, gated_recv
    )
    mine_chunks = half // chunk

    def hand(i, owner):
        c = owner * mine_chunks + i
        return remote(handed.at[i], gated.at[place, c], hand_send, hand_recv.at[i], ctx=sibling)

    def gate_half(step, carry):
        k = 1 - step

        @pl.when((k == 0) & (pair == 1))
        def _():
            tail.wait_recv()

        def gate_chunk(i, inner):
            def lanes(block, nothing):
                filter_lanes(k, block)
                return nothing

            per_chunk = chunk // LANES
            lax.fori_loop(i * per_chunk, (i + 1) * per_chunk, lanes, 0)
            where, c = span(i, chunk), core * mine_chunks + i
            value = (mine[0, k, :, where] * filtered[:, where]).astype(jnp.bfloat16)

            @pl.when(k == core)
            def _():
                gated[place, c] = value
                gated_line.send(place, c, 0)
                gated_line.send(place, c, 1)

            @pl.when(k != core)
            def _():
                handed[i] = value
                hand(i, core).start()

            return inner

        lax.fori_loop(0, mine_chunks, gate_chunk, 0)
        return carry

    lax.fori_loop(0, 2, gate_half, 0)

    def take(i, carry):
        hand(i, 1 - core).wait_recv()
        c = (1 - core) * mine_chunks + i
        gated_line.send(place, c, 0)
        gated_line.send(place, c, 1)
        return carry

    lax.fori_loop(0, mine_chunks, take, 0)
    last_load.wait()
    wide = min(512, columns)

    def multiply(origin, c, fresh):
        deep = span(origin * chunks + c, chunk)

        def column(index, carry):
            where = span(index, wide)
            value = jnp.dot(
                gated[origin, c], weight[deep, where], preferred_element_type=jnp.float32
            )
            total[:, where] = value if fresh else total[:, where] + value
            return carry

        lax.fori_loop(0, columns // wide, column, 0)

    multiply(place, 0, True)

    def multiply_own(c, carry):
        multiply(place, c, False)
        return carry

    lax.fori_loop(1, chunks, multiply_own, 0)
    first_up = jnp.where(2 * place >= shards, 1, 0)

    def collect(index, carry):
        distance, side = index // (2 * chunks) + 1, lax.rem(index // chunks, 2)
        step = lax.rem(index, chunks)
        c = lax.rem(step + core * mine_chunks, chunks)
        up = lax.rem(first_up + side, 2)
        gated_line.pass_on(distance, c, up)
        origin = place - distance * (2 * up - 1)

        @pl.when(gated_line.inside(origin))
        def _():
            multiply(jnp.clip(origin, 0, shards - 1), c, False)

        return carry

    lax.fori_loop(0, 2 * chunks * (shards - 1), collect, 0)
    for index in range(columns // wide):
        where = pl.ds(index * wide, wide)
        out_ref[:, where] = total[:, where].astype(jnp.bfloat16)

    for swap in swaps:
        swap.wait_send()

    @pl.when(pair == 0)
    def _():
        tail.wait_send()

    line.sent()
    gated_line.sent()
    slices = slots.at[:, :, pl.ds(0, depth)]
    pltpu.make_async_copy(slices, slices, pair_send).wait()
    pltpu.make_async_copy(handed, handed, hand_send).wait()
    pltpu.make_async_copy(outgoing, outgoing, sum_send).wait()
    sent_planes = planes.at[:, pl.ds(0, depth)]
    pltpu.make_async_copy(sent_planes, sent_planes, planes_send).wait()


def on_paired_device(
    hidden_in, norm_gain, weight_in, filter_taps, filter_decay, skip_gain, tail_cache, output_weight
):
    shards, parts = lax.axis_size("tensor"), lax.axis_size("ctx")
    rows = hidden_in.shape[0]
    depth, _, channels = weight_in.shape
    groups, taps = filter_taps.shape
    columns = output_weight.shape[1]
    all_rows = shards * rows
    half = channels // 2
    chunk = min(256, half)
    chunks = channels // chunk
    anywhere = pl.BlockSpec(memory_space=pl.ANY)
    dma = pltpu.SemaphoreType.DMA
    bf16, f32 = jnp.bfloat16, jnp.float32
    return pl.pallas_call(
        functools.partial(paired_kernel, shards),
        out_shape=pltpu.VMEM((all_rows, columns), bf16),
        in_specs=[anywhere] * 8,
        out_specs=pl.BlockSpec(memory_space=pltpu.VMEM),
        scratch_shapes=[
            pltpu.VMEM(hidden_in.shape, bf16),
            pltpu.VMEM((1, norm_gain.shape[0]), f32),
            pltpu.VMEM(filter_taps.shape, f32),
            pltpu.VMEM((1, groups), f32),
            pltpu.VMEM((1, channels), f32),
            pltpu.VMEM(tail_cache.shape, bf16),
            pltpu.VMEM((rows, hidden_in.shape[1]), bf16),
            pltpu.VMEM((groups, 2 * taps), f32),
            pltpu.VMEM((3, 2 * depth, half), bf16),
            pltpu.VMEM((shards, parts * rows, 2 * depth), bf16),
            pltpu.VMEM((3, 2, all_rows, half), f32),
            pltpu.VMEM((3, 2, all_rows, half), bf16),
            pltpu.VMEM((3, 2, all_rows, half), bf16),
            pltpu.VMEM((taps + 2 * all_rows, half), bf16),
            pltpu.VMEM((all_rows, half), f32),
            pltpu.VMEM((groups // 2, taps, 2 * taps), bf16),
            pltpu.VMEM(output_weight.shape, bf16),
            pltpu.VMEM((shards, chunks, all_rows, chunk), bf16),
            pltpu.VMEM((chunks // 2, all_rows, chunk), bf16),
            pltpu.VMEM((all_rows, columns), f32),
            dma((6,)),
            dma((4,)),
            dma,
            dma,
            dma((3,)),
            dma((2,)),
            dma((2, shards, parts)),
            dma((shards, parts)),
            dma,
            dma((shards, parts)),
            dma,
            dma((3, shards)),
            dma,
            dma,
            dma,
            dma((chunks // 2,)),
            dma((2, shards, chunks)),
            dma((shards, chunks)),
        ],
        compiler_params=pltpu.CompilerParams(
            collective_id=0, has_side_effects=True, vmem_limit_bytes=54 << 20
        ),
    )(
        hidden_in,
        norm_gain.reshape(1, norm_gain.shape[0]),
        weight_in.transpose(1, 0, 2),
        filter_taps,
        filter_decay.reshape(1, groups),
        skip_gain.reshape(1, channels),
        tail_cache,
        output_weight,
    )


def on_device(
    hidden_in, norm_gain, weight_in, filter_taps, filter_decay, skip_gain, tail_cache, output_weight
):
    shards, parts = lax.axis_size("tensor"), lax.axis_size("ctx")
    rows = hidden_in.shape[0]
    depth, _, channels = weight_in.shape
    groups, taps = filter_taps.shape
    columns = output_weight.shape[1]
    all_rows = shards * rows
    chunk = min(256, channels)
    chunks = channels // chunk
    vmem, anywhere = pl.BlockSpec(memory_space=pltpu.VMEM), pl.BlockSpec(memory_space=pl.ANY)
    dma = pltpu.SemaphoreType.DMA
    bf16, f32 = jnp.bfloat16, jnp.float32
    return pl.pallas_call(
        functools.partial(mixer_kernel, shards, parts),
        out_shape=jax.ShapeDtypeStruct((all_rows, columns), bf16),
        in_specs=[vmem, vmem, anywhere, vmem, vmem, vmem, vmem, anywhere],
        out_specs=vmem,
        scratch_shapes=[
            pltpu.VMEM((rows, hidden_in.shape[1]), bf16),
            pltpu.VMEM((groups, 2 * taps), f32),
            pltpu.VMEM((3, depth, channels), bf16),
            pltpu.VMEM((shards, parts * rows, depth), bf16),
            pltpu.VMEM((3, shards, parts * rows, channels), bf16),
            pltpu.VMEM((3, parts - 1, all_rows, channels), bf16),
            pltpu.VMEM((all_rows, channels), f32),
            pltpu.VMEM((all_rows, channels), bf16),
            pltpu.VMEM((taps, channels), bf16),
            pltpu.VMEM((groups, taps, 2 * taps), bf16),
            pltpu.VMEM(output_weight.shape, bf16),
            pltpu.VMEM((shards, chunks, all_rows, chunk), bf16),
            pltpu.VMEM((all_rows, columns), f32),
            dma((4,)),
            dma,
            dma((parts - 1,)),
            dma((parts - 1,)),
            dma((2, shards, parts)),
            dma((shards, parts)),
            dma,
            dma((3,)),
            dma,
            dma,
            dma((2, shards, chunks)),
            dma((shards, chunks)),
        ],
        compiler_params=pltpu.CompilerParams(
            collective_id=0, has_side_effects=True, vmem_limit_bytes=56 << 20
        ),
    )(
        hidden_in,
        norm_gain.reshape(1, norm_gain.shape[0]),
        weight_in.transpose(1, 0, 2),
        filter_taps,
        filter_decay.reshape(1, groups),
        skip_gain.reshape(1, channels),
        tail_cache,
        output_weight,
    )


def solution(mesh):
    in_specs = (
        P(("prompt", "ctx", "tensor"), None),
        P(),
        P("ctx", None, "tensor"),
        P("tensor", None),
        P("tensor"),
        P("tensor"),
        P("prompt", "tensor"),
        P(None, "tensor"),
    )
    out_specs = P(("prompt", "ctx"), "tensor")
    paired = mesh.shape["ctx"] == 4
    return jax.shard_map(
        on_paired_device if paired else on_device, mesh=mesh, in_specs=in_specs, out_specs=out_specs, check_vma=False
    )
```

```python
import functools

import jax
import jax.numpy as jnp
from jax import lax
from jax.experimental import pallas as pl
from jax.experimental.pallas import tpu as pltpu
from jax.sharding import PartitionSpec as P

GROUP = 16
LANES = 128
MESH = pl.DeviceIdType.MESH


def span(index, size):
    return pl.ds(pl.multiple_of(index * size, size), size)


def greet(peers):
    barrier = pltpu.get_barrier_semaphore()
    for axis, peer, there in peers:

        @pl.when(there)
        def _(axis=axis, peer=peer):
            pl.semaphore_signal(barrier, inc=1, device_id={axis: peer}, device_id_type=MESH)

    return sum(jnp.where(there, 1, 0) for _, _, there in peers)


def normalize_rows(hidden_ref, gain_ref, normed):
    rows, width = hidden_ref.shape
    few, part = min(16, rows), 1024

    def step(index, carry):
        where = span(index, few)

        def values(start):
            return hidden_ref[where, pl.ds(start, part)].astype(jnp.float32)

        squares = jnp.zeros((few, part), jnp.float32)
        for start in range(0, width, part):
            squares = squares + values(start) * values(start)
        scaled = lax.rsqrt(jnp.sum(squares, axis=-1, keepdims=True) / width + 1e-06)
        for start in range(0, width, part):
            inner = pl.ds(start, part)
            normed[where, inner] = (values(start) * scaled * gain_ref[:, inner]).astype(
                jnp.bfloat16
            )
        return carry

    lax.fori_loop(0, rows // few, step, 0)


def first_rows(taps_ref, decay_ref):
    groups, taps = taps_ref.shape
    lags = lax.broadcasted_iota(jnp.int32, (groups, taps), 1).astype(jnp.float32)
    across = lax.broadcasted_iota(jnp.int32, (groups, groups), 1)
    down = lax.broadcasted_iota(jnp.int32, (groups, groups), 0)
    decay = jnp.sum(jnp.where(across == down, decay_ref[...], 0.0), axis=1, keepdims=True)
    taps_full = (taps_ref[...] * jnp.exp(-decay * lags)).astype(jnp.bfloat16)
    lag = lax.broadcasted_iota(jnp.int32, (taps, 2 * taps), 0)
    column = lax.broadcasted_iota(jnp.int32, (taps, 2 * taps), 1)
    turned = jnp.where(lag + column == taps, 1.0, 0.0).astype(jnp.bfloat16)
    return jnp.dot(taps_full, turned, preferred_element_type=jnp.float32)


class Line:
    def __init__(self, count, pieces, view, send_sem, recv_sem):
        self.count, self.pieces, self.view = count, pieces, view
        self.send_sem, self.recv_sem = send_sem, recv_sem
        self.place = lax.axis_index("tensor")

    def inside(self, position):
        return (position >= 0) & (position < self.count)

    def hop(self, origin, piece, up, source=None):
        ref = self.view(origin, piece)
        return pltpu.make_async_remote_copy(
            src_ref=ref if source is None else source,
            dst_ref=ref,
            send_sem=self.send_sem.at[up, origin, piece],
            recv_sem=self.recv_sem.at[origin, piece],
            device_id={"tensor": jnp.clip(self.place + 2 * up - 1, 0, self.count - 1)},
            device_id_type=MESH,
        )

    def send(self, origin, piece, up, source=None):
        @pl.when(self.inside(self.place + 2 * up - 1))
        def _():
            self.hop(origin, piece, up, source).start()

    def pass_on(self, distance, piece, up):
        origin = self.place - distance * (2 * up - 1)

        @pl.when(self.inside(origin))
        def _():
            source = jnp.clip(origin, 0, self.count - 1)
            self.hop(source, piece, up).wait_recv()
            self.send(source, piece, up)

    def sent(self):
        def step(index, carry):
            origin, piece = index // self.pieces, lax.rem(index, self.pieces)

            @pl.when((origin <= self.place) & (self.place + 1 < self.count))
            def _():
                self.hop(origin, piece, 1).wait_send()

            @pl.when((origin >= self.place) & (self.place > 0))
            def _():
                self.hop(origin, piece, 0).wait_send()

            return carry

        lax.fori_loop(0, self.count * self.pieces, step, 0)


def mixer_kernel(
    shards,
    parts,
    hidden_ref,
    gain_ref,
    planes_ref,
    taps_ref,
    decay_ref,
    skip_ref,
    tail_ref,
    weight_ref,
    out_ref,
    normed,
    first,
    planes,
    slots,
    partial,
    arrived,
    filtered,
    product,
    before,
    bands,
    weight,
    gated,
    total,
    load_sem,
    own_sem,
    swap_send,
    swap_recv,
    line_send,
    line_recv,
    sum_send,
    sum_recv,
    tail_send,
    tail_recv,
    gated_send,
    gated_recv,
):
    rows = hidden_ref.shape[0]
    _, depth, channels = planes.shape
    groups, taps, _ = bands.shape
    chunks, all_rows, chunk = gated.shape[1:]
    columns = out_ref.shape[1]
    tile = min(256, channels)
    me, place = lax.axis_index("ctx"), lax.axis_index("tensor")
    others = [lax.rem(me + 1 + k, parts) for k in range(parts - 1)]

    loads = [
        pltpu.make_async_copy(planes_ref.at[g], planes.at[g], load_sem.at[g]) for g in (1, 2, 0)
    ]
    for load in loads:
        load.start()
    last_load = pltpu.make_async_copy(weight_ref, weight, load_sem.at[3])
    last_load.start()
    neighbours = [
        ("tensor", jnp.maximum(place - 1, 0), place > 0),
        ("tensor", jnp.minimum(place + 1, shards - 1), place < shards - 1),
    ]
    greeted = greet([("ctx", other, me >= 0) for other in others] + neighbours)
    normalize_rows(hidden_ref, gain_ref, normed)
    own = pltpu.make_async_copy(
        normed.at[:, span(me, depth)], slots.at[place, span(me, rows)], own_sem
    )
    own.start()
    pl.semaphore_wait(pltpu.get_barrier_semaphore(), greeted)

    swaps = [
        pltpu.make_async_remote_copy(
            src_ref=normed.at[:, span(other, depth)],
            dst_ref=slots.at[place, span(me, rows)],
            send_sem=swap_send.at[k],
            recv_sem=swap_recv.at[parts - 2 - k],
            device_id={"ctx": other},
            device_id_type=MESH,
        )
        for k, other in enumerate(others)
    ]
    for swap in swaps:
        swap.start()
    line = Line(
        shards, parts, lambda origin, c: slots.at[origin, span(c, rows)], line_send, line_recv
    )
    own.wait()
    line.send(place, me, 0)
    line.send(place, me, 1)

    first[...] = first_rows(taps_ref, decay_ref)

    @pl.when(me == 0)
    def _():
        padding = jnp.zeros((taps - tail_ref.shape[0], channels), jnp.float32)
        before[...] = jnp.concatenate(
            [padding, tail_ref[...].astype(jnp.float32)], axis=0
        ).astype(jnp.bfloat16)

    for k in range(parts - 1):
        swaps[parts - 2 - k].wait_recv()
        line.send(place, others[k], 0)
        line.send(place, others[k], 1)

    def write_band(group, carry):
        row = jnp.broadcast_to(first[pl.ds(group, 1), :], (taps, 2 * taps))
        bands[group] = pltpu.roll(row, 0, 1, stride=1, stride_axis=0).astype(jnp.bfloat16)
        return carry

    lax.fori_loop(0, groups, write_band, 0)
    for load in loads:
        load.wait()

    tiles = channels // tile

    def project(origin, k):
        def step(index, carry):
            g, column = lax.rem(index // tiles + 1, 3), lax.rem(index, tiles)
            where = span(column, tile)
            partial[g, origin, :, where] = jnp.dot(
                slots[origin], planes[g, :, where], preferred_element_type=jnp.float32
            ).astype(jnp.bfloat16)

            @pl.when(column == tiles - 1)
            def _():
                for k, other in enumerate(others):
                    pltpu.make_async_remote_copy(
                        src_ref=partial.at[g, origin, span(other, rows)],
                        dst_ref=arrived.at[g, parts - 2 - k, span(origin, rows)],
                        send_sem=sum_send,
                        recv_sem=sum_recv.at[g],
                        device_id={"ctx": other},
                        device_id_type=MESH,
                    ).start()

            return carry

        steps = 3 * tiles
        lax.fori_loop(k * steps // parts, (k + 1) * steps // parts, step, 0)

    def project_from(distance, k):
        below, above = place - distance, place + distance

        @pl.when(line.inside(below))
        def _():
            project(jnp.maximum(below, 0), k)

        @pl.when(line.inside(above) & (distance > 0))
        def _():
            project(jnp.minimum(above, shards - 1), k)

    def project_piece(origin, piece):
        mine = span(piece, rows)

        def plane(step, carry):
            g = lax.rem(step + 1, 3)

            def columns(column, inner):
                where = span(column, tile)
                partial[g, origin, mine, where] = jnp.dot(
                    slots[origin, mine], planes[g, :, where], preferred_element_type=jnp.float32
                ).astype(jnp.bfloat16)
                return inner

            lax.fori_loop(0, tiles, columns, 0)

            @pl.when(piece != me)
            def _():
                slot = jnp.clip(lax.rem(me - piece - 1 + parts, parts), 0, parts - 2)
                pltpu.make_async_remote_copy(
                    src_ref=partial.at[g, origin, mine],
                    dst_ref=arrived.at[g, slot, span(origin, rows)],
                    send_sem=sum_send,
                    recv_sem=sum_recv.at[g],
                    device_id={"ctx": piece},
                    device_id_type=MESH,
                ).start()

            return carry

        lax.fori_loop(0, 3, plane, 0)

    def stage(index, carry):
        distance, k = index // parts, lax.rem(index, parts)
        project_from(distance, k)
        piece = lax.rem(me + k, parts)
        line.pass_on(distance + 1, piece, 1)
        line.pass_on(distance + 1, piece, 0)

        @pl.when((distance == shards - 2) & ((place == 0) | (place == shards - 1)))
        def _():
            project_piece(shards - 1 - place, piece)

        return carry

    lax.fori_loop(0, (shards - 1) * parts, stage, 0)

    def summed(g, origin, where=slice(None)):
        value = partial[g, origin, span(me, rows), where].astype(jnp.float32)
        for k in range(parts - 1):
            value = value + arrived[g, k, span(origin, rows), where].astype(jnp.float32)
        return value

    for g in (1, 2):
        pltpu.make_async_copy(arrived.at[g], arrived.at[g], sum_recv.at[g]).wait()

    def write_product(step, carry):
        origin = shards - 1 - step
        product[span(origin, rows), :] = (summed(1, origin) * summed(2, origin)).astype(
            jnp.bfloat16
        )
        return carry

    tail_steps = -(-taps // rows)
    lax.fori_loop(0, tail_steps, write_product, 0)
    tail = pltpu.make_async_remote_copy(
        src_ref=product.at[pl.ds(all_rows - taps, taps)],
        dst_ref=before,
        send_sem=tail_send,
        recv_sem=tail_recv,
        device_id={"ctx": jnp.minimum(me + 1, parts - 1)},
        device_id_type=MESH,
    )

    @pl.when(me + 1 < parts)
    def _():
        tail.start()

    lax.fori_loop(tail_steps, shards, write_product, 0)
    @pl.when(me > 0)
    def _():
        tail.wait_recv()

    per, windows_count = LANES // GROUP, all_rows // taps

    def filter_lanes(block, carry):
        where = span(block, LANES)
        extended = jnp.concatenate([before[:, where], product[:, where]], axis=0)
        windows = jnp.concatenate(
            [extended[b * taps : (b + 2) * taps] for b in range(windows_count)], axis=1
        )
        lane = lax.broadcasted_iota(jnp.int32, windows.shape, 1)
        owner = lax.rem(lane, LANES) // GROUP
        sums = jnp.zeros((taps, windows_count * LANES), jnp.float32)
        for group in range(per):
            mine = jnp.where(owner == group, windows, jnp.zeros_like(windows))
            sums = sums + jnp.dot(
                bands[block * per + group], mine, preferred_element_type=jnp.float32
            )
        for b in range(windows_count):
            inner = pl.ds(b * taps, taps)
            direct = skip_ref[:, where] * product[inner, where].astype(jnp.float32)
            filtered[inner, where] = sums[:, b * LANES : (b + 1) * LANES] + direct
        return carry

    lax.fori_loop(0, channels // LANES, filter_lanes, 0)
    pltpu.make_async_copy(arrived.at[0], arrived.at[0], sum_recv.at[0]).wait()

    gated_line = Line(
        shards, chunks, lambda origin, c: gated.at[origin, c], gated_send, gated_recv
    )

    def gate_chunk(c, carry):
        where = span(c, chunk)

        def gate(origin, inner):
            mine = span(origin, rows)
            gated[place, c, mine, :] = (
                summed(0, origin, where) * filtered[mine, where]
            ).astype(jnp.bfloat16)
            return inner

        lax.fori_loop(0, shards, gate, 0)
        gated_line.send(place, c, 0)
        gated_line.send(place, c, 1)
        return carry

    lax.fori_loop(0, chunks, gate_chunk, 0)
    last_load.wait()
    wide = min(512, columns)

    def multiply(origin, c, fresh):
        deep = span(origin * chunks + c, chunk)

        def column(index, carry):
            where = span(index, wide)
            value = jnp.dot(
                gated[origin, c], weight[deep, where], preferred_element_type=jnp.float32
            )
            total[:, where] = value if fresh else total[:, where] + value
            return carry

        lax.fori_loop(0, columns // wide, column, 0)

    multiply(place, 0, True)

    def multiply_own(c, carry):
        multiply(place, c, False)
        return carry

    lax.fori_loop(1, chunks, multiply_own, 0)
    first_up = jnp.where(2 * place >= shards, 1, 0)

    def collect(index, carry):
        distance, side = index // (2 * chunks) + 1, lax.rem(index // chunks, 2)
        c = lax.rem(index, chunks)
        up = lax.rem(first_up + side, 2)
        gated_line.pass_on(distance, c, up)
        origin = place - distance * (2 * up - 1)

        @pl.when(gated_line.inside(origin))
        def _():
            multiply(jnp.clip(origin, 0, shards - 1), c, False)

        return carry

    lax.fori_loop(0, 2 * chunks * (shards - 1), collect, 0)
    out_ref[...] = total[...].astype(jnp.bfloat16)

    for swap in swaps:
        swap.wait_send()

    @pl.when(me + 1 < parts)
    def _():
        tail.wait_send()

    line.sent()
    gated_line.sent()
    pltpu.make_async_copy(arrived, arrived, sum_send).wait()


def paired_kernel(
    shards,
    hidden_in,
    gain_in,
    planes_ref,
    taps_in,
    decay_in,
    skip_in,
    tail_in,
    weight_ref,
    out_ref,
    hidden_ref,
    gain_ref,
    taps_ref,
    decay_ref,
    skip_ref,
    tail_ref,
    normed,
    first,
    planes,
    slots,
    mine,
    outgoing,
    arrived,
    extended,
    filtered,
    bands,
    weight,
    gated,
    handed,
    total,
    input_sem,
    load_sem,
    own_sem,
    planes_send,
    planes_recv,
    swap_send,
    line_send,
    line_recv,
    pair_send,
    pair_recv,
    sum_send,
    sum_recv,
    tail_send,
    tail_recv,
    hand_send,
    hand_recv,
    gated_send,
    gated_recv,
):
    rows = hidden_ref.shape[0]
    parts = slots.shape[1] // rows
    _, both_depths, half = planes.shape
    depth = both_depths // 2
    _, taps, _ = bands.shape
    chunks, all_rows, chunk = gated.shape[1:]
    columns = out_ref.shape[1]
    tile = min(256, half)
    tiles = half // tile
    me, place = lax.axis_index("ctx"), lax.axis_index("tensor")
    pair, core = me // 2, lax.rem(me, 2)
    across = 1 - pair
    sibling, peer = 2 * pair + 1 - core, 2 * across + core

    others = [lax.rem(me + 1 + k, parts) for k in range(parts - 1)]
    neighbours = [
        ("tensor", jnp.maximum(place - 1, 0), place > 0),
        ("tensor", jnp.minimum(place + 1, shards - 1), place < shards - 1),
    ]
    greeted = greet([("ctx", other, me >= 0) for other in others] + neighbours)
    inputs = [
        pltpu.make_async_copy(source, target, input_sem.at[k])
        for k, (source, target) in enumerate(
            [
                (hidden_in, hidden_ref),
                (gain_in, gain_ref),
                (taps_in, taps_ref),
                (decay_in, decay_ref),
                (skip_in, skip_ref),
                (tail_in, tail_ref),
            ]
        )
    ]
    for load in inputs:
        load.start()
    loads = [
        pltpu.make_async_copy(
            planes_ref.at[g, :, span(core, half)], planes.at[g, span(core, depth)], load_sem.at[g]
        )
        for g in (1, 2, 0)
    ]
    for load in loads:
        load.start()
    last_load = pltpu.make_async_copy(weight_ref, weight, load_sem.at[3])
    for load in inputs[:2]:
        load.wait()
    normalize_rows(hidden_ref, gain_ref, normed)
    mine_in = normed.at[:, span(pair, both_depths)]
    own = pltpu.make_async_copy(mine_in, slots.at[place, span(me, rows)], own_sem)
    own.start()
    pl.semaphore_wait(pltpu.get_barrier_semaphore(), greeted)

    def remote(source, target, send, recv, **device):
        return pltpu.make_async_remote_copy(
            src_ref=source,
            dst_ref=target,
            send_sem=send,
            recv_sem=recv,
            device_id=device,
            device_id_type=MESH,
        )

    line = Line(
        shards,
        parts,
        lambda origin, c: slots.at[origin, span(c, rows), span(core, depth)],
        line_send,
        line_recv,
    )
    line.send(place, me, 0, normed.at[:, span(me, depth)])
    line.send(place, me, 1, normed.at[:, span(me, depth)])
    to_sibling = remote(
        mine_in, slots.at[place, span(me, rows)], pair_send, pair_recv.at[place, me], ctx=sibling
    )
    to_sibling.start()
    swaps = [
        remote(
            normed.at[:, span(2 * across + k, depth)],
            slots.at[place, span(me, rows), pl.ds(k * depth, depth)],
            swap_send.at[k],
            line_recv.at[place, me],
            ctx=2 * across + k,
        )
        for k in range(2)
    ]
    swaps[0].start()
    shares = [
        remote(
            planes_ref.at[g, :, span(1 - core, half)],
            planes.at[g, span(core, depth)],
            planes_send,
            planes_recv.at[g],
            ctx=sibling,
        )
        for g in (1, 2, 0)
    ]
    for share in shares:
        share.start()

    def share_piece(origin, c):
        ref = slots.at[origin, span(c, rows), span(core, depth)]
        return remote(ref, ref, pair_send, pair_recv.at[origin, c], ctx=sibling)

    def from_sibling(origin, c):
        ref = slots.at[origin, span(c, rows), span(1 - core, depth)]
        return remote(ref, ref, pair_send, pair_recv.at[origin, c], ctx=sibling)

    for load in inputs[2:]:
        load.wait()
    first[...] = first_rows(taps_ref, decay_ref)

    @pl.when(pair == 0)
    def _():
        padding = jnp.zeros((taps - tail_ref.shape[0], half), jnp.float32)
        extended[pl.ds(0, taps), :] = jnp.concatenate(
            [padding, tail_ref[:, span(core, half)].astype(jnp.float32)], axis=0
        ).astype(jnp.bfloat16)

    remote(
        mine_in,
        slots.at[place, span(sibling, rows)],
        pair_send,
        pair_recv.at[place, sibling],
        ctx=sibling,
    ).wait_recv()
    line.send(place, sibling, 0)
    line.send(place, sibling, 1)

    def write_band(group, carry):
        row = jnp.broadcast_to(first[pl.ds(core * (half // GROUP) + group, 1), :], (taps, 2 * taps))
        bands[group] = pltpu.roll(row, 0, 1, stride=1, stride_axis=0).astype(jnp.bfloat16)
        return carry

    lax.fori_loop(0, half // GROUP, write_band, 0)
    swaps[0].wait_send()
    swaps[1].start()
    for k in range(2):
        c = 2 * across + k
        line.hop(place, c, 1).wait_recv()
        line.send(place, c, 0)
        line.send(place, c, 1)
        share_piece(place, c).start()
    own.wait()
    for load in loads:
        load.wait()
    for share in shares:
        share.wait_recv()
    last_load.start()

    def sum_piece(g, origin):
        where = span(origin, rows)
        return remote(
            outgoing.at[g, :, where],
            arrived.at[g, :, where],
            sum_send,
            sum_recv.at[g, origin],
            ctx=peer,
        )

    def group_of(far):
        return jnp.where(far == 1, across, pair)

    def project(origin, far):
        tokens = span(group_of(far), 2 * rows)

        def step(index, carry):
            g, column = lax.rem(index // tiles + 1, 3), lax.rem(index, tiles)
            where = span(column, tile)
            value = jnp.dot(
                slots[origin, tokens], planes[g, :, where], preferred_element_type=jnp.float32
            )

            def keep(target):
                for k in range(2):
                    target[g, k, span(origin, rows), where] = value[
                        k * rows : (k + 1) * rows
                    ].astype(target.dtype)

            @pl.when(far == 0)
            def _():
                keep(mine)

            @pl.when(far == 1)
            def _():
                keep(outgoing)

            @pl.when((far == 1) & (column == tiles - 1))
            def _():
                sum_piece(g, origin).start()

            return carry

        lax.fori_loop(0, 3 * tiles, step, 0)

    def combine(origin):
        where = span(origin, rows)
        for g in (1, 2, 0):
            sum_piece(g, origin).wait_recv()
        for k in range(2):
            q, key, value = [
                mine[g, k, where] + arrived[g, k, where].astype(jnp.float32) for g in range(3)
            ]
            mine[0, k, where] = q
            start = pl.multiple_of(taps + k * all_rows + origin * rows, rows)
            extended[pl.ds(start, rows), :] = (key * value).astype(jnp.bfloat16)

    def beside(distance, work):
        for origin in (place - distance, place + distance):

            @pl.when(line.inside(origin))
            def _(origin=origin):
                work(jnp.clip(origin, 0, shards - 1))

    def project_own(far, carry):
        @pl.when(far == 1)
        def _():
            for k in range(2):
                from_sibling(place, 2 * across + k).wait_recv()

        project(place, far)
        return carry

    lax.fori_loop(0, 2, project_own, 0)

    def from_side(distance, up):
        origin = place - distance * (2 * up - 1)
        return line.inside(origin), jnp.clip(origin, 0, shards - 1), origin == (1 - up) * (shards - 1)

    def far_at(distance, turn, last):
        return jnp.where(last & (distance > 1), 1 - turn, turn)

    def flow(distance, turn, up):
        there, origin, last = from_side(distance, up)
        held = last & (distance == 1)

        @pl.when(there)
        def _():
            group = group_of(far_at(distance, turn, last))
            for k in range(2):
                line.hop(origin, 2 * group + k, up).wait_recv()

                @pl.when(~held | (turn == 1))
                def _(k=k):
                    line.send(origin, 2 * group + k, up)

                share_piece(origin, 2 * group + k).start()

            @pl.when(held & (turn == 1))
            def _():
                for k in range(2):
                    line.send(origin, 2 * pair + k, up)

    def project_side(distance, turn, up):
        there, origin, last = from_side(distance, up)

        @pl.when(there)
        def _():
            far = far_at(distance, turn, last)
            for k in range(2):
                from_sibling(origin, 2 * group_of(far) + k).wait_recv()
            project(origin, far)

    def stage(distance, carry):
        def half_stage(turn, inner):
            flow(distance, turn, 1)
            flow(distance, turn, 0)

            def side(up, nothing):
                project_side(distance, turn, up)
                return nothing

            lax.fori_loop(0, 2, side, 0)
            return inner

        lax.fori_loop(0, 2, half_stage, 0)

        @pl.when(distance == 1)
        def _():
            combine(place)

        @pl.when(distance > 1)
        def _():
            beside(distance - 1, combine)

        return carry

    lax.fori_loop(1, shards, stage, 0)
    beside(shards - 1, combine)
    before = extended.at[pl.ds(0, taps)]
    tail = remote(
        extended.at[pl.ds(2 * all_rows, taps)], before, tail_send, tail_recv, ctx=peer
    )

    @pl.when(pair == 0)
    def _():
        tail.start()

    per, windows_count = LANES // GROUP, all_rows // taps

    def filter_lanes(k, block):
        where = span(block, LANES)
        values = extended[pl.ds(k * all_rows, taps + all_rows), where]
        windows = jnp.concatenate(
            [values[b * taps : (b + 2) * taps] for b in range(windows_count)], axis=1
        )
        lane = lax.broadcasted_iota(jnp.int32, windows.shape, 1)
        owner = lax.rem(lane, LANES) // GROUP
        sums = jnp.zeros((taps, windows_count * LANES), jnp.float32)
        for group in range(per):
            some = jnp.where(owner == group, windows, jnp.zeros_like(windows))
            sums = sums + jnp.dot(
                bands[block * per + group], some, preferred_element_type=jnp.float32
            )
        skip = skip_ref[:, pl.ds(pl.multiple_of(core * half + block * LANES, LANES), LANES)]
        for b in range(windows_count):
            direct = skip * values[(b + 1) * taps : (b + 2) * taps].astype(jnp.float32)
            filtered[pl.ds(b * taps, taps), where] = sums[:, b * LANES : (b + 1) * LANES] + direct

    gated_line = Line(
        shards, chunks, lambda origin, c: gated.at[origin, c], gated_send, gated_recv
    )
    mine_chunks = half // chunk

    def hand(i, owner):
        c = owner * mine_chunks + i
        return remote(handed.at[i], gated.at[place, c], hand_send, hand_recv.at[i], ctx=sibling)

    def gate_half(step, carry):
        k = 1 - step

        @pl.when((k == 0) & (pair == 1))
        def _():
            tail.wait_recv()

        def gate_chunk(i, inner):
            def lanes(block, nothing):
                filter_lanes(k, block)
                return nothing

            per_chunk = chunk // LANES
            lax.fori_loop(i * per_chunk, (i + 1) * per_chunk, lanes, 0)
            where, c = span(i, chunk), core * mine_chunks + i
            value = (mine[0, k, :, where] * filtered[:, where]).astype(jnp.bfloat16)

            @pl.when(k == core)
            def _():
                gated[place, c] = value
                gated_line.send(place, c, 0)
                gated_line.send(place, c, 1)

            @pl.when(k != core)
            def _():
                handed[i] = value
                hand(i, core).start()

            return inner

        lax.fori_loop(0, mine_chunks, gate_chunk, 0)
        return carry

    lax.fori_loop(0, 2, gate_half, 0)

    def take(i, carry):
        hand(i, 1 - core).wait_recv()
        c = (1 - core) * mine_chunks + i
        gated_line.send(place, c, 0)
        gated_line.send(place, c, 1)
        return carry

    lax.fori_loop(0, mine_chunks, take, 0)
    last_load.wait()
    wide = min(512, columns)

    def multiply(origin, c, fresh=False, last=False):
        deep = span(origin * chunks + c, chunk)
        for start in range(0, columns, wide):
            where = pl.ds(start, wide)
            value = jnp.dot(
                gated[origin, c], weight[deep, where], preferred_element_type=jnp.float32
            )
            if not fresh:
                value = total[:, where] + value
            if last:
                out_ref[:, where] = value.astype(jnp.bfloat16)
            else:
                total[:, where] = value

    multiply(place, 0, True)

    def multiply_own(c, carry):
        multiply(place, c)
        return carry

    lax.fori_loop(1, chunks, multiply_own, 0)
    first_up = jnp.where(2 * place >= shards, 1, 0)

    def collect(index, carry):
        distance, side = index // (2 * chunks) + 1, lax.rem(index // chunks, 2)
        step = lax.rem(index, chunks)
        c = lax.rem(step + core * mine_chunks, chunks)
        up = lax.rem(first_up + side, 2)
        gated_line.pass_on(distance, c, up)
        origin = place - distance * (2 * up - 1)

        final = (distance == shards - 1) & (step == chunks - 1)

        @pl.when(gated_line.inside(origin) & ~final)
        def _():
            multiply(jnp.clip(origin, 0, shards - 1), c)

        @pl.when(gated_line.inside(origin) & final)
        def _():
            multiply(jnp.clip(origin, 0, shards - 1), c, last=True)

        return carry

    lax.fori_loop(0, 2 * chunks * (shards - 1), collect, 0)

    @pl.when((place > 0) & (place < shards - 1))
    def _():
        out_ref[...] = total[...].astype(jnp.bfloat16)

    swaps[1].wait_send()

    @pl.when(pair == 0)
    def _():
        tail.wait_send()

    line.sent()
    gated_line.sent()
    slices = slots.at[:, :, pl.ds(0, depth)]
    pltpu.make_async_copy(slices, slices, pair_send).wait()
    pltpu.make_async_copy(handed, handed, hand_send).wait()
    pltpu.make_async_copy(outgoing, outgoing, sum_send).wait()
    sent_planes = planes.at[:, pl.ds(0, depth)]
    pltpu.make_async_copy(sent_planes, sent_planes, planes_send).wait()


def on_paired_device(
    hidden_in, norm_gain, weight_in, filter_taps, filter_decay, skip_gain, tail_cache, output_weight
):
    shards, parts = lax.axis_size("tensor"), lax.axis_size("ctx")
    rows = hidden_in.shape[0]
    depth, _, channels = weight_in.shape
    groups, taps = filter_taps.shape
    columns = output_weight.shape[1]
    all_rows = shards * rows
    half = channels // 2
    chunk = min(256, half)
    chunks = channels // chunk
    anywhere = pl.BlockSpec(memory_space=pl.ANY)
    dma = pltpu.SemaphoreType.DMA
    bf16, f32 = jnp.bfloat16, jnp.float32
    return pl.pallas_call(
        functools.partial(paired_kernel, shards),
        out_shape=pltpu.VMEM((all_rows, columns), bf16),
        in_specs=[anywhere] * 8,
        out_specs=pl.BlockSpec(memory_space=pltpu.VMEM),
        scratch_shapes=[
            pltpu.VMEM(hidden_in.shape, bf16),
            pltpu.VMEM((1, norm_gain.shape[0]), f32),
            pltpu.VMEM(filter_taps.shape, f32),
            pltpu.VMEM((1, groups), f32),
            pltpu.VMEM((1, channels), f32),
            pltpu.VMEM(tail_cache.shape, bf16),
            pltpu.VMEM((rows, hidden_in.shape[1]), bf16),
            pltpu.VMEM((groups, 2 * taps), f32),
            pltpu.VMEM((3, 2 * depth, half), bf16),
            pltpu.VMEM((shards, parts * rows, 2 * depth), bf16),
            pltpu.VMEM((3, 2, all_rows, half), f32),
            pltpu.VMEM((3, 2, all_rows, half), bf16),
            pltpu.VMEM((3, 2, all_rows, half), bf16),
            pltpu.VMEM((taps + 2 * all_rows, half), bf16),
            pltpu.VMEM((all_rows, half), f32),
            pltpu.VMEM((groups // 2, taps, 2 * taps), bf16),
            pltpu.VMEM(output_weight.shape, bf16),
            pltpu.VMEM((shards, chunks, all_rows, chunk), bf16),
            pltpu.VMEM((chunks // 2, all_rows, chunk), bf16),
            pltpu.VMEM((all_rows, columns), f32),
            dma((6,)),
            dma((4,)),
            dma,
            dma,
            dma((3,)),
            dma((2,)),
            dma((2, shards, parts)),
            dma((shards, parts)),
            dma,
            dma((shards, parts)),
            dma,
            dma((3, shards)),
            dma,
            dma,
            dma,
            dma((chunks // 2,)),
            dma((2, shards, chunks)),
            dma((shards, chunks)),
        ],
        compiler_params=pltpu.CompilerParams(
            collective_id=0, has_side_effects=True, vmem_limit_bytes=54 << 20
        ),
    )(
        hidden_in,
        norm_gain.reshape(1, norm_gain.shape[0]),
        weight_in.transpose(1, 0, 2),
        filter_taps,
        filter_decay.reshape(1, groups),
        skip_gain.reshape(1, channels),
        tail_cache,
        output_weight,
    )


def on_device(
    hidden_in, norm_gain, weight_in, filter_taps, filter_decay, skip_gain, tail_cache, output_weight
):
    shards, parts = lax.axis_size("tensor"), lax.axis_size("ctx")
    rows = hidden_in.shape[0]
    depth, _, channels = weight_in.shape
    groups, taps = filter_taps.shape
    columns = output_weight.shape[1]
    all_rows = shards * rows
    chunk = min(256, channels)
    chunks = channels // chunk
    vmem, anywhere = pl.BlockSpec(memory_space=pltpu.VMEM), pl.BlockSpec(memory_space=pl.ANY)
    dma = pltpu.SemaphoreType.DMA
    bf16, f32 = jnp.bfloat16, jnp.float32
    return pl.pallas_call(
        functools.partial(mixer_kernel, shards, parts),
        out_shape=jax.ShapeDtypeStruct((all_rows, columns), bf16),
        in_specs=[vmem, vmem, anywhere, vmem, vmem, vmem, vmem, anywhere],
        out_specs=vmem,
        scratch_shapes=[
            pltpu.VMEM((rows, hidden_in.shape[1]), bf16),
            pltpu.VMEM((groups, 2 * taps), f32),
            pltpu.VMEM((3, depth, channels), bf16),
            pltpu.VMEM((shards, parts * rows, depth), bf16),
            pltpu.VMEM((3, shards, parts * rows, channels), bf16),
            pltpu.VMEM((3, parts - 1, all_rows, channels), bf16),
            pltpu.VMEM((all_rows, channels), f32),
            pltpu.VMEM((all_rows, channels), bf16),
            pltpu.VMEM((taps, channels), bf16),
            pltpu.VMEM((groups, taps, 2 * taps), bf16),
            pltpu.VMEM(output_weight.shape, bf16),
            pltpu.VMEM((shards, chunks, all_rows, chunk), bf16),
            pltpu.VMEM((all_rows, columns), f32),
            dma((4,)),
            dma,
            dma((parts - 1,)),
            dma((parts - 1,)),
            dma((2, shards, parts)),
            dma((shards, parts)),
            dma,
            dma((3,)),
            dma,
            dma,
            dma((2, shards, chunks)),
            dma((shards, chunks)),
        ],
        compiler_params=pltpu.CompilerParams(
            collective_id=0, has_side_effects=True, vmem_limit_bytes=56 << 20
        ),
    )(
        hidden_in,
        norm_gain.reshape(1, norm_gain.shape[0]),
        weight_in.transpose(1, 0, 2),
        filter_taps,
        filter_decay.reshape(1, groups),
        skip_gain.reshape(1, channels),
        tail_cache,
        output_weight,
    )


def solution(mesh):
    in_specs = (
        P(("prompt", "ctx", "tensor"), None),
        P(),
        P("ctx", None, "tensor"),
        P("tensor", None),
        P("tensor"),
        P("tensor"),
        P("prompt", "tensor"),
        P(None, "tensor"),
    )
    out_specs = P(("prompt", "ctx"), "tensor")
    paired = mesh.shape["ctx"] == 4 and mesh.shape["tensor"] > 1
    return jax.shard_map(
        on_paired_device if paired else on_device, mesh=mesh, in_specs=in_specs, out_specs=out_specs, check_vma=False
    )
```

```python
import functools

import jax
import jax.numpy as jnp
from jax import lax
from jax.experimental import pallas as pl
from jax.experimental.pallas import tpu as pltpu
from jax.sharding import PartitionSpec as P

GROUP = 16
LANES = 128
MESH = pl.DeviceIdType.MESH


def span(index, size):
    return pl.ds(pl.multiple_of(index * size, size), size)


def greet(peers):
    barrier = pltpu.get_barrier_semaphore()
    for axis, peer, there in peers:

        @pl.when(there)
        def _(axis=axis, peer=peer):
            pl.semaphore_signal(barrier, inc=1, device_id={axis: peer}, device_id_type=MESH)

    return sum(jnp.where(there, 1, 0) for _, _, there in peers)


def normalize_rows(hidden_ref, gain_ref, normed):
    rows, width = hidden_ref.shape
    few, part = min(16, rows), 1024

    def step(index, carry):
        where = span(index, few)

        def values(start):
            return hidden_ref[where, pl.ds(start, part)].astype(jnp.float32)

        squares = jnp.zeros((few, part), jnp.float32)
        for start in range(0, width, part):
            squares = squares + values(start) * values(start)
        scaled = lax.rsqrt(jnp.sum(squares, axis=-1, keepdims=True) / width + 1e-06)
        for start in range(0, width, part):
            inner = pl.ds(start, part)
            normed[where, inner] = (values(start) * scaled * gain_ref[:, inner]).astype(
                jnp.bfloat16
            )
        return carry

    lax.fori_loop(0, rows // few, step, 0)


def first_rows(taps_ref, decay_ref):
    groups, taps = taps_ref.shape
    lags = lax.broadcasted_iota(jnp.int32, (groups, taps), 1).astype(jnp.float32)
    across = lax.broadcasted_iota(jnp.int32, (groups, groups), 1)
    down = lax.broadcasted_iota(jnp.int32, (groups, groups), 0)
    decay = jnp.sum(jnp.where(across == down, decay_ref[...], 0.0), axis=1, keepdims=True)
    taps_full = (taps_ref[...] * jnp.exp(-decay * lags)).astype(jnp.bfloat16)
    lag = lax.broadcasted_iota(jnp.int32, (taps, 2 * taps), 0)
    column = lax.broadcasted_iota(jnp.int32, (taps, 2 * taps), 1)
    turned = jnp.where(lag + column == taps, 1.0, 0.0).astype(jnp.bfloat16)
    return jnp.dot(taps_full, turned, preferred_element_type=jnp.float32)


class Line:
    def __init__(self, count, pieces, view, send_sem, recv_sem):
        self.count, self.pieces, self.view = count, pieces, view
        self.send_sem, self.recv_sem = send_sem, recv_sem
        self.place = lax.axis_index("tensor")

    def inside(self, position):
        return (position >= 0) & (position < self.count)

    def hop(self, origin, piece, up, source=None):
        ref = self.view(origin, piece)
        return pltpu.make_async_remote_copy(
            src_ref=ref if source is None else source,
            dst_ref=ref,
            send_sem=self.send_sem.at[up, origin, piece],
            recv_sem=self.recv_sem.at[origin, piece],
            device_id={"tensor": jnp.clip(self.place + 2 * up - 1, 0, self.count - 1)},
            device_id_type=MESH,
        )

    def send(self, origin, piece, up, source=None):
        @pl.when(self.inside(self.place + 2 * up - 1))
        def _():
            self.hop(origin, piece, up, source).start()

    def pass_on(self, distance, piece, up):
        origin = self.place - distance * (2 * up - 1)

        @pl.when(self.inside(origin))
        def _():
            source = jnp.clip(origin, 0, self.count - 1)
            self.hop(source, piece, up).wait_recv()
            self.send(source, piece, up)

    def sent(self):
        def step(index, carry):
            origin, piece = index // self.pieces, lax.rem(index, self.pieces)

            @pl.when((origin <= self.place) & (self.place + 1 < self.count))
            def _():
                self.hop(origin, piece, 1).wait_send()

            @pl.when((origin >= self.place) & (self.place > 0))
            def _():
                self.hop(origin, piece, 0).wait_send()

            return carry

        lax.fori_loop(0, self.count * self.pieces, step, 0)


def mixer_kernel(
    shards,
    parts,
    hidden_ref,
    gain_ref,
    planes_ref,
    taps_ref,
    decay_ref,
    skip_ref,
    tail_ref,
    weight_ref,
    out_ref,
    normed,
    first,
    planes,
    slots,
    partial,
    arrived,
    filtered,
    product,
    before,
    bands,
    weight,
    gated,
    total,
    load_sem,
    own_sem,
    swap_send,
    swap_recv,
    line_send,
    line_recv,
    sum_send,
    sum_recv,
    tail_send,
    tail_recv,
    gated_send,
    gated_recv,
):
    rows = hidden_ref.shape[0]
    _, depth, channels = planes.shape
    groups, taps, _ = bands.shape
    chunks, all_rows, chunk = gated.shape[1:]
    columns = out_ref.shape[1]
    tile = min(256, channels)
    me, place = lax.axis_index("ctx"), lax.axis_index("tensor")
    others = [lax.rem(me + 1 + k, parts) for k in range(parts - 1)]

    loads = [
        pltpu.make_async_copy(planes_ref.at[g], planes.at[g], load_sem.at[g]) for g in (1, 2, 0)
    ]
    for load in loads:
        load.start()
    last_load = pltpu.make_async_copy(weight_ref, weight, load_sem.at[3])
    last_load.start()
    neighbours = [
        ("tensor", jnp.maximum(place - 1, 0), place > 0),
        ("tensor", jnp.minimum(place + 1, shards - 1), place < shards - 1),
    ]
    greeted = greet([("ctx", other, me >= 0) for other in others] + neighbours)
    normalize_rows(hidden_ref, gain_ref, normed)
    own = pltpu.make_async_copy(
        normed.at[:, span(me, depth)], slots.at[place, span(me, rows)], own_sem
    )
    own.start()
    pl.semaphore_wait(pltpu.get_barrier_semaphore(), greeted)

    swaps = [
        pltpu.make_async_remote_copy(
            src_ref=normed.at[:, span(other, depth)],
            dst_ref=slots.at[place, span(me, rows)],
            send_sem=swap_send.at[k],
            recv_sem=swap_recv.at[parts - 2 - k],
            device_id={"ctx": other},
            device_id_type=MESH,
        )
        for k, other in enumerate(others)
    ]
    for swap in swaps:
        swap.start()
    line = Line(
        shards, parts, lambda origin, c: slots.at[origin, span(c, rows)], line_send, line_recv
    )
    own.wait()
    line.send(place, me, 0)
    line.send(place, me, 1)

    first[...] = first_rows(taps_ref, decay_ref)

    @pl.when(me == 0)
    def _():
        padding = jnp.zeros((taps - tail_ref.shape[0], channels), jnp.float32)
        before[...] = jnp.concatenate(
            [padding, tail_ref[...].astype(jnp.float32)], axis=0
        ).astype(jnp.bfloat16)

    for k in range(parts - 1):
        swaps[parts - 2 - k].wait_recv()
        line.send(place, others[k], 0)
        line.send(place, others[k], 1)

    def write_band(group, carry):
        row = jnp.broadcast_to(first[pl.ds(group, 1), :], (taps, 2 * taps))
        bands[group] = pltpu.roll(row, 0, 1, stride=1, stride_axis=0).astype(jnp.bfloat16)
        return carry

    lax.fori_loop(0, groups, write_band, 0)
    for load in loads:
        load.wait()

    tiles = channels // tile

    def project(origin, k):
        def step(index, carry):
            g, column = lax.rem(index // tiles + 1, 3), lax.rem(index, tiles)
            where = span(column, tile)
            partial[g, origin, :, where] = jnp.dot(
                slots[origin], planes[g, :, where], preferred_element_type=jnp.float32
            ).astype(jnp.bfloat16)

            @pl.when(column == tiles - 1)
            def _():
                for k, other in enumerate(others):
                    pltpu.make_async_remote_copy(
                        src_ref=partial.at[g, origin, span(other, rows)],
                        dst_ref=arrived.at[g, parts - 2 - k, span(origin, rows)],
                        send_sem=sum_send,
                        recv_sem=sum_recv.at[g],
                        device_id={"ctx": other},
                        device_id_type=MESH,
                    ).start()

            return carry

        steps = 3 * tiles
        lax.fori_loop(k * steps // parts, (k + 1) * steps // parts, step, 0)

    def project_from(distance, k):
        below, above = place - distance, place + distance

        @pl.when(line.inside(below))
        def _():
            project(jnp.maximum(below, 0), k)

        @pl.when(line.inside(above) & (distance > 0))
        def _():
            project(jnp.minimum(above, shards - 1), k)

    def project_piece(origin, piece):
        mine = span(piece, rows)

        def plane(step, carry):
            g = lax.rem(step + 1, 3)

            def columns(column, inner):
                where = span(column, tile)
                partial[g, origin, mine, where] = jnp.dot(
                    slots[origin, mine], planes[g, :, where], preferred_element_type=jnp.float32
                ).astype(jnp.bfloat16)
                return inner

            lax.fori_loop(0, tiles, columns, 0)

            @pl.when(piece != me)
            def _():
                slot = jnp.clip(lax.rem(me - piece - 1 + parts, parts), 0, parts - 2)
                pltpu.make_async_remote_copy(
                    src_ref=partial.at[g, origin, mine],
                    dst_ref=arrived.at[g, slot, span(origin, rows)],
                    send_sem=sum_send,
                    recv_sem=sum_recv.at[g],
                    device_id={"ctx": piece},
                    device_id_type=MESH,
                ).start()

            return carry

        lax.fori_loop(0, 3, plane, 0)

    def stage(index, carry):
        distance, k = index // parts, lax.rem(index, parts)
        project_from(distance, k)
        piece = lax.rem(me + k, parts)
        line.pass_on(distance + 1, piece, 1)
        line.pass_on(distance + 1, piece, 0)

        @pl.when((distance == shards - 2) & ((place == 0) | (place == shards - 1)))
        def _():
            project_piece(shards - 1 - place, piece)

        return carry

    lax.fori_loop(0, (shards - 1) * parts, stage, 0)

    def summed(g, origin, where=slice(None)):
        value = partial[g, origin, span(me, rows), where].astype(jnp.float32)
        for k in range(parts - 1):
            value = value + arrived[g, k, span(origin, rows), where].astype(jnp.float32)
        return value

    for g in (1, 2):
        pltpu.make_async_copy(arrived.at[g], arrived.at[g], sum_recv.at[g]).wait()

    def write_product(step, carry):
        origin = shards - 1 - step
        product[span(origin, rows), :] = (summed(1, origin) * summed(2, origin)).astype(
            jnp.bfloat16
        )
        return carry

    tail_steps = -(-taps // rows)
    lax.fori_loop(0, tail_steps, write_product, 0)
    tail = pltpu.make_async_remote_copy(
        src_ref=product.at[pl.ds(all_rows - taps, taps)],
        dst_ref=before,
        send_sem=tail_send,
        recv_sem=tail_recv,
        device_id={"ctx": jnp.minimum(me + 1, parts - 1)},
        device_id_type=MESH,
    )

    @pl.when(me + 1 < parts)
    def _():
        tail.start()

    lax.fori_loop(tail_steps, shards, write_product, 0)
    @pl.when(me > 0)
    def _():
        tail.wait_recv()

    per, windows_count = LANES // GROUP, all_rows // taps

    def filter_lanes(block, carry):
        where = span(block, LANES)
        extended = jnp.concatenate([before[:, where], product[:, where]], axis=0)
        windows = jnp.concatenate(
            [extended[b * taps : (b + 2) * taps] for b in range(windows_count)], axis=1
        )
        lane = lax.broadcasted_iota(jnp.int32, windows.shape, 1)
        owner = lax.rem(lane, LANES) // GROUP
        sums = jnp.zeros((taps, windows_count * LANES), jnp.float32)
        for group in range(per):
            mine = jnp.where(owner == group, windows, jnp.zeros_like(windows))
            sums = sums + jnp.dot(
                bands[block * per + group], mine, preferred_element_type=jnp.float32
            )
        for b in range(windows_count):
            inner = pl.ds(b * taps, taps)
            direct = skip_ref[:, where] * product[inner, where].astype(jnp.float32)
            filtered[inner, where] = sums[:, b * LANES : (b + 1) * LANES] + direct
        return carry

    lax.fori_loop(0, channels // LANES, filter_lanes, 0)
    pltpu.make_async_copy(arrived.at[0], arrived.at[0], sum_recv.at[0]).wait()

    gated_line = Line(
        shards, chunks, lambda origin, c: gated.at[origin, c], gated_send, gated_recv
    )

    def gate_chunk(c, carry):
        where = span(c, chunk)

        def gate(origin, inner):
            mine = span(origin, rows)
            gated[place, c, mine, :] = (
                summed(0, origin, where) * filtered[mine, where]
            ).astype(jnp.bfloat16)
            return inner

        lax.fori_loop(0, shards, gate, 0)
        gated_line.send(place, c, 0)
        gated_line.send(place, c, 1)
        return carry

    lax.fori_loop(0, chunks, gate_chunk, 0)
    last_load.wait()
    wide = min(512, columns)

    def multiply(origin, c, fresh):
        deep = span(origin * chunks + c, chunk)

        def column(index, carry):
            where = span(index, wide)
            value = jnp.dot(
                gated[origin, c], weight[deep, where], preferred_element_type=jnp.float32
            )
            total[:, where] = value if fresh else total[:, where] + value
            return carry

        lax.fori_loop(0, columns // wide, column, 0)

    multiply(place, 0, True)

    def multiply_own(c, carry):
        multiply(place, c, False)
        return carry

    lax.fori_loop(1, chunks, multiply_own, 0)
    first_up = jnp.where(2 * place >= shards, 1, 0)

    def collect(index, carry):
        distance, side = index // (2 * chunks) + 1, lax.rem(index // chunks, 2)
        c = lax.rem(index, chunks)
        up = lax.rem(first_up + side, 2)
        gated_line.pass_on(distance, c, up)
        origin = place - distance * (2 * up - 1)

        @pl.when(gated_line.inside(origin))
        def _():
            multiply(jnp.clip(origin, 0, shards - 1), c, False)

        return carry

    lax.fori_loop(0, 2 * chunks * (shards - 1), collect, 0)
    out_ref[...] = total[...].astype(jnp.bfloat16)

    for swap in swaps:
        swap.wait_send()

    @pl.when(me + 1 < parts)
    def _():
        tail.wait_send()

    line.sent()
    gated_line.sent()
    pltpu.make_async_copy(arrived, arrived, sum_send).wait()


def paired_kernel(
    shards,
    hidden_in,
    gain_in,
    planes_ref,
    taps_in,
    decay_in,
    skip_in,
    tail_in,
    weight_ref,
    out_ref,
    hidden_ref,
    gain_ref,
    taps_ref,
    decay_ref,
    skip_ref,
    tail_ref,
    normed,
    first,
    planes,
    slots,
    mine,
    outgoing,
    arrived,
    extended,
    filtered,
    bands,
    weight,
    gated,
    handed,
    total,
    input_sem,
    load_sem,
    own_sem,
    planes_send,
    planes_recv,
    swap_send,
    line_send,
    line_recv,
    pair_send,
    pair_recv,
    sum_send,
    sum_recv,
    tail_send,
    tail_recv,
    hand_send,
    hand_recv,
    gated_send,
    gated_recv,
):
    rows = hidden_ref.shape[0]
    parts = slots.shape[1] // rows
    _, both_depths, half = planes.shape
    depth = both_depths // 2
    _, taps, _ = bands.shape
    chunks, all_rows, chunk = gated.shape[1:]
    columns = out_ref.shape[1]
    tile = min(256, half)
    tiles = half // tile
    me, place = lax.axis_index("ctx"), lax.axis_index("tensor")
    pair, core = me // 2, lax.rem(me, 2)
    across = 1 - pair
    sibling, peer = 2 * pair + 1 - core, 2 * across + core

    others = [lax.rem(me + 1 + k, parts) for k in range(parts - 1)]
    neighbours = [
        ("tensor", jnp.maximum(place - 1, 0), place > 0),
        ("tensor", jnp.minimum(place + 1, shards - 1), place < shards - 1),
    ]
    greeted = greet([("ctx", other, me >= 0) for other in others] + neighbours)
    inputs = [
        pltpu.make_async_copy(source, target, input_sem.at[k])
        for k, (source, target) in enumerate(
            [
                (hidden_in, hidden_ref),
                (gain_in, gain_ref),
                (taps_in, taps_ref),
                (decay_in, decay_ref),
                (skip_in, skip_ref),
                (tail_in, tail_ref),
            ]
        )
    ]
    for load in inputs:
        load.start()
    loads = [
        pltpu.make_async_copy(
            planes_ref.at[g, :, span(core, half)], planes.at[g, span(core, depth)], load_sem.at[g]
        )
        for g in (1, 2, 0)
    ]
    for load in loads:
        load.start()
    last_load = pltpu.make_async_copy(weight_ref, weight, load_sem.at[3])
    for load in inputs[:2]:
        load.wait()
    normalize_rows(hidden_ref, gain_ref, normed)
    mine_in = normed.at[:, span(pair, both_depths)]
    own = pltpu.make_async_copy(mine_in, slots.at[place, span(me, rows)], own_sem)
    own.start()
    pl.semaphore_wait(pltpu.get_barrier_semaphore(), greeted)

    def remote(source, target, send, recv, **device):
        return pltpu.make_async_remote_copy(
            src_ref=source,
            dst_ref=target,
            send_sem=send,
            recv_sem=recv,
            device_id=device,
            device_id_type=MESH,
        )

    line = Line(
        shards,
        parts,
        lambda origin, c: slots.at[origin, span(c, rows), span(core, depth)],
        line_send,
        line_recv,
    )
    line.send(place, me, 0, normed.at[:, span(me, depth)])
    line.send(place, me, 1, normed.at[:, span(me, depth)])
    to_sibling = remote(
        mine_in, slots.at[place, span(me, rows)], pair_send, pair_recv.at[place, me], ctx=sibling
    )
    to_sibling.start()
    swaps = [
        remote(
            normed.at[:, span(2 * across + k, depth)],
            slots.at[place, span(me, rows), pl.ds(k * depth, depth)],
            swap_send.at[k],
            line_recv.at[place, me],
            ctx=2 * across + k,
        )
        for k in range(2)
    ]
    swaps[0].start()
    shares = [
        remote(
            planes_ref.at[g, :, span(1 - core, half)],
            planes.at[g, span(core, depth)],
            planes_send,
            planes_recv.at[g],
            ctx=sibling,
        )
        for g in (1, 2, 0)
    ]
    for share in shares:
        share.start()

    def share_piece(origin, c):
        ref = slots.at[origin, span(c, rows), span(core, depth)]
        return remote(ref, ref, pair_send, pair_recv.at[origin, c], ctx=sibling)

    def from_sibling(origin, c):
        ref = slots.at[origin, span(c, rows), span(1 - core, depth)]
        return remote(ref, ref, pair_send, pair_recv.at[origin, c], ctx=sibling)

    for load in inputs[2:]:
        load.wait()
    first[...] = first_rows(taps_ref, decay_ref)

    @pl.when(pair == 0)
    def _():
        padding = jnp.zeros((taps - tail_ref.shape[0], half), jnp.float32)
        extended[pl.ds(0, taps), :] = jnp.concatenate(
            [padding, tail_ref[:, span(core, half)].astype(jnp.float32)], axis=0
        ).astype(jnp.bfloat16)

    remote(
        mine_in,
        slots.at[place, span(sibling, rows)],
        pair_send,
        pair_recv.at[place, sibling],
        ctx=sibling,
    ).wait_recv()
    line.send(place, sibling, 0)
    line.send(place, sibling, 1)

    def write_band(group, carry):
        row = jnp.broadcast_to(first[pl.ds(core * (half // GROUP) + group, 1), :], (taps, 2 * taps))
        bands[group] = pltpu.roll(row, 0, 1, stride=1, stride_axis=0).astype(jnp.bfloat16)
        return carry

    lax.fori_loop(0, half // GROUP, write_band, 0)
    swaps[0].wait_send()
    swaps[1].start()
    for k in range(2):
        c = 2 * across + k
        line.hop(place, c, 1).wait_recv()
        line.send(place, c, 0)
        line.send(place, c, 1)
        share_piece(place, c).start()
    own.wait()
    for load in loads:
        load.wait()
    for share in shares:
        share.wait_recv()
    last_load.start()

    def sum_piece(g, origin):
        where = span(origin, rows)
        return remote(
            outgoing.at[g, :, where],
            arrived.at[g, :, where],
            sum_send,
            sum_recv.at[g, origin],
            ctx=peer,
        )

    def group_of(far):
        return jnp.where(far == 1, across, pair)

    def project(origin, far):
        tokens = span(group_of(far), 2 * rows)

        def step(index, carry):
            g, column = lax.rem(index // tiles + 1, 3), lax.rem(index, tiles)
            where = span(column, tile)
            value = jnp.dot(
                slots[origin, tokens], planes[g, :, where], preferred_element_type=jnp.float32
            )

            def keep(target):
                for k in range(2):
                    target[g, k, span(origin, rows), where] = value[
                        k * rows : (k + 1) * rows
                    ].astype(target.dtype)

            @pl.when(far == 0)
            def _():
                keep(mine)

            @pl.when(far == 1)
            def _():
                keep(outgoing)

            @pl.when((far == 1) & (column == tiles - 1))
            def _():
                sum_piece(g, origin).start()

            return carry

        lax.fori_loop(0, 3 * tiles, step, 0)

    def combine(origin):
        where = span(origin, rows)
        for g in (1, 2, 0):
            sum_piece(g, origin).wait_recv()
        for k in range(2):
            q, key, value = [
                mine[g, k, where] + arrived[g, k, where].astype(jnp.float32) for g in range(3)
            ]
            mine[0, k, where] = q
            start = pl.multiple_of(taps + k * all_rows + origin * rows, rows)
            extended[pl.ds(start, rows), :] = (key * value).astype(jnp.bfloat16)

    def beside(distance, work):
        for origin in (place - distance, place + distance):

            @pl.when(line.inside(origin))
            def _(origin=origin):
                work(jnp.clip(origin, 0, shards - 1))

    def project_own(far, carry):
        @pl.when(far == 1)
        def _():
            for k in range(2):
                from_sibling(place, 2 * across + k).wait_recv()

        project(place, far)
        return carry

    lax.fori_loop(0, 2, project_own, 0)

    def from_side(distance, up):
        origin = place - distance * (2 * up - 1)
        return line.inside(origin), jnp.clip(origin, 0, shards - 1), origin == (1 - up) * (shards - 1)

    def far_at(distance, turn, last):
        return jnp.where(last & (distance > 1), 1 - turn, turn)

    def flow(distance, turn, up):
        there, origin, last = from_side(distance, up)
        held = last & (distance == 1)

        @pl.when(there)
        def _():
            group = group_of(far_at(distance, turn, last))
            for k in range(2):
                line.hop(origin, 2 * group + k, up).wait_recv()

                @pl.when(~held | (turn == 1))
                def _(k=k):
                    line.send(origin, 2 * group + k, up)

                share_piece(origin, 2 * group + k).start()

            @pl.when(held & (turn == 1))
            def _():
                for k in range(2):
                    line.send(origin, 2 * pair + k, up)

    def project_side(distance, turn, up):
        there, origin, last = from_side(distance, up)

        @pl.when(there)
        def _():
            far = far_at(distance, turn, last)
            for k in range(2):
                from_sibling(origin, 2 * group_of(far) + k).wait_recv()
            project(origin, far)

    def stage(distance, carry):
        def half_stage(turn, inner):
            flow(distance, turn, 1)
            flow(distance, turn, 0)

            def side(up, nothing):
                project_side(distance, turn, up)
                return nothing

            lax.fori_loop(0, 2, side, 0)
            return inner

        lax.fori_loop(0, 2, half_stage, 0)

        @pl.when(distance == 1)
        def _():
            combine(place)

        @pl.when(distance > 1)
        def _():
            beside(distance - 1, combine)

        return carry

    lax.fori_loop(1, shards, stage, 0)
    beside(shards - 1, combine)
    before = extended.at[pl.ds(0, taps)]
    tail = remote(
        extended.at[pl.ds(2 * all_rows, taps)], before, tail_send, tail_recv, ctx=peer
    )

    @pl.when(pair == 0)
    def _():
        tail.start()

    per, windows_count = LANES // GROUP, all_rows // taps

    def filter_lanes(k, block):
        where = span(block, LANES)
        values = extended[pl.ds(k * all_rows, taps + all_rows), where]
        windows = jnp.concatenate(
            [values[b * taps : (b + 2) * taps] for b in range(windows_count)], axis=1
        )
        lane = lax.broadcasted_iota(jnp.int32, windows.shape, 1)
        owner = lax.rem(lane, LANES) // GROUP
        sums = jnp.zeros((taps, windows_count * LANES), jnp.float32)
        for group in range(per):
            some = jnp.where(owner == group, windows, jnp.zeros_like(windows))
            sums = sums + jnp.dot(
                bands[block * per + group], some, preferred_element_type=jnp.float32
            )
        skip = skip_ref[:, pl.ds(pl.multiple_of(core * half + block * LANES, LANES), LANES)]
        for b in range(windows_count):
            direct = skip * values[(b + 1) * taps : (b + 2) * taps].astype(jnp.float32)
            filtered[pl.ds(b * taps, taps), where] = sums[:, b * LANES : (b + 1) * LANES] + direct

    gated_line = Line(
        shards, chunks, lambda origin, c: gated.at[origin, c], gated_send, gated_recv
    )
    mine_chunks = half // chunk

    def hand(i, owner):
        c = owner * mine_chunks + i
        return remote(handed.at[i], gated.at[place, c], hand_send, hand_recv.at[i], ctx=sibling)

    inner_place = (place > 0) & (place < shards - 1)

    def send_gated(c):
        gated_line.send(place, c, 0)
        gated_line.send(place, c, 1)

    def gate_half(step, carry):
        k = 1 - step

        @pl.when((k == 0) & (pair == 1))
        def _():
            tail.wait_recv()

        def gate_chunk(i, inner):
            def lanes(block, nothing):
                filter_lanes(k, block)
                return nothing

            per_chunk = chunk // LANES
            lax.fori_loop(i * per_chunk, (i + 1) * per_chunk, lanes, 0)
            where, c = span(i, chunk), core * mine_chunks + i
            value = (mine[0, k, :, where] * filtered[:, where]).astype(jnp.bfloat16)

            @pl.when(k == core)
            def _():
                gated[place, c] = value

            @pl.when((k == core) & ~inner_place)
            def _():
                send_gated(c)

            @pl.when(k != core)
            def _():
                handed[i] = value
                hand(i, core).start()

            return inner

        lax.fori_loop(0, mine_chunks, gate_chunk, 0)
        return carry

    lax.fori_loop(0, 2, gate_half, 0)

    def take(i, carry):
        hand(i, 1 - core).wait_recv()

        @pl.when(~inner_place)
        def _():
            send_gated((1 - core) * mine_chunks + i)

        return carry

    lax.fori_loop(0, mine_chunks, take, 0)
    line.sent()

    @pl.when(inner_place)
    def _():
        for i in range(chunks):
            send_gated(lax.rem(core * mine_chunks + i, chunks))

    last_load.wait()
    wide = min(512, columns)

    def multiply(origin, c, fresh=False, last=False):
        deep = span(origin * chunks + c, chunk)
        for start in range(0, columns, wide):
            where = pl.ds(start, wide)
            value = jnp.dot(
                gated[origin, c], weight[deep, where], preferred_element_type=jnp.float32
            )
            if not fresh:
                value = total[:, where] + value
            if last:
                out_ref[:, where] = value.astype(jnp.bfloat16)
            else:
                total[:, where] = value

    multiply(place, 0, True)

    def multiply_own(c, carry):
        multiply(place, c)
        return carry

    lax.fori_loop(1, chunks, multiply_own, 0)
    first_up = jnp.where(2 * place >= shards, 1, 0)

    def collect(index, carry):
        distance, side = index // (2 * chunks) + 1, lax.rem(index // chunks, 2)
        step = lax.rem(index, chunks)
        c = lax.rem(step + core * mine_chunks, chunks)
        up = lax.rem(first_up + side, 2)
        gated_line.pass_on(distance, c, up)
        origin = place - distance * (2 * up - 1)

        final = (distance == shards - 1) & (step == chunks - 1)

        @pl.when(gated_line.inside(origin) & ~final)
        def _():
            multiply(jnp.clip(origin, 0, shards - 1), c)

        @pl.when(gated_line.inside(origin) & final)
        def _():
            multiply(jnp.clip(origin, 0, shards - 1), c, last=True)

        return carry

    lax.fori_loop(0, 2 * chunks * (shards - 1), collect, 0)

    @pl.when(inner_place)
    def _():
        out_ref[...] = total[...].astype(jnp.bfloat16)

    swaps[1].wait_send()

    @pl.when(pair == 0)
    def _():
        tail.wait_send()

    gated_line.sent()
    slices = slots.at[:, :, pl.ds(0, depth)]
    pltpu.make_async_copy(slices, slices, pair_send).wait()
    pltpu.make_async_copy(handed, handed, hand_send).wait()
    pltpu.make_async_copy(outgoing, outgoing, sum_send).wait()
    sent_planes = planes.at[:, pl.ds(0, depth)]
    pltpu.make_async_copy(sent_planes, sent_planes, planes_send).wait()


def on_paired_device(
    hidden_in, norm_gain, weight_in, filter_taps, filter_decay, skip_gain, tail_cache, output_weight
):
    shards, parts = lax.axis_size("tensor"), lax.axis_size("ctx")
    rows = hidden_in.shape[0]
    depth, _, channels = weight_in.shape
    groups, taps = filter_taps.shape
    columns = output_weight.shape[1]
    all_rows = shards * rows
    half = channels // 2
    chunk = min(256, half)
    chunks = channels // chunk
    anywhere = pl.BlockSpec(memory_space=pl.ANY)
    dma = pltpu.SemaphoreType.DMA
    bf16, f32 = jnp.bfloat16, jnp.float32
    return pl.pallas_call(
        functools.partial(paired_kernel, shards),
        out_shape=pltpu.VMEM((all_rows, columns), bf16),
        in_specs=[anywhere] * 8,
        out_specs=pl.BlockSpec(memory_space=pltpu.VMEM),
        scratch_shapes=[
            pltpu.VMEM(hidden_in.shape, bf16),
            pltpu.VMEM((1, norm_gain.shape[0]), f32),
            pltpu.VMEM(filter_taps.shape, f32),
            pltpu.VMEM((1, groups), f32),
            pltpu.VMEM((1, channels), f32),
            pltpu.VMEM(tail_cache.shape, bf16),
            pltpu.VMEM((rows, hidden_in.shape[1]), bf16),
            pltpu.VMEM((groups, 2 * taps), f32),
            pltpu.VMEM((3, 2 * depth, half), bf16),
            pltpu.VMEM((shards, parts * rows, 2 * depth), bf16),
            pltpu.VMEM((3, 2, all_rows, half), f32),
            pltpu.VMEM((3, 2, all_rows, half), bf16),
            pltpu.VMEM((3, 2, all_rows, half), bf16),
            pltpu.VMEM((taps + 2 * all_rows, half), bf16),
            pltpu.VMEM((all_rows, half), f32),
            pltpu.VMEM((groups // 2, taps, 2 * taps), bf16),
            pltpu.VMEM(output_weight.shape, bf16),
            pltpu.VMEM((shards, chunks, all_rows, chunk), bf16),
            pltpu.VMEM((chunks // 2, all_rows, chunk), bf16),
            pltpu.VMEM((all_rows, columns), f32),
            dma((6,)),
            dma((4,)),
            dma,
            dma,
            dma((3,)),
            dma((2,)),
            dma((2, shards, parts)),
            dma((shards, parts)),
            dma,
            dma((shards, parts)),
            dma,
            dma((3, shards)),
            dma,
            dma,
            dma,
            dma((chunks // 2,)),
            dma((2, shards, chunks)),
            dma((shards, chunks)),
        ],
        compiler_params=pltpu.CompilerParams(
            collective_id=0, has_side_effects=True, vmem_limit_bytes=54 << 20
        ),
    )(
        hidden_in,
        norm_gain.reshape(1, norm_gain.shape[0]),
        weight_in.transpose(1, 0, 2),
        filter_taps,
        filter_decay.reshape(1, groups),
        skip_gain.reshape(1, channels),
        tail_cache,
        output_weight,
    )


def on_device(
    hidden_in, norm_gain, weight_in, filter_taps, filter_decay, skip_gain, tail_cache, output_weight
):
    shards, parts = lax.axis_size("tensor"), lax.axis_size("ctx")
    rows = hidden_in.shape[0]
    depth, _, channels = weight_in.shape
    groups, taps = filter_taps.shape
    columns = output_weight.shape[1]
    all_rows = shards * rows
    chunk = min(256, channels)
    chunks = channels // chunk
    vmem, anywhere = pl.BlockSpec(memory_space=pltpu.VMEM), pl.BlockSpec(memory_space=pl.ANY)
    dma = pltpu.SemaphoreType.DMA
    bf16, f32 = jnp.bfloat16, jnp.float32
    return pl.pallas_call(
        functools.partial(mixer_kernel, shards, parts),
        out_shape=jax.ShapeDtypeStruct((all_rows, columns), bf16),
        in_specs=[vmem, vmem, anywhere, vmem, vmem, vmem, vmem, anywhere],
        out_specs=vmem,
        scratch_shapes=[
            pltpu.VMEM((rows, hidden_in.shape[1]), bf16),
            pltpu.VMEM((groups, 2 * taps), f32),
            pltpu.VMEM((3, depth, channels), bf16),
            pltpu.VMEM((shards, parts * rows, depth), bf16),
            pltpu.VMEM((3, shards, parts * rows, channels), bf16),
            pltpu.VMEM((3, parts - 1, all_rows, channels), bf16),
            pltpu.VMEM((all_rows, channels), f32),
            pltpu.VMEM((all_rows, channels), bf16),
            pltpu.VMEM((taps, channels), bf16),
            pltpu.VMEM((groups, taps, 2 * taps), bf16),
            pltpu.VMEM(output_weight.shape, bf16),
            pltpu.VMEM((shards, chunks, all_rows, chunk), bf16),
            pltpu.VMEM((all_rows, columns), f32),
            dma((4,)),
            dma,
            dma((parts - 1,)),
            dma((parts - 1,)),
            dma((2, shards, parts)),
            dma((shards, parts)),
            dma,
            dma((3,)),
            dma,
            dma,
            dma((2, shards, chunks)),
            dma((shards, chunks)),
        ],
        compiler_params=pltpu.CompilerParams(
            collective_id=0, has_side_effects=True, vmem_limit_bytes=56 << 20
        ),
    )(
        hidden_in,
        norm_gain.reshape(1, norm_gain.shape[0]),
        weight_in.transpose(1, 0, 2),
        filter_taps,
        filter_decay.reshape(1, groups),
        skip_gain.reshape(1, channels),
        tail_cache,
        output_weight,
    )


def solution(mesh):
    in_specs = (
        P(("prompt", "ctx", "tensor"), None),
        P(),
        P("ctx", None, "tensor"),
        P("tensor", None),
        P("tensor"),
        P("tensor"),
        P("prompt", "tensor"),
        P(None, "tensor"),
    )
    out_specs = P(("prompt", "ctx"), "tensor")
    paired = mesh.shape["ctx"] == 4 and mesh.shape["tensor"] > 1
    return jax.shard_map(
        on_paired_device if paired else on_device, mesh=mesh, in_specs=in_specs, out_specs=out_specs, check_vma=False
    )
```

```python
import functools

import jax
import jax.numpy as jnp
from jax import lax
from jax.experimental import pallas as pl
from jax.experimental.pallas import tpu as pltpu
from jax.sharding import PartitionSpec as P

GROUP = 16
LANES = 128
MESH = pl.DeviceIdType.MESH


def span(index, size):
    return pl.ds(pl.multiple_of(index * size, size), size)


def greet(peers):
    barrier = pltpu.get_barrier_semaphore()
    for axis, peer, there in peers:

        @pl.when(there)
        def _(axis=axis, peer=peer):
            pl.semaphore_signal(barrier, inc=1, device_id={axis: peer}, device_id_type=MESH)

    return sum(jnp.where(there, 1, 0) for _, _, there in peers)


def normalize_rows(hidden_ref, gain_ref, normed):
    rows, width = hidden_ref.shape
    few, part = min(16, rows), 1024

    def step(index, carry):
        where = span(index, few)

        def values(start):
            return hidden_ref[where, pl.ds(start, part)].astype(jnp.float32)

        squares = jnp.zeros((few, part), jnp.float32)
        for start in range(0, width, part):
            squares = squares + values(start) * values(start)
        scaled = lax.rsqrt(jnp.sum(squares, axis=-1, keepdims=True) / width + 1e-06)
        for start in range(0, width, part):
            inner = pl.ds(start, part)
            normed[where, inner] = (values(start) * scaled * gain_ref[:, inner]).astype(
                jnp.bfloat16
            )
        return carry

    lax.fori_loop(0, rows // few, step, 0)


def first_rows(taps_ref, decay_ref):
    groups, taps = taps_ref.shape
    lags = lax.broadcasted_iota(jnp.int32, (groups, taps), 1).astype(jnp.float32)
    across = lax.broadcasted_iota(jnp.int32, (groups, groups), 1)
    down = lax.broadcasted_iota(jnp.int32, (groups, groups), 0)
    decay = jnp.sum(jnp.where(across == down, decay_ref[...], 0.0), axis=1, keepdims=True)
    taps_full = (taps_ref[...] * jnp.exp(-decay * lags)).astype(jnp.bfloat16)
    lag = lax.broadcasted_iota(jnp.int32, (taps, 2 * taps), 0)
    column = lax.broadcasted_iota(jnp.int32, (taps, 2 * taps), 1)
    turned = jnp.where(lag + column == taps, 1.0, 0.0).astype(jnp.bfloat16)
    return jnp.dot(taps_full, turned, preferred_element_type=jnp.float32)


class Line:
    def __init__(self, count, pieces, view, send_sem, recv_sem):
        self.count, self.pieces, self.view = count, pieces, view
        self.send_sem, self.recv_sem = send_sem, recv_sem
        self.place = lax.axis_index("tensor")

    def inside(self, position):
        return (position >= 0) & (position < self.count)

    def hop(self, origin, piece, up, source=None):
        ref = self.view(origin, piece)
        return pltpu.make_async_remote_copy(
            src_ref=ref if source is None else source,
            dst_ref=ref,
            send_sem=self.send_sem.at[up, origin, piece],
            recv_sem=self.recv_sem.at[origin, piece],
            device_id={"tensor": jnp.clip(self.place + 2 * up - 1, 0, self.count - 1)},
            device_id_type=MESH,
        )

    def send(self, origin, piece, up, source=None):
        @pl.when(self.inside(self.place + 2 * up - 1))
        def _():
            self.hop(origin, piece, up, source).start()

    def pass_on(self, distance, piece, up):
        origin = self.place - distance * (2 * up - 1)

        @pl.when(self.inside(origin))
        def _():
            source = jnp.clip(origin, 0, self.count - 1)
            self.hop(source, piece, up).wait_recv()
            self.send(source, piece, up)

    def follow(self, origin, piece, up, before):
        @pl.when(self.inside(self.place + 2 * up - 1))
        def _():
            self.hop(jnp.clip(origin + 2 * up - 1, 0, self.count - 1), before, up).wait_send()
            self.hop(origin, piece, up).start()

    def last_sent(self):
        for up in (0, 1):

            @pl.when(self.inside(self.place + 2 * up - 1))
            def _(up=up):
                def step(piece, carry):
                    self.hop((1 - up) * (self.count - 1), piece, up).wait_send()
                    return carry

                lax.fori_loop(0, self.pieces, step, 0)

    def sent(self):
        def step(index, carry):
            origin, piece = index // self.pieces, lax.rem(index, self.pieces)

            @pl.when((origin <= self.place) & (self.place + 1 < self.count))
            def _():
                self.hop(origin, piece, 1).wait_send()

            @pl.when((origin >= self.place) & (self.place > 0))
            def _():
                self.hop(origin, piece, 0).wait_send()

            return carry

        lax.fori_loop(0, self.count * self.pieces, step, 0)


def mixer_kernel(
    shards,
    parts,
    hidden_ref,
    gain_ref,
    planes_ref,
    taps_ref,
    decay_ref,
    skip_ref,
    tail_ref,
    weight_ref,
    out_ref,
    normed,
    first,
    planes,
    slots,
    partial,
    arrived,
    filtered,
    product,
    before,
    bands,
    weight,
    gated,
    total,
    load_sem,
    own_sem,
    swap_send,
    swap_recv,
    line_send,
    line_recv,
    sum_send,
    sum_recv,
    tail_send,
    tail_recv,
    gated_send,
    gated_recv,
):
    rows = hidden_ref.shape[0]
    _, depth, channels = planes.shape
    groups, taps, _ = bands.shape
    chunks, all_rows, chunk = gated.shape[1:]
    columns = out_ref.shape[1]
    tile = min(256, channels)
    me, place = lax.axis_index("ctx"), lax.axis_index("tensor")
    others = [lax.rem(me + 1 + k, parts) for k in range(parts - 1)]

    loads = [
        pltpu.make_async_copy(planes_ref.at[g], planes.at[g], load_sem.at[g]) for g in (1, 2, 0)
    ]
    for load in loads:
        load.start()
    last_load = pltpu.make_async_copy(weight_ref, weight, load_sem.at[3])
    last_load.start()
    neighbours = [
        ("tensor", jnp.maximum(place - 1, 0), place > 0),
        ("tensor", jnp.minimum(place + 1, shards - 1), place < shards - 1),
    ]
    greeted = greet([("ctx", other, me >= 0) for other in others] + neighbours)
    normalize_rows(hidden_ref, gain_ref, normed)
    own = pltpu.make_async_copy(
        normed.at[:, span(me, depth)], slots.at[place, span(me, rows)], own_sem
    )
    own.start()
    pl.semaphore_wait(pltpu.get_barrier_semaphore(), greeted)

    swaps = [
        pltpu.make_async_remote_copy(
            src_ref=normed.at[:, span(other, depth)],
            dst_ref=slots.at[place, span(me, rows)],
            send_sem=swap_send.at[k],
            recv_sem=swap_recv.at[parts - 2 - k],
            device_id={"ctx": other},
            device_id_type=MESH,
        )
        for k, other in enumerate(others)
    ]
    for swap in swaps:
        swap.start()
    line = Line(
        shards, parts, lambda origin, c: slots.at[origin, span(c, rows)], line_send, line_recv
    )
    own.wait()
    line.send(place, me, 0)
    line.send(place, me, 1)

    first[...] = first_rows(taps_ref, decay_ref)

    @pl.when(me == 0)
    def _():
        padding = jnp.zeros((taps - tail_ref.shape[0], channels), jnp.float32)
        before[...] = jnp.concatenate(
            [padding, tail_ref[...].astype(jnp.float32)], axis=0
        ).astype(jnp.bfloat16)

    for k in range(parts - 1):
        swaps[parts - 2 - k].wait_recv()
        line.send(place, others[k], 0)
        line.send(place, others[k], 1)

    def write_band(group, carry):
        row = jnp.broadcast_to(first[pl.ds(group, 1), :], (taps, 2 * taps))
        bands[group] = pltpu.roll(row, 0, 1, stride=1, stride_axis=0).astype(jnp.bfloat16)
        return carry

    lax.fori_loop(0, groups, write_band, 0)
    for load in loads:
        load.wait()

    tiles = channels // tile

    def project(origin, k):
        def step(index, carry):
            g, column = lax.rem(index // tiles + 1, 3), lax.rem(index, tiles)
            where = span(column, tile)
            partial[g, origin, :, where] = jnp.dot(
                slots[origin], planes[g, :, where], preferred_element_type=jnp.float32
            ).astype(jnp.bfloat16)

            @pl.when(column == tiles - 1)
            def _():
                for k, other in enumerate(others):
                    pltpu.make_async_remote_copy(
                        src_ref=partial.at[g, origin, span(other, rows)],
                        dst_ref=arrived.at[g, parts - 2 - k, span(origin, rows)],
                        send_sem=sum_send,
                        recv_sem=sum_recv.at[g],
                        device_id={"ctx": other},
                        device_id_type=MESH,
                    ).start()

            return carry

        steps = 3 * tiles
        lax.fori_loop(k * steps // parts, (k + 1) * steps // parts, step, 0)

    def project_from(distance, k):
        below, above = place - distance, place + distance

        @pl.when(line.inside(below))
        def _():
            project(jnp.maximum(below, 0), k)

        @pl.when(line.inside(above) & (distance > 0))
        def _():
            project(jnp.minimum(above, shards - 1), k)

    def project_piece(origin, piece):
        mine = span(piece, rows)

        def plane(step, carry):
            g = lax.rem(step + 1, 3)

            def columns(column, inner):
                where = span(column, tile)
                partial[g, origin, mine, where] = jnp.dot(
                    slots[origin, mine], planes[g, :, where], preferred_element_type=jnp.float32
                ).astype(jnp.bfloat16)
                return inner

            lax.fori_loop(0, tiles, columns, 0)

            @pl.when(piece != me)
            def _():
                slot = jnp.clip(lax.rem(me - piece - 1 + parts, parts), 0, parts - 2)
                pltpu.make_async_remote_copy(
                    src_ref=partial.at[g, origin, mine],
                    dst_ref=arrived.at[g, slot, span(origin, rows)],
                    send_sem=sum_send,
                    recv_sem=sum_recv.at[g],
                    device_id={"ctx": piece},
                    device_id_type=MESH,
                ).start()

            return carry

        lax.fori_loop(0, 3, plane, 0)

    def stage(index, carry):
        distance, k = index // parts, lax.rem(index, parts)
        project_from(distance, k)
        piece = lax.rem(me + k, parts)
        line.pass_on(distance + 1, piece, 1)
        line.pass_on(distance + 1, piece, 0)

        @pl.when((distance == shards - 2) & ((place == 0) | (place == shards - 1)))
        def _():
            project_piece(shards - 1 - place, piece)

        return carry

    lax.fori_loop(0, (shards - 1) * parts, stage, 0)

    def summed(g, origin, where=slice(None)):
        value = partial[g, origin, span(me, rows), where].astype(jnp.float32)
        for k in range(parts - 1):
            value = value + arrived[g, k, span(origin, rows), where].astype(jnp.float32)
        return value

    for g in (1, 2):
        pltpu.make_async_copy(arrived.at[g], arrived.at[g], sum_recv.at[g]).wait()

    def write_product(step, carry):
        origin = shards - 1 - step
        product[span(origin, rows), :] = (summed(1, origin) * summed(2, origin)).astype(
            jnp.bfloat16
        )
        return carry

    tail_steps = -(-taps // rows)
    lax.fori_loop(0, tail_steps, write_product, 0)
    tail = pltpu.make_async_remote_copy(
        src_ref=product.at[pl.ds(all_rows - taps, taps)],
        dst_ref=before,
        send_sem=tail_send,
        recv_sem=tail_recv,
        device_id={"ctx": jnp.minimum(me + 1, parts - 1)},
        device_id_type=MESH,
    )

    @pl.when(me + 1 < parts)
    def _():
        tail.start()

    lax.fori_loop(tail_steps, shards, write_product, 0)
    @pl.when(me > 0)
    def _():
        tail.wait_recv()

    per, windows_count = LANES // GROUP, all_rows // taps

    def filter_lanes(block, carry):
        where = span(block, LANES)
        extended = jnp.concatenate([before[:, where], product[:, where]], axis=0)
        windows = jnp.concatenate(
            [extended[b * taps : (b + 2) * taps] for b in range(windows_count)], axis=1
        )
        lane = lax.broadcasted_iota(jnp.int32, windows.shape, 1)
        owner = lax.rem(lane, LANES) // GROUP
        sums = jnp.zeros((taps, windows_count * LANES), jnp.float32)
        for group in range(per):
            mine = jnp.where(owner == group, windows, jnp.zeros_like(windows))
            sums = sums + jnp.dot(
                bands[block * per + group], mine, preferred_element_type=jnp.float32
            )
        for b in range(windows_count):
            inner = pl.ds(b * taps, taps)
            direct = skip_ref[:, where] * product[inner, where].astype(jnp.float32)
            filtered[inner, where] = sums[:, b * LANES : (b + 1) * LANES] + direct
        return carry

    lax.fori_loop(0, channels // LANES, filter_lanes, 0)
    pltpu.make_async_copy(arrived.at[0], arrived.at[0], sum_recv.at[0]).wait()

    gated_line = Line(
        shards, chunks, lambda origin, c: gated.at[origin, c], gated_send, gated_recv
    )

    def gate_chunk(c, carry):
        where = span(c, chunk)

        def gate(origin, inner):
            mine = span(origin, rows)
            gated[place, c, mine, :] = (
                summed(0, origin, where) * filtered[mine, where]
            ).astype(jnp.bfloat16)
            return inner

        lax.fori_loop(0, shards, gate, 0)
        gated_line.send(place, c, 0)
        gated_line.send(place, c, 1)
        return carry

    lax.fori_loop(0, chunks, gate_chunk, 0)
    last_load.wait()
    wide = min(512, columns)

    def multiply(origin, c, fresh):
        deep = span(origin * chunks + c, chunk)

        def column(index, carry):
            where = span(index, wide)
            value = jnp.dot(
                gated[origin, c], weight[deep, where], preferred_element_type=jnp.float32
            )
            total[:, where] = value if fresh else total[:, where] + value
            return carry

        lax.fori_loop(0, columns // wide, column, 0)

    multiply(place, 0, True)

    def multiply_own(c, carry):
        multiply(place, c, False)
        return carry

    lax.fori_loop(1, chunks, multiply_own, 0)
    first_up = jnp.where(2 * place >= shards, 1, 0)

    def collect(index, carry):
        distance, side = index // (2 * chunks) + 1, lax.rem(index // chunks, 2)
        c = lax.rem(index, chunks)
        up = lax.rem(first_up + side, 2)
        gated_line.pass_on(distance, c, up)
        origin = place - distance * (2 * up - 1)

        @pl.when(gated_line.inside(origin))
        def _():
            multiply(jnp.clip(origin, 0, shards - 1), c, False)

        return carry

    lax.fori_loop(0, 2 * chunks * (shards - 1), collect, 0)
    out_ref[...] = total[...].astype(jnp.bfloat16)

    for swap in swaps:
        swap.wait_send()

    @pl.when(me + 1 < parts)
    def _():
        tail.wait_send()

    line.sent()
    gated_line.sent()
    pltpu.make_async_copy(arrived, arrived, sum_send).wait()


def paired_kernel(
    shards,
    hidden_in,
    gain_in,
    planes_ref,
    taps_in,
    decay_in,
    skip_in,
    tail_in,
    weight_ref,
    out_ref,
    hidden_ref,
    gain_ref,
    taps_ref,
    decay_ref,
    skip_ref,
    tail_ref,
    normed,
    first,
    planes,
    slots,
    mine,
    outgoing,
    arrived,
    extended,
    filtered,
    bands,
    weight,
    gated,
    handed,
    total,
    input_sem,
    load_sem,
    own_sem,
    planes_send,
    planes_recv,
    swap_send,
    line_send,
    line_recv,
    pair_send,
    pair_recv,
    sum_send,
    sum_recv,
    tail_send,
    tail_recv,
    hand_send,
    hand_recv,
    gated_send,
    gated_recv,
):
    rows = hidden_ref.shape[0]
    parts = slots.shape[1] // rows
    _, both_depths, half = planes.shape
    depth = both_depths // 2
    _, taps, _ = bands.shape
    chunks, all_rows, chunk = gated.shape[1:]
    columns = out_ref.shape[1]
    tile = min(256, half)
    tiles = half // tile
    me, place = lax.axis_index("ctx"), lax.axis_index("tensor")
    pair, core = me // 2, lax.rem(me, 2)
    across = 1 - pair
    sibling, peer = 2 * pair + 1 - core, 2 * across + core

    others = [lax.rem(me + 1 + k, parts) for k in range(parts - 1)]
    neighbours = [
        ("tensor", jnp.maximum(place - 1, 0), place > 0),
        ("tensor", jnp.minimum(place + 1, shards - 1), place < shards - 1),
    ]
    greeted = greet([("ctx", other, me >= 0) for other in others] + neighbours)
    inputs = [
        pltpu.make_async_copy(source, target, input_sem.at[k])
        for k, (source, target) in enumerate(
            [
                (hidden_in, hidden_ref),
                (gain_in, gain_ref),
                (taps_in, taps_ref),
                (decay_in, decay_ref),
                (skip_in, skip_ref),
                (tail_in, tail_ref),
            ]
        )
    ]
    for load in inputs:
        load.start()
    loads = [
        pltpu.make_async_copy(
            planes_ref.at[g, :, span(core, half)], planes.at[g, span(core, depth)], load_sem.at[g]
        )
        for g in (1, 2, 0)
    ]
    for load in loads:
        load.start()
    last_load = pltpu.make_async_copy(weight_ref, weight, load_sem.at[3])
    for load in inputs[:2]:
        load.wait()
    normalize_rows(hidden_ref, gain_ref, normed)
    mine_in = normed.at[:, span(pair, both_depths)]
    own = pltpu.make_async_copy(mine_in, slots.at[place, span(me, rows)], own_sem)
    own.start()
    pl.semaphore_wait(pltpu.get_barrier_semaphore(), greeted)

    def remote(source, target, send, recv, **device):
        return pltpu.make_async_remote_copy(
            src_ref=source,
            dst_ref=target,
            send_sem=send,
            recv_sem=recv,
            device_id=device,
            device_id_type=MESH,
        )

    line = Line(
        shards,
        parts,
        lambda origin, c: slots.at[origin, span(c, rows), span(core, depth)],
        line_send,
        line_recv,
    )
    line.send(place, me, 0, normed.at[:, span(me, depth)])
    line.send(place, me, 1, normed.at[:, span(me, depth)])
    to_sibling = remote(
        mine_in, slots.at[place, span(me, rows)], pair_send, pair_recv.at[place, me], ctx=sibling
    )
    to_sibling.start()
    swaps = [
        remote(
            normed.at[:, span(2 * across + k, depth)],
            slots.at[place, span(me, rows), pl.ds(k * depth, depth)],
            swap_send.at[k],
            line_recv.at[place, me],
            ctx=2 * across + k,
        )
        for k in range(2)
    ]
    swaps[0].start()
    shares = [
        remote(
            planes_ref.at[g, :, span(1 - core, half)],
            planes.at[g, span(core, depth)],
            planes_send,
            planes_recv.at[g],
            ctx=sibling,
        )
        for g in (1, 2, 0)
    ]
    for share in shares:
        share.start()

    def share_piece(origin, c):
        ref = slots.at[origin, span(c, rows), span(core, depth)]
        return remote(ref, ref, pair_send, pair_recv.at[origin, c], ctx=sibling)

    def from_sibling(origin, c):
        ref = slots.at[origin, span(c, rows), span(1 - core, depth)]
        return remote(ref, ref, pair_send, pair_recv.at[origin, c], ctx=sibling)

    for load in inputs[2:]:
        load.wait()
    first[...] = first_rows(taps_ref, decay_ref)

    @pl.when(pair == 0)
    def _():
        padding = jnp.zeros((taps - tail_ref.shape[0], half), jnp.float32)
        extended[pl.ds(0, taps), :] = jnp.concatenate(
            [padding, tail_ref[:, span(core, half)].astype(jnp.float32)], axis=0
        ).astype(jnp.bfloat16)

    remote(
        mine_in,
        slots.at[place, span(sibling, rows)],
        pair_send,
        pair_recv.at[place, sibling],
        ctx=sibling,
    ).wait_recv()
    line.send(place, sibling, 0)
    line.send(place, sibling, 1)

    def write_band(group, carry):
        row = jnp.broadcast_to(first[pl.ds(core * (half // GROUP) + group, 1), :], (taps, 2 * taps))
        bands[group] = pltpu.roll(row, 0, 1, stride=1, stride_axis=0).astype(jnp.bfloat16)
        return carry

    lax.fori_loop(0, half // GROUP, write_band, 0)
    swaps[0].wait_send()
    swaps[1].start()
    for k in range(2):
        c = 2 * across + k
        line.hop(place, c, 1).wait_recv()
        line.send(place, c, 0)
        line.send(place, c, 1)
        share_piece(place, c).start()
    own.wait()
    for load in loads:
        load.wait()
    for share in shares:
        share.wait_recv()
    last_load.start()

    def sum_piece(g, origin):
        where = span(origin, rows)
        return remote(
            outgoing.at[g, :, where],
            arrived.at[g, :, where],
            sum_send,
            sum_recv.at[g, origin],
            ctx=peer,
        )

    def group_of(far):
        return jnp.where(far == 1, across, pair)

    def project(origin, far):
        tokens = span(group_of(far), 2 * rows)

        def step(index, carry):
            g, column = lax.rem(index // tiles + 1, 3), lax.rem(index, tiles)
            where = span(column, tile)
            value = jnp.dot(
                slots[origin, tokens], planes[g, :, where], preferred_element_type=jnp.float32
            )

            def keep(target):
                for k in range(2):
                    target[g, k, span(origin, rows), where] = value[
                        k * rows : (k + 1) * rows
                    ].astype(target.dtype)

            @pl.when(far == 0)
            def _():
                keep(mine)

            @pl.when(far == 1)
            def _():
                keep(outgoing)

            @pl.when((far == 1) & (column == tiles - 1))
            def _():
                sum_piece(g, origin).start()

            return carry

        lax.fori_loop(0, 3 * tiles, step, 0)

    def combine(origin):
        where = span(origin, rows)
        for g in (1, 2, 0):
            sum_piece(g, origin).wait_recv()
        for k in range(2):
            q, key, value = [
                mine[g, k, where] + arrived[g, k, where].astype(jnp.float32) for g in range(3)
            ]
            mine[0, k, where] = q
            start = pl.multiple_of(taps + k * all_rows + origin * rows, rows)
            extended[pl.ds(start, rows), :] = (key * value).astype(jnp.bfloat16)

    def beside(distance, work):
        for origin in (place - distance, place + distance):

            @pl.when(line.inside(origin))
            def _(origin=origin):
                work(jnp.clip(origin, 0, shards - 1))

    def project_own(far, carry):
        @pl.when(far == 1)
        def _():
            for k in range(2):
                from_sibling(place, 2 * across + k).wait_recv()

        project(place, far)
        return carry

    lax.fori_loop(0, 2, project_own, 0)

    def from_side(distance, up):
        origin = place - distance * (2 * up - 1)
        return line.inside(origin), jnp.clip(origin, 0, shards - 1), origin == (1 - up) * (shards - 1)

    def far_at(distance, turn, last):
        return jnp.where(last & (distance > 1), 1 - turn, turn)

    def flow(distance, turn, up):
        there, origin, last = from_side(distance, up)
        held = last & (distance == 1)

        @pl.when(there)
        def _():
            group = group_of(far_at(distance, turn, last))
            for k in range(2):
                line.hop(origin, 2 * group + k, up).wait_recv()

                @pl.when(~held | (turn == 1))
                def _(k=k):
                    usual = jnp.where(held, pair, group_of(turn))
                    line.follow(origin, 2 * group + k, up, 2 * usual + k)

                share_piece(origin, 2 * group + k).start()

            @pl.when(held & (turn == 1))
            def _():
                for k in range(2):
                    line.follow(origin, 2 * pair + k, up, 2 * across + k)

    def project_side(distance, turn, up):
        there, origin, last = from_side(distance, up)

        @pl.when(there)
        def _():
            far = far_at(distance, turn, last)
            for k in range(2):
                from_sibling(origin, 2 * group_of(far) + k).wait_recv()
            project(origin, far)

    def stage(distance, carry):
        def half_stage(turn, inner):
            flow(distance, turn, 1)
            flow(distance, turn, 0)

            def side(up, nothing):
                project_side(distance, turn, up)
                return nothing

            lax.fori_loop(0, 2, side, 0)
            return inner

        lax.fori_loop(0, 2, half_stage, 0)

        @pl.when(distance == 1)
        def _():
            combine(place)

        @pl.when(distance > 1)
        def _():
            beside(distance - 1, combine)

        return carry

    lax.fori_loop(1, shards, stage, 0)
    beside(shards - 1, combine)
    before = extended.at[pl.ds(0, taps)]
    tail = remote(
        extended.at[pl.ds(2 * all_rows, taps)], before, tail_send, tail_recv, ctx=peer
    )

    @pl.when(pair == 0)
    def _():
        tail.start()

    per, windows_count = LANES // GROUP, all_rows // taps

    def filter_lanes(k, block):
        where = span(block, LANES)
        values = extended[pl.ds(k * all_rows, taps + all_rows), where]
        windows = jnp.concatenate(
            [values[b * taps : (b + 2) * taps] for b in range(windows_count)], axis=1
        )
        lane = lax.broadcasted_iota(jnp.int32, windows.shape, 1)
        owner = lax.rem(lane, LANES) // GROUP
        sums = jnp.zeros((taps, windows_count * LANES), jnp.float32)
        for group in range(per):
            some = jnp.where(owner == group, windows, jnp.zeros_like(windows))
            sums = sums + jnp.dot(
                bands[block * per + group], some, preferred_element_type=jnp.float32
            )
        skip = skip_ref[:, pl.ds(pl.multiple_of(core * half + block * LANES, LANES), LANES)]
        for b in range(windows_count):
            direct = skip * values[(b + 1) * taps : (b + 2) * taps].astype(jnp.float32)
            filtered[pl.ds(b * taps, taps), where] = sums[:, b * LANES : (b + 1) * LANES] + direct

    gated_line = Line(
        shards, chunks, lambda origin, c: gated.at[origin, c], gated_send, gated_recv
    )
    mine_chunks = half // chunk

    def hand(i, owner):
        c = owner * mine_chunks + i
        return remote(handed.at[i], gated.at[place, c], hand_send, hand_recv.at[i], ctx=sibling)

    inner_place = (place > 0) & (place < shards - 1)

    outward = jnp.where(2 * place >= shards, 1, 0)

    def send_gated(c):
        gated_line.send(place, c, 1 - outward)

        @pl.when(~inner_place)
        def _():
            gated_line.send(place, c, outward)

    def gate_half(step, carry):
        k = 1 - step

        @pl.when((k == 0) & (pair == 1))
        def _():
            tail.wait_recv()

        def gate_chunk(i, inner):
            def lanes(block, nothing):
                filter_lanes(k, block)
                return nothing

            per_chunk = chunk // LANES
            lax.fori_loop(i * per_chunk, (i + 1) * per_chunk, lanes, 0)
            where, c = span(i, chunk), core * mine_chunks + i
            value = (mine[0, k, :, where] * filtered[:, where]).astype(jnp.bfloat16)

            @pl.when(k == core)
            def _():
                gated[place, c] = value
                send_gated(c)

            @pl.when(k != core)
            def _():
                handed[i] = value
                hand(i, core).start()

            return inner

        lax.fori_loop(0, mine_chunks, gate_chunk, 0)
        return carry

    lax.fori_loop(0, 2, gate_half, 0)

    def take(i, carry):
        hand(i, 1 - core).wait_recv()
        send_gated((1 - core) * mine_chunks + i)
        return carry

    lax.fori_loop(0, mine_chunks, take, 0)
    line.last_sent()

    @pl.when(inner_place)
    def _():
        for i in range(chunks):
            gated_line.send(place, lax.rem(core * mine_chunks + i, chunks), outward)

    last_load.wait()
    wide = min(512, columns)

    def multiply(origin, c, fresh=False, last=False):
        deep = span(origin * chunks + c, chunk)
        for start in range(0, columns, wide):
            where = pl.ds(start, wide)
            value = jnp.dot(
                gated[origin, c], weight[deep, where], preferred_element_type=jnp.float32
            )
            if not fresh:
                value = total[:, where] + value
            if last:
                out_ref[:, where] = value.astype(jnp.bfloat16)
            else:
                total[:, where] = value

    multiply(place, 0, True)

    def multiply_own(c, carry):
        multiply(place, c)
        return carry

    lax.fori_loop(1, chunks, multiply_own, 0)
    def collect(index, carry):
        distance, side = index // (2 * chunks) + 1, lax.rem(index // chunks, 2)
        step = lax.rem(index, chunks)
        c = lax.rem(step + core * mine_chunks, chunks)
        up = lax.rem(outward + side, 2)
        origin = place - distance * (2 * up - 1)

        @pl.when(gated_line.inside(origin))
        def _():
            source = jnp.clip(origin, 0, shards - 1)
            gated_line.hop(source, c, up).wait_recv()
            gated_line.follow(source, c, up, c)


        final = (distance == shards - 1) & (step == chunks - 1)

        @pl.when(gated_line.inside(origin) & ~final)
        def _():
            multiply(jnp.clip(origin, 0, shards - 1), c)

        @pl.when(gated_line.inside(origin) & final)
        def _():
            multiply(jnp.clip(origin, 0, shards - 1), c, last=True)

        return carry

    lax.fori_loop(0, 2 * chunks * (shards - 1), collect, 0)

    @pl.when(inner_place)
    def _():
        out_ref[...] = total[...].astype(jnp.bfloat16)

    swaps[1].wait_send()

    @pl.when(pair == 0)
    def _():
        tail.wait_send()

    gated_line.last_sent()
    slices = slots.at[:, :, pl.ds(0, depth)]
    pltpu.make_async_copy(slices, slices, pair_send).wait()
    pltpu.make_async_copy(handed, handed, hand_send).wait()
    pltpu.make_async_copy(outgoing, outgoing, sum_send).wait()
    sent_planes = planes.at[:, pl.ds(0, depth)]
    pltpu.make_async_copy(sent_planes, sent_planes, planes_send).wait()


def on_paired_device(
    hidden_in, norm_gain, weight_in, filter_taps, filter_decay, skip_gain, tail_cache, output_weight
):
    shards, parts = lax.axis_size("tensor"), lax.axis_size("ctx")
    rows = hidden_in.shape[0]
    depth, _, channels = weight_in.shape
    groups, taps = filter_taps.shape
    columns = output_weight.shape[1]
    all_rows = shards * rows
    half = channels // 2
    chunk = min(256, half)
    chunks = channels // chunk
    anywhere = pl.BlockSpec(memory_space=pl.ANY)
    dma = pltpu.SemaphoreType.DMA
    bf16, f32 = jnp.bfloat16, jnp.float32
    return pl.pallas_call(
        functools.partial(paired_kernel, shards),
        out_shape=pltpu.VMEM((all_rows, columns), bf16),
        in_specs=[anywhere] * 8,
        out_specs=pl.BlockSpec(memory_space=pltpu.VMEM),
        scratch_shapes=[
            pltpu.VMEM(hidden_in.shape, bf16),
            pltpu.VMEM((1, norm_gain.shape[0]), f32),
            pltpu.VMEM(filter_taps.shape, f32),
            pltpu.VMEM((1, groups), f32),
            pltpu.VMEM((1, channels), f32),
            pltpu.VMEM(tail_cache.shape, bf16),
            pltpu.VMEM((rows, hidden_in.shape[1]), bf16),
            pltpu.VMEM((groups, 2 * taps), f32),
            pltpu.VMEM((3, 2 * depth, half), bf16),
            pltpu.VMEM((shards, parts * rows, 2 * depth), bf16),
            pltpu.VMEM((3, 2, all_rows, half), f32),
            pltpu.VMEM((3, 2, all_rows, half), bf16),
            pltpu.VMEM((3, 2, all_rows, half), bf16),
            pltpu.VMEM((taps + 2 * all_rows, half), bf16),
            pltpu.VMEM((all_rows, half), f32),
            pltpu.VMEM((groups // 2, taps, 2 * taps), bf16),
            pltpu.VMEM(output_weight.shape, bf16),
            pltpu.VMEM((shards, chunks, all_rows, chunk), bf16),
            pltpu.VMEM((chunks // 2, all_rows, chunk), bf16),
            pltpu.VMEM((all_rows, columns), f32),
            dma((6,)),
            dma((4,)),
            dma,
            dma,
            dma((3,)),
            dma((2,)),
            dma((2, shards, parts)),
            dma((shards, parts)),
            dma,
            dma((shards, parts)),
            dma,
            dma((3, shards)),
            dma,
            dma,
            dma,
            dma((chunks // 2,)),
            dma((2, shards, chunks)),
            dma((shards, chunks)),
        ],
        compiler_params=pltpu.CompilerParams(
            collective_id=0, has_side_effects=True, vmem_limit_bytes=54 << 20
        ),
    )(
        hidden_in,
        norm_gain.reshape(1, norm_gain.shape[0]),
        weight_in.transpose(1, 0, 2),
        filter_taps,
        filter_decay.reshape(1, groups),
        skip_gain.reshape(1, channels),
        tail_cache,
        output_weight,
    )


def on_device(
    hidden_in, norm_gain, weight_in, filter_taps, filter_decay, skip_gain, tail_cache, output_weight
):
    shards, parts = lax.axis_size("tensor"), lax.axis_size("ctx")
    rows = hidden_in.shape[0]
    depth, _, channels = weight_in.shape
    groups, taps = filter_taps.shape
    columns = output_weight.shape[1]
    all_rows = shards * rows
    chunk = min(256, channels)
    chunks = channels // chunk
    vmem, anywhere = pl.BlockSpec(memory_space=pltpu.VMEM), pl.BlockSpec(memory_space=pl.ANY)
    dma = pltpu.SemaphoreType.DMA
    bf16, f32 = jnp.bfloat16, jnp.float32
    return pl.pallas_call(
        functools.partial(mixer_kernel, shards, parts),
        out_shape=jax.ShapeDtypeStruct((all_rows, columns), bf16),
        in_specs=[vmem, vmem, anywhere, vmem, vmem, vmem, vmem, anywhere],
        out_specs=vmem,
        scratch_shapes=[
            pltpu.VMEM((rows, hidden_in.shape[1]), bf16),
            pltpu.VMEM((groups, 2 * taps), f32),
            pltpu.VMEM((3, depth, channels), bf16),
            pltpu.VMEM((shards, parts * rows, depth), bf16),
            pltpu.VMEM((3, shards, parts * rows, channels), bf16),
            pltpu.VMEM((3, parts - 1, all_rows, channels), bf16),
            pltpu.VMEM((all_rows, channels), f32),
            pltpu.VMEM((all_rows, channels), bf16),
            pltpu.VMEM((taps, channels), bf16),
            pltpu.VMEM((groups, taps, 2 * taps), bf16),
            pltpu.VMEM(output_weight.shape, bf16),
            pltpu.VMEM((shards, chunks, all_rows, chunk), bf16),
            pltpu.VMEM((all_rows, columns), f32),
            dma((4,)),
            dma,
            dma((parts - 1,)),
            dma((parts - 1,)),
            dma((2, shards, parts)),
            dma((shards, parts)),
            dma,
            dma((3,)),
            dma,
            dma,
            dma((2, shards, chunks)),
            dma((shards, chunks)),
        ],
        compiler_params=pltpu.CompilerParams(
            collective_id=0, has_side_effects=True, vmem_limit_bytes=56 << 20
        ),
    )(
        hidden_in,
        norm_gain.reshape(1, norm_gain.shape[0]),
        weight_in.transpose(1, 0, 2),
        filter_taps,
        filter_decay.reshape(1, groups),
        skip_gain.reshape(1, channels),
        tail_cache,
        output_weight,
    )


def solution(mesh):
    in_specs = (
        P(("prompt", "ctx", "tensor"), None),
        P(),
        P("ctx", None, "tensor"),
        P("tensor", None),
        P("tensor"),
        P("tensor"),
        P("prompt", "tensor"),
        P(None, "tensor"),
    )
    out_specs = P(("prompt", "ctx"), "tensor")
    paired = mesh.shape["ctx"] == 4 and mesh.shape["tensor"] > 1
    return jax.shard_map(
        on_paired_device if paired else on_device, mesh=mesh, in_specs=in_specs, out_specs=out_specs, check_vma=False
    )
```

```python
import functools

import jax
import jax.numpy as jnp
from jax import lax
from jax.experimental import pallas as pl
from jax.experimental.pallas import tpu as pltpu
from jax.sharding import PartitionSpec as P

GROUP = 16
LANES = 128
MESH = pl.DeviceIdType.MESH


def span(index, size):
    return pl.ds(pl.multiple_of(index * size, size), size)


def greet(peers):
    barrier = pltpu.get_barrier_semaphore()
    for axis, peer, there in peers:

        @pl.when(there)
        def _(axis=axis, peer=peer):
            pl.semaphore_signal(barrier, inc=1, device_id={axis: peer}, device_id_type=MESH)

    return sum(jnp.where(there, 1, 0) for _, _, there in peers)


def normalize_rows(hidden_ref, gain_ref, normed):
    rows, width = hidden_ref.shape
    few, part = min(16, rows), 1024

    def step(index, carry):
        where = span(index, few)

        def values(start):
            return hidden_ref[where, pl.ds(start, part)].astype(jnp.float32)

        squares = jnp.zeros((few, part), jnp.float32)
        for start in range(0, width, part):
            squares = squares + values(start) * values(start)
        scaled = lax.rsqrt(jnp.sum(squares, axis=-1, keepdims=True) / width + 1e-06)
        for start in range(0, width, part):
            inner = pl.ds(start, part)
            normed[where, inner] = (values(start) * scaled * gain_ref[:, inner]).astype(
                jnp.bfloat16
            )
        return carry

    lax.fori_loop(0, rows // few, step, 0)


def first_rows(taps_ref, decay_ref):
    groups, taps = taps_ref.shape
    lags = lax.broadcasted_iota(jnp.int32, (groups, taps), 1).astype(jnp.float32)
    across = lax.broadcasted_iota(jnp.int32, (groups, groups), 1)
    down = lax.broadcasted_iota(jnp.int32, (groups, groups), 0)
    decay = jnp.sum(jnp.where(across == down, decay_ref[...], 0.0), axis=1, keepdims=True)
    taps_full = (taps_ref[...] * jnp.exp(-decay * lags)).astype(jnp.bfloat16)
    lag = lax.broadcasted_iota(jnp.int32, (taps, 2 * taps), 0)
    column = lax.broadcasted_iota(jnp.int32, (taps, 2 * taps), 1)
    turned = jnp.where(lag + column == taps, 1.0, 0.0).astype(jnp.bfloat16)
    return jnp.dot(taps_full, turned, preferred_element_type=jnp.float32)


class Line:
    def __init__(self, count, pieces, view, send_sem, recv_sem):
        self.count, self.pieces, self.view = count, pieces, view
        self.send_sem, self.recv_sem = send_sem, recv_sem
        self.place = lax.axis_index("tensor")

    def inside(self, position):
        return (position >= 0) & (position < self.count)

    def hop(self, origin, piece, up, source=None):
        ref = self.view(origin, piece)
        return pltpu.make_async_remote_copy(
            src_ref=ref if source is None else source,
            dst_ref=ref,
            send_sem=self.send_sem.at[up, origin, piece],
            recv_sem=self.recv_sem.at[origin, piece],
            device_id={"tensor": jnp.clip(self.place + 2 * up - 1, 0, self.count - 1)},
            device_id_type=MESH,
        )

    def send(self, origin, piece, up, source=None):
        @pl.when(self.inside(self.place + 2 * up - 1))
        def _():
            self.hop(origin, piece, up, source).start()

    def pass_on(self, distance, piece, up):
        origin = self.place - distance * (2 * up - 1)

        @pl.when(self.inside(origin))
        def _():
            source = jnp.clip(origin, 0, self.count - 1)
            self.hop(source, piece, up).wait_recv()
            self.send(source, piece, up)

    def follow(self, origin, piece, up, before):
        @pl.when(self.inside(self.place + 2 * up - 1))
        def _():
            self.hop(jnp.clip(origin + 2 * up - 1, 0, self.count - 1), before, up).wait_send()
            self.hop(origin, piece, up).start()

    def last_sent(self):
        for up in (0, 1):

            @pl.when(self.inside(self.place + 2 * up - 1))
            def _(up=up):
                def step(piece, carry):
                    self.hop((1 - up) * (self.count - 1), piece, up).wait_send()
                    return carry

                lax.fori_loop(0, self.pieces, step, 0)

    def sent(self):
        def step(index, carry):
            origin, piece = index // self.pieces, lax.rem(index, self.pieces)

            @pl.when((origin <= self.place) & (self.place + 1 < self.count))
            def _():
                self.hop(origin, piece, 1).wait_send()

            @pl.when((origin >= self.place) & (self.place > 0))
            def _():
                self.hop(origin, piece, 0).wait_send()

            return carry

        lax.fori_loop(0, self.count * self.pieces, step, 0)


def mixer_kernel(
    shards,
    parts,
    hidden_ref,
    gain_ref,
    planes_ref,
    taps_ref,
    decay_ref,
    skip_ref,
    tail_ref,
    weight_ref,
    out_ref,
    normed,
    first,
    planes,
    slots,
    partial,
    arrived,
    filtered,
    product,
    before,
    bands,
    weight,
    gated,
    total,
    load_sem,
    own_sem,
    swap_send,
    swap_recv,
    line_send,
    line_recv,
    sum_send,
    sum_recv,
    tail_send,
    tail_recv,
    gated_send,
    gated_recv,
):
    rows = hidden_ref.shape[0]
    _, depth, channels = planes.shape
    groups, taps, _ = bands.shape
    chunks, all_rows, chunk = gated.shape[1:]
    columns = out_ref.shape[1]
    tile = min(256, channels)
    me, place = lax.axis_index("ctx"), lax.axis_index("tensor")
    others = [lax.rem(me + 1 + k, parts) for k in range(parts - 1)]

    loads = [
        pltpu.make_async_copy(planes_ref.at[g], planes.at[g], load_sem.at[g]) for g in (1, 2, 0)
    ]
    for load in loads:
        load.start()
    last_load = pltpu.make_async_copy(weight_ref, weight, load_sem.at[3])
    last_load.start()
    neighbours = [
        ("tensor", jnp.maximum(place - 1, 0), place > 0),
        ("tensor", jnp.minimum(place + 1, shards - 1), place < shards - 1),
    ]
    greeted = greet([("ctx", other, me >= 0) for other in others] + neighbours)
    normalize_rows(hidden_ref, gain_ref, normed)
    own = pltpu.make_async_copy(
        normed.at[:, span(me, depth)], slots.at[place, span(me, rows)], own_sem
    )
    own.start()
    pl.semaphore_wait(pltpu.get_barrier_semaphore(), greeted)

    swaps = [
        pltpu.make_async_remote_copy(
            src_ref=normed.at[:, span(other, depth)],
            dst_ref=slots.at[place, span(me, rows)],
            send_sem=swap_send.at[k],
            recv_sem=swap_recv.at[parts - 2 - k],
            device_id={"ctx": other},
            device_id_type=MESH,
        )
        for k, other in enumerate(others)
    ]
    for swap in swaps:
        swap.start()
    line = Line(
        shards, parts, lambda origin, c: slots.at[origin, span(c, rows)], line_send, line_recv
    )
    own.wait()
    line.send(place, me, 0)
    line.send(place, me, 1)

    first[...] = first_rows(taps_ref, decay_ref)

    @pl.when(me == 0)
    def _():
        padding = jnp.zeros((taps - tail_ref.shape[0], channels), jnp.float32)
        before[...] = jnp.concatenate(
            [padding, tail_ref[...].astype(jnp.float32)], axis=0
        ).astype(jnp.bfloat16)

    for k in range(parts - 1):
        swaps[parts - 2 - k].wait_recv()
        line.send(place, others[k], 0)
        line.send(place, others[k], 1)

    def write_band(group, carry):
        row = jnp.broadcast_to(first[pl.ds(group, 1), :], (taps, 2 * taps))
        bands[group] = pltpu.roll(row, 0, 1, stride=1, stride_axis=0).astype(jnp.bfloat16)
        return carry

    lax.fori_loop(0, groups, write_band, 0)
    for load in loads:
        load.wait()

    tiles = channels // tile

    def project(origin, k):
        def step(index, carry):
            g, column = lax.rem(index // tiles + 1, 3), lax.rem(index, tiles)
            where = span(column, tile)
            partial[g, origin, :, where] = jnp.dot(
                slots[origin], planes[g, :, where], preferred_element_type=jnp.float32
            ).astype(jnp.bfloat16)

            @pl.when(column == tiles - 1)
            def _():
                for k, other in enumerate(others):
                    pltpu.make_async_remote_copy(
                        src_ref=partial.at[g, origin, span(other, rows)],
                        dst_ref=arrived.at[g, parts - 2 - k, span(origin, rows)],
                        send_sem=sum_send,
                        recv_sem=sum_recv.at[g],
                        device_id={"ctx": other},
                        device_id_type=MESH,
                    ).start()

            return carry

        steps = 3 * tiles
        lax.fori_loop(k * steps // parts, (k + 1) * steps // parts, step, 0)

    def project_from(distance, k):
        below, above = place - distance, place + distance

        @pl.when(line.inside(below))
        def _():
            project(jnp.maximum(below, 0), k)

        @pl.when(line.inside(above) & (distance > 0))
        def _():
            project(jnp.minimum(above, shards - 1), k)

    def project_piece(origin, piece):
        mine = span(piece, rows)

        def plane(step, carry):
            g = lax.rem(step + 1, 3)

            def columns(column, inner):
                where = span(column, tile)
                partial[g, origin, mine, where] = jnp.dot(
                    slots[origin, mine], planes[g, :, where], preferred_element_type=jnp.float32
                ).astype(jnp.bfloat16)
                return inner

            lax.fori_loop(0, tiles, columns, 0)

            @pl.when(piece != me)
            def _():
                slot = jnp.clip(lax.rem(me - piece - 1 + parts, parts), 0, parts - 2)
                pltpu.make_async_remote_copy(
                    src_ref=partial.at[g, origin, mine],
                    dst_ref=arrived.at[g, slot, span(origin, rows)],
                    send_sem=sum_send,
                    recv_sem=sum_recv.at[g],
                    device_id={"ctx": piece},
                    device_id_type=MESH,
                ).start()

            return carry

        lax.fori_loop(0, 3, plane, 0)

    def stage(index, carry):
        distance, k = index // parts, lax.rem(index, parts)
        project_from(distance, k)
        piece = lax.rem(me + k, parts)
        line.pass_on(distance + 1, piece, 1)
        line.pass_on(distance + 1, piece, 0)

        @pl.when((distance == shards - 2) & ((place == 0) | (place == shards - 1)))
        def _():
            project_piece(shards - 1 - place, piece)

        return carry

    lax.fori_loop(0, (shards - 1) * parts, stage, 0)

    def summed(g, origin, where=slice(None)):
        value = partial[g, origin, span(me, rows), where].astype(jnp.float32)
        for k in range(parts - 1):
            value = value + arrived[g, k, span(origin, rows), where].astype(jnp.float32)
        return value

    for g in (1, 2):
        pltpu.make_async_copy(arrived.at[g], arrived.at[g], sum_recv.at[g]).wait()

    def write_product(step, carry):
        origin = shards - 1 - step
        product[span(origin, rows), :] = (summed(1, origin) * summed(2, origin)).astype(
            jnp.bfloat16
        )
        return carry

    tail_steps = -(-taps // rows)
    lax.fori_loop(0, tail_steps, write_product, 0)
    tail = pltpu.make_async_remote_copy(
        src_ref=product.at[pl.ds(all_rows - taps, taps)],
        dst_ref=before,
        send_sem=tail_send,
        recv_sem=tail_recv,
        device_id={"ctx": jnp.minimum(me + 1, parts - 1)},
        device_id_type=MESH,
    )

    @pl.when(me + 1 < parts)
    def _():
        tail.start()

    lax.fori_loop(tail_steps, shards, write_product, 0)
    @pl.when(me > 0)
    def _():
        tail.wait_recv()

    per, windows_count = LANES // GROUP, all_rows // taps

    def filter_lanes(block, carry):
        where = span(block, LANES)
        extended = jnp.concatenate([before[:, where], product[:, where]], axis=0)
        windows = jnp.concatenate(
            [extended[b * taps : (b + 2) * taps] for b in range(windows_count)], axis=1
        )
        lane = lax.broadcasted_iota(jnp.int32, windows.shape, 1)
        owner = lax.rem(lane, LANES) // GROUP
        sums = jnp.zeros((taps, windows_count * LANES), jnp.float32)
        for group in range(per):
            mine = jnp.where(owner == group, windows, jnp.zeros_like(windows))
            sums = sums + jnp.dot(
                bands[block * per + group], mine, preferred_element_type=jnp.float32
            )
        for b in range(windows_count):
            inner = pl.ds(b * taps, taps)
            direct = skip_ref[:, where] * product[inner, where].astype(jnp.float32)
            filtered[inner, where] = sums[:, b * LANES : (b + 1) * LANES] + direct
        return carry

    lax.fori_loop(0, channels // LANES, filter_lanes, 0)
    pltpu.make_async_copy(arrived.at[0], arrived.at[0], sum_recv.at[0]).wait()

    gated_line = Line(
        shards, chunks, lambda origin, c: gated.at[origin, c], gated_send, gated_recv
    )

    def gate_chunk(c, carry):
        where = span(c, chunk)

        def gate(origin, inner):
            mine = span(origin, rows)
            gated[place, c, mine, :] = (
                summed(0, origin, where) * filtered[mine, where]
            ).astype(jnp.bfloat16)
            return inner

        lax.fori_loop(0, shards, gate, 0)
        gated_line.send(place, c, 0)
        gated_line.send(place, c, 1)
        return carry

    lax.fori_loop(0, chunks, gate_chunk, 0)
    last_load.wait()
    wide = min(512, columns)

    def multiply(origin, c, fresh):
        deep = span(origin * chunks + c, chunk)

        def column(index, carry):
            where = span(index, wide)
            value = jnp.dot(
                gated[origin, c], weight[deep, where], preferred_element_type=jnp.float32
            )
            total[:, where] = value if fresh else total[:, where] + value
            return carry

        lax.fori_loop(0, columns // wide, column, 0)

    multiply(place, 0, True)

    def multiply_own(c, carry):
        multiply(place, c, False)
        return carry

    lax.fori_loop(1, chunks, multiply_own, 0)
    first_up = jnp.where(2 * place >= shards, 1, 0)

    def collect(index, carry):
        distance, side = index // (2 * chunks) + 1, lax.rem(index // chunks, 2)
        c = lax.rem(index, chunks)
        up = lax.rem(first_up + side, 2)
        gated_line.pass_on(distance, c, up)
        origin = place - distance * (2 * up - 1)

        @pl.when(gated_line.inside(origin))
        def _():
            multiply(jnp.clip(origin, 0, shards - 1), c, False)

        return carry

    lax.fori_loop(0, 2 * chunks * (shards - 1), collect, 0)
    out_ref[...] = total[...].astype(jnp.bfloat16)

    for swap in swaps:
        swap.wait_send()

    @pl.when(me + 1 < parts)
    def _():
        tail.wait_send()

    line.sent()
    gated_line.sent()
    pltpu.make_async_copy(arrived, arrived, sum_send).wait()


def paired_kernel(
    shards,
    hidden_in,
    gain_in,
    planes_ref,
    taps_in,
    decay_in,
    skip_in,
    tail_in,
    weight_ref,
    total,
    hidden_ref,
    gain_ref,
    taps_ref,
    decay_ref,
    skip_ref,
    tail_ref,
    normed,
    first,
    planes,
    slots,
    mine,
    outgoing,
    arrived,
    extended,
    filtered,
    bands,
    weight,
    gated,
    handed,
    input_sem,
    load_sem,
    own_sem,
    planes_send,
    planes_recv,
    swap_send,
    line_send,
    line_recv,
    pair_send,
    pair_recv,
    sum_send,
    sum_recv,
    tail_send,
    tail_recv,
    hand_send,
    hand_recv,
    gated_send,
    gated_recv,
):
    rows = hidden_ref.shape[0]
    parts = slots.shape[1] // rows
    _, both_depths, half = planes.shape
    depth = both_depths // 2
    _, taps, _ = bands.shape
    chunks, all_rows, chunk = gated.shape[1:]
    columns = total.shape[1]
    tile = min(256, half)
    tiles = half // tile
    me, place = lax.axis_index("ctx"), lax.axis_index("tensor")
    pair, core = me // 2, lax.rem(me, 2)
    across = 1 - pair
    sibling, peer = 2 * pair + 1 - core, 2 * across + core

    others = [lax.rem(me + 1 + k, parts) for k in range(parts - 1)]
    neighbours = [
        ("tensor", jnp.maximum(place - 1, 0), place > 0),
        ("tensor", jnp.minimum(place + 1, shards - 1), place < shards - 1),
    ]
    greeted = greet([("ctx", other, me >= 0) for other in others] + neighbours)
    inputs = [
        pltpu.make_async_copy(source, target, input_sem.at[k])
        for k, (source, target) in enumerate(
            [
                (hidden_in, hidden_ref),
                (gain_in, gain_ref),
                (taps_in, taps_ref),
                (decay_in, decay_ref),
                (skip_in, skip_ref),
                (tail_in, tail_ref),
            ]
        )
    ]
    for load in inputs:
        load.start()
    loads = [
        pltpu.make_async_copy(
            planes_ref.at[g, :, span(core, half)], planes.at[g, span(core, depth)], load_sem.at[g]
        )
        for g in (1, 2, 0)
    ]
    for load in loads:
        load.start()
    last_load = pltpu.make_async_copy(weight_ref, weight, load_sem.at[3])
    for load in inputs[:2]:
        load.wait()
    normalize_rows(hidden_ref, gain_ref, normed)
    mine_in = normed.at[:, span(pair, both_depths)]
    own = pltpu.make_async_copy(mine_in, slots.at[place, span(me, rows)], own_sem)
    own.start()
    pl.semaphore_wait(pltpu.get_barrier_semaphore(), greeted)

    def remote(source, target, send, recv, **device):
        return pltpu.make_async_remote_copy(
            src_ref=source,
            dst_ref=target,
            send_sem=send,
            recv_sem=recv,
            device_id=device,
            device_id_type=MESH,
        )

    line = Line(
        shards,
        parts,
        lambda origin, c: slots.at[origin, span(c, rows), span(core, depth)],
        line_send,
        line_recv,
    )
    line.send(place, me, 0, normed.at[:, span(me, depth)])
    line.send(place, me, 1, normed.at[:, span(me, depth)])
    to_sibling = remote(
        mine_in, slots.at[place, span(me, rows)], pair_send, pair_recv.at[place, me], ctx=sibling
    )
    to_sibling.start()
    swaps = [
        remote(
            normed.at[:, span(2 * across + k, depth)],
            slots.at[place, span(me, rows), pl.ds(k * depth, depth)],
            swap_send.at[k],
            line_recv.at[place, me],
            ctx=2 * across + k,
        )
        for k in range(2)
    ]
    swaps[0].start()
    shares = [
        remote(
            planes_ref.at[g, :, span(1 - core, half)],
            planes.at[g, span(core, depth)],
            planes_send,
            planes_recv.at[g],
            ctx=sibling,
        )
        for g in (1, 2, 0)
    ]
    for share in shares:
        share.start()

    def share_piece(origin, c):
        ref = slots.at[origin, span(c, rows), span(core, depth)]
        return remote(ref, ref, pair_send, pair_recv.at[origin, c], ctx=sibling)

    def from_sibling(origin, c):
        ref = slots.at[origin, span(c, rows), span(1 - core, depth)]
        return remote(ref, ref, pair_send, pair_recv.at[origin, c], ctx=sibling)

    for load in inputs[2:]:
        load.wait()
    first[...] = first_rows(taps_ref, decay_ref)

    @pl.when(pair == 0)
    def _():
        padding = jnp.zeros((taps - tail_ref.shape[0], half), jnp.float32)
        extended[pl.ds(0, taps), :] = jnp.concatenate(
            [padding, tail_ref[:, span(core, half)].astype(jnp.float32)], axis=0
        ).astype(jnp.bfloat16)

    remote(
        mine_in,
        slots.at[place, span(sibling, rows)],
        pair_send,
        pair_recv.at[place, sibling],
        ctx=sibling,
    ).wait_recv()
    line.send(place, sibling, 0)
    line.send(place, sibling, 1)

    def write_band(group, carry):
        row = jnp.broadcast_to(first[pl.ds(core * (half // GROUP) + group, 1), :], (taps, 2 * taps))
        bands[group] = pltpu.roll(row, 0, 1, stride=1, stride_axis=0).astype(jnp.bfloat16)
        return carry

    lax.fori_loop(0, half // GROUP, write_band, 0)
    swaps[0].wait_send()
    swaps[1].start()
    for k in range(2):
        c = 2 * across + k
        line.hop(place, c, 1).wait_recv()
        line.send(place, c, 0)
        line.send(place, c, 1)
        share_piece(place, c).start()
    own.wait()
    for load in loads:
        load.wait()
    for share in shares:
        share.wait_recv()
    last_load.start()

    def sum_piece(g, origin):
        where = span(origin, rows)
        return remote(
            outgoing.at[g, :, where],
            arrived.at[g, :, where],
            sum_send,
            sum_recv.at[g, origin],
            ctx=peer,
        )

    def group_of(far):
        return jnp.where(far == 1, across, pair)

    def project(origin, far):
        tokens = span(group_of(far), 2 * rows)

        def step(index, carry):
            g, column = lax.rem(index // tiles + 1, 3), lax.rem(index, tiles)
            where = span(column, tile)
            value = jnp.dot(
                slots[origin, tokens], planes[g, :, where], preferred_element_type=jnp.float32
            )

            def keep(target):
                for k in range(2):
                    target[g, k, span(origin, rows), where] = value[
                        k * rows : (k + 1) * rows
                    ].astype(target.dtype)

            @pl.when(far == 0)
            def _():
                keep(mine)

            @pl.when(far == 1)
            def _():
                keep(outgoing)

            @pl.when((far == 1) & (column == tiles - 1))
            def _():
                sum_piece(g, origin).start()

            return carry

        lax.fori_loop(0, 3 * tiles, step, 0)

    def combine(origin):
        where = span(origin, rows)
        for g in (1, 2, 0):
            sum_piece(g, origin).wait_recv()
        for k in range(2):
            q, key, value = [
                mine[g, k, where] + arrived[g, k, where].astype(jnp.float32) for g in range(3)
            ]
            mine[0, k, where] = q
            start = pl.multiple_of(taps + k * all_rows + origin * rows, rows)
            extended[pl.ds(start, rows), :] = (key * value).astype(jnp.bfloat16)

    def beside(distance, work):
        for origin in (place - distance, place + distance):

            @pl.when(line.inside(origin))
            def _(origin=origin):
                work(jnp.clip(origin, 0, shards - 1))

    def project_own(far, carry):
        @pl.when(far == 1)
        def _():
            for k in range(2):
                from_sibling(place, 2 * across + k).wait_recv()

        project(place, far)
        return carry

    lax.fori_loop(0, 2, project_own, 0)

    def from_side(distance, up):
        origin = place - distance * (2 * up - 1)
        return line.inside(origin), jnp.clip(origin, 0, shards - 1), origin == (1 - up) * (shards - 1)

    def far_at(distance, turn, last):
        return jnp.where(last & (distance > 1), 1 - turn, turn)

    def flow(distance, turn, up):
        there, origin, last = from_side(distance, up)
        held = last & (distance == 1)

        @pl.when(there)
        def _():
            group = group_of(far_at(distance, turn, last))
            for k in range(2):
                line.hop(origin, 2 * group + k, up).wait_recv()

                @pl.when(~held | (turn == 1))
                def _(k=k):
                    usual = jnp.where(held, pair, group_of(turn))
                    line.follow(origin, 2 * group + k, up, 2 * usual + k)

                share_piece(origin, 2 * group + k).start()

            @pl.when(held & (turn == 1))
            def _():
                for k in range(2):
                    line.follow(origin, 2 * pair + k, up, 2 * across + k)

    def project_side(distance, turn, up):
        there, origin, last = from_side(distance, up)

        @pl.when(there)
        def _():
            far = far_at(distance, turn, last)
            for k in range(2):
                from_sibling(origin, 2 * group_of(far) + k).wait_recv()
            project(origin, far)

    def stage(distance, carry):
        def half_stage(turn, inner):
            flow(distance, turn, 1)
            flow(distance, turn, 0)

            def side(up, nothing):
                project_side(distance, turn, up)
                return nothing

            lax.fori_loop(0, 2, side, 0)
            return inner

        lax.fori_loop(0, 2, half_stage, 0)

        @pl.when(distance == 1)
        def _():
            combine(place)

        @pl.when(distance > 1)
        def _():
            beside(distance - 1, combine)

        return carry

    lax.fori_loop(1, shards, stage, 0)
    beside(shards - 1, combine)
    before = extended.at[pl.ds(0, taps)]
    tail = remote(
        extended.at[pl.ds(2 * all_rows, taps)], before, tail_send, tail_recv, ctx=peer
    )

    @pl.when(pair == 0)
    def _():
        tail.start()

    per, windows_count = LANES // GROUP, all_rows // taps

    def filter_lanes(k, block):
        where = span(block, LANES)
        values = extended[pl.ds(k * all_rows, taps + all_rows), where]
        windows = jnp.concatenate(
            [values[b * taps : (b + 2) * taps] for b in range(windows_count)], axis=1
        )
        lane = lax.broadcasted_iota(jnp.int32, windows.shape, 1)
        owner = lax.rem(lane, LANES) // GROUP
        sums = jnp.zeros((taps, windows_count * LANES), jnp.float32)
        for group in range(per):
            some = jnp.where(owner == group, windows, jnp.zeros_like(windows))
            sums = sums + jnp.dot(
                bands[block * per + group], some, preferred_element_type=jnp.float32
            )
        skip = skip_ref[:, pl.ds(pl.multiple_of(core * half + block * LANES, LANES), LANES)]
        for b in range(windows_count):
            direct = skip * values[(b + 1) * taps : (b + 2) * taps].astype(jnp.float32)
            filtered[pl.ds(b * taps, taps), where] = sums[:, b * LANES : (b + 1) * LANES] + direct

    gated_line = Line(
        shards, chunks, lambda origin, c: gated.at[origin, c], gated_send, gated_recv
    )
    mine_chunks = half // chunk

    def hand(i, owner):
        c = owner * mine_chunks + i
        return remote(handed.at[i], gated.at[place, c], hand_send, hand_recv.at[i], ctx=sibling)

    inner_place = (place > 0) & (place < shards - 1)

    outward = jnp.where(2 * place >= shards, 1, 0)

    def send_gated(c):
        gated_line.send(place, c, 1 - outward)

        @pl.when(~inner_place)
        def _():
            gated_line.send(place, c, outward)

    def gate_half(step, carry):
        k = 1 - step

        @pl.when((k == 0) & (pair == 1))
        def _():
            tail.wait_recv()

        def gate_chunk(i, inner):
            def lanes(block, nothing):
                filter_lanes(k, block)
                return nothing

            per_chunk = chunk // LANES
            lax.fori_loop(i * per_chunk, (i + 1) * per_chunk, lanes, 0)
            where, c = span(i, chunk), core * mine_chunks + i
            value = (mine[0, k, :, where] * filtered[:, where]).astype(jnp.bfloat16)

            @pl.when(k == core)
            def _():
                gated[place, c] = value
                send_gated(c)

            @pl.when(k != core)
            def _():
                handed[i] = value
                hand(i, core).start()

            return inner

        lax.fori_loop(0, mine_chunks, gate_chunk, 0)
        return carry

    lax.fori_loop(0, 2, gate_half, 0)

    def take(i, carry):
        hand(i, 1 - core).wait_recv()
        send_gated((1 - core) * mine_chunks + i)
        return carry

    lax.fori_loop(0, mine_chunks, take, 0)
    line.last_sent()

    @pl.when(inner_place)
    def _():
        for i in range(chunks):
            gated_line.send(place, lax.rem(core * mine_chunks + i, chunks), outward)

    last_load.wait()
    wide = min(512, columns)

    def multiply(origin, c, fresh=False):
        deep = span(origin * chunks + c, chunk)
        for start in range(0, columns, wide):
            where = pl.ds(start, wide)
            value = jnp.dot(
                gated[origin, c], weight[deep, where], preferred_element_type=jnp.float32
            )
            total[:, where] = value if fresh else total[:, where] + value

    multiply(place, 0, True)

    def multiply_own(c, carry):
        multiply(place, c)
        return carry

    lax.fori_loop(1, chunks, multiply_own, 0)
    def collect(index, carry):
        distance, side = index // (2 * chunks) + 1, lax.rem(index // chunks, 2)
        step = lax.rem(index, chunks)
        c = lax.rem(step + core * mine_chunks, chunks)
        up = lax.rem(outward + side, 2)
        origin = place - distance * (2 * up - 1)

        @pl.when(gated_line.inside(origin))
        def _():
            source = jnp.clip(origin, 0, shards - 1)
            gated_line.hop(source, c, up).wait_recv()
            gated_line.follow(source, c, up, c)


        @pl.when(gated_line.inside(origin))
        def _():
            multiply(jnp.clip(origin, 0, shards - 1), c)

        return carry

    lax.fori_loop(0, 2 * chunks * (shards - 1), collect, 0)

    swaps[1].wait_send()

    @pl.when(pair == 0)
    def _():
        tail.wait_send()

    gated_line.last_sent()
    slices = slots.at[:, :, pl.ds(0, depth)]
    pltpu.make_async_copy(slices, slices, pair_send).wait()
    pltpu.make_async_copy(handed, handed, hand_send).wait()
    pltpu.make_async_copy(outgoing, outgoing, sum_send).wait()
    sent_planes = planes.at[:, pl.ds(0, depth)]
    pltpu.make_async_copy(sent_planes, sent_planes, planes_send).wait()


def on_paired_device(
    hidden_in, norm_gain, weight_in, filter_taps, filter_decay, skip_gain, tail_cache, output_weight
):
    shards, parts = lax.axis_size("tensor"), lax.axis_size("ctx")
    rows = hidden_in.shape[0]
    depth, _, channels = weight_in.shape
    groups, taps = filter_taps.shape
    columns = output_weight.shape[1]
    all_rows = shards * rows
    half = channels // 2
    chunk = min(256, half)
    chunks = channels // chunk
    anywhere = pl.BlockSpec(memory_space=pl.ANY)
    dma = pltpu.SemaphoreType.DMA
    bf16, f32 = jnp.bfloat16, jnp.float32
    total = pl.pallas_call(
        functools.partial(paired_kernel, shards),
        out_shape=pltpu.VMEM((all_rows, columns), f32),
        in_specs=[anywhere] * 8,
        out_specs=pl.BlockSpec(memory_space=pltpu.VMEM),
        scratch_shapes=[
            pltpu.VMEM(hidden_in.shape, bf16),
            pltpu.VMEM((1, norm_gain.shape[0]), f32),
            pltpu.VMEM(filter_taps.shape, f32),
            pltpu.VMEM((1, groups), f32),
            pltpu.VMEM((1, channels), f32),
            pltpu.VMEM(tail_cache.shape, bf16),
            pltpu.VMEM((rows, hidden_in.shape[1]), bf16),
            pltpu.VMEM((groups, 2 * taps), f32),
            pltpu.VMEM((3, 2 * depth, half), bf16),
            pltpu.VMEM((shards, parts * rows, 2 * depth), bf16),
            pltpu.VMEM((3, 2, all_rows, half), f32),
            pltpu.VMEM((3, 2, all_rows, half), bf16),
            pltpu.VMEM((3, 2, all_rows, half), bf16),
            pltpu.VMEM((taps + 2 * all_rows, half), bf16),
            pltpu.VMEM((all_rows, half), f32),
            pltpu.VMEM((groups // 2, taps, 2 * taps), bf16),
            pltpu.VMEM(output_weight.shape, bf16),
            pltpu.VMEM((shards, chunks, all_rows, chunk), bf16),
            pltpu.VMEM((chunks // 2, all_rows, chunk), bf16),
            dma((6,)),
            dma((4,)),
            dma,
            dma,
            dma((3,)),
            dma((2,)),
            dma((2, shards, parts)),
            dma((shards, parts)),
            dma,
            dma((shards, parts)),
            dma,
            dma((3, shards)),
            dma,
            dma,
            dma,
            dma((chunks // 2,)),
            dma((2, shards, chunks)),
            dma((shards, chunks)),
        ],
        compiler_params=pltpu.CompilerParams(
            collective_id=0, has_side_effects=True, vmem_limit_bytes=54 << 20
        ),
    )(
        hidden_in,
        norm_gain.reshape(1, norm_gain.shape[0]),
        weight_in.transpose(1, 0, 2),
        filter_taps,
        filter_decay.reshape(1, groups),
        skip_gain.reshape(1, channels),
        tail_cache,
        output_weight,
    )
    return total.astype(bf16)


def on_device(
    hidden_in, norm_gain, weight_in, filter_taps, filter_decay, skip_gain, tail_cache, output_weight
):
    shards, parts = lax.axis_size("tensor"), lax.axis_size("ctx")
    rows = hidden_in.shape[0]
    depth, _, channels = weight_in.shape
    groups, taps = filter_taps.shape
    columns = output_weight.shape[1]
    all_rows = shards * rows
    chunk = min(256, channels)
    chunks = channels // chunk
    vmem, anywhere = pl.BlockSpec(memory_space=pltpu.VMEM), pl.BlockSpec(memory_space=pl.ANY)
    dma = pltpu.SemaphoreType.DMA
    bf16, f32 = jnp.bfloat16, jnp.float32
    return pl.pallas_call(
        functools.partial(mixer_kernel, shards, parts),
        out_shape=jax.ShapeDtypeStruct((all_rows, columns), bf16),
        in_specs=[vmem, vmem, anywhere, vmem, vmem, vmem, vmem, anywhere],
        out_specs=vmem,
        scratch_shapes=[
            pltpu.VMEM((rows, hidden_in.shape[1]), bf16),
            pltpu.VMEM((groups, 2 * taps), f32),
            pltpu.VMEM((3, depth, channels), bf16),
            pltpu.VMEM((shards, parts * rows, depth), bf16),
            pltpu.VMEM((3, shards, parts * rows, channels), bf16),
            pltpu.VMEM((3, parts - 1, all_rows, channels), bf16),
            pltpu.VMEM((all_rows, channels), f32),
            pltpu.VMEM((all_rows, channels), bf16),
            pltpu.VMEM((taps, channels), bf16),
            pltpu.VMEM((groups, taps, 2 * taps), bf16),
            pltpu.VMEM(output_weight.shape, bf16),
            pltpu.VMEM((shards, chunks, all_rows, chunk), bf16),
            pltpu.VMEM((all_rows, columns), f32),
            dma((4,)),
            dma,
            dma((parts - 1,)),
            dma((parts - 1,)),
            dma((2, shards, parts)),
            dma((shards, parts)),
            dma,
            dma((3,)),
            dma,
            dma,
            dma((2, shards, chunks)),
            dma((shards, chunks)),
        ],
        compiler_params=pltpu.CompilerParams(
            collective_id=0, has_side_effects=True, vmem_limit_bytes=56 << 20
        ),
    )(
        hidden_in,
        norm_gain.reshape(1, norm_gain.shape[0]),
        weight_in.transpose(1, 0, 2),
        filter_taps,
        filter_decay.reshape(1, groups),
        skip_gain.reshape(1, channels),
        tail_cache,
        output_weight,
    )


def solution(mesh):
    in_specs = (
        P(("prompt", "ctx", "tensor"), None),
        P(),
        P("ctx", None, "tensor"),
        P("tensor", None),
        P("tensor"),
        P("tensor"),
        P("prompt", "tensor"),
        P(None, "tensor"),
    )
    out_specs = P(("prompt", "ctx"), "tensor")
    paired = mesh.shape["ctx"] == 4 and mesh.shape["tensor"] > 1
    return jax.shard_map(
        on_paired_device if paired else on_device, mesh=mesh, in_specs=in_specs, out_specs=out_specs, check_vma=False
    )
```

```python
import functools

import jax
import jax.numpy as jnp
from jax import lax
from jax.experimental import pallas as pl
from jax.experimental.pallas import tpu as pltpu
from jax.sharding import PartitionSpec as P

GROUP = 16
LANES = 128
MESH = pl.DeviceIdType.MESH


def span(index, size):
    return pl.ds(pl.multiple_of(index * size, size), size)


def greet(peers):
    barrier = pltpu.get_barrier_semaphore()
    for axis, peer, there in peers:

        @pl.when(there)
        def _(axis=axis, peer=peer):
            pl.semaphore_signal(barrier, inc=1, device_id={axis: peer}, device_id_type=MESH)

    return sum(jnp.where(there, 1, 0) for _, _, there in peers)


def normalize_rows(hidden_ref, gain_ref, normed):
    rows, width = hidden_ref.shape
    few, part = min(16, rows), 1024

    def step(index, carry):
        where = span(index, few)

        def values(start):
            return hidden_ref[where, pl.ds(start, part)].astype(jnp.float32)

        squares = jnp.zeros((few, part), jnp.float32)
        for start in range(0, width, part):
            squares = squares + values(start) * values(start)
        scaled = lax.rsqrt(jnp.sum(squares, axis=-1, keepdims=True) / width + 1e-06)
        for start in range(0, width, part):
            inner = pl.ds(start, part)
            normed[where, inner] = (values(start) * scaled * gain_ref[:, inner]).astype(
                jnp.bfloat16
            )
        return carry

    lax.fori_loop(0, rows // few, step, 0)


def first_rows(taps_ref, decay_ref):
    groups, taps = taps_ref.shape
    lags = lax.broadcasted_iota(jnp.int32, (groups, taps), 1).astype(jnp.float32)
    across = lax.broadcasted_iota(jnp.int32, (groups, groups), 1)
    down = lax.broadcasted_iota(jnp.int32, (groups, groups), 0)
    decay = jnp.sum(jnp.where(across == down, decay_ref[...], 0.0), axis=1, keepdims=True)
    taps_full = (taps_ref[...] * jnp.exp(-decay * lags)).astype(jnp.bfloat16)
    lag = lax.broadcasted_iota(jnp.int32, (taps, 2 * taps), 0)
    column = lax.broadcasted_iota(jnp.int32, (taps, 2 * taps), 1)
    turned = jnp.where(lag + column == taps, 1.0, 0.0).astype(jnp.bfloat16)
    return jnp.dot(taps_full, turned, preferred_element_type=jnp.float32)


class Line:
    def __init__(self, count, pieces, view, send_sem, recv_sem):
        self.count, self.pieces, self.view = count, pieces, view
        self.send_sem, self.recv_sem = send_sem, recv_sem
        self.place = lax.axis_index("tensor")

    def inside(self, position):
        return (position >= 0) & (position < self.count)

    def hop(self, origin, piece, up, source=None):
        ref = self.view(origin, piece)
        return pltpu.make_async_remote_copy(
            src_ref=ref if source is None else source,
            dst_ref=ref,
            send_sem=self.send_sem.at[up, origin, piece],
            recv_sem=self.recv_sem.at[origin, piece],
            device_id={"tensor": jnp.clip(self.place + 2 * up - 1, 0, self.count - 1)},
            device_id_type=MESH,
        )

    def send(self, origin, piece, up, source=None):
        @pl.when(self.inside(self.place + 2 * up - 1))
        def _():
            self.hop(origin, piece, up, source).start()

    def pass_on(self, distance, piece, up):
        origin = self.place - distance * (2 * up - 1)

        @pl.when(self.inside(origin))
        def _():
            source = jnp.clip(origin, 0, self.count - 1)
            self.hop(source, piece, up).wait_recv()
            self.send(source, piece, up)

    def follow(self, origin, piece, up, before):
        @pl.when(self.inside(self.place + 2 * up - 1))
        def _():
            self.hop(jnp.clip(origin + 2 * up - 1, 0, self.count - 1), before, up).wait_send()
            self.hop(origin, piece, up).start()

    def last_sent(self):
        for up in (0, 1):

            @pl.when(self.inside(self.place + 2 * up - 1))
            def _(up=up):
                def step(piece, carry):
                    self.hop((1 - up) * (self.count - 1), piece, up).wait_send()
                    return carry

                lax.fori_loop(0, self.pieces, step, 0)

    def sent(self):
        def step(index, carry):
            origin, piece = index // self.pieces, lax.rem(index, self.pieces)

            @pl.when((origin <= self.place) & (self.place + 1 < self.count))
            def _():
                self.hop(origin, piece, 1).wait_send()

            @pl.when((origin >= self.place) & (self.place > 0))
            def _():
                self.hop(origin, piece, 0).wait_send()

            return carry

        lax.fori_loop(0, self.count * self.pieces, step, 0)


def mixer_kernel(
    shards,
    parts,
    hidden_ref,
    gain_ref,
    planes_ref,
    taps_ref,
    decay_ref,
    skip_ref,
    tail_ref,
    weight_ref,
    out_ref,
    normed,
    first,
    planes,
    slots,
    partial,
    arrived,
    filtered,
    product,
    before,
    bands,
    weight,
    gated,
    total,
    load_sem,
    own_sem,
    swap_send,
    swap_recv,
    line_send,
    line_recv,
    sum_send,
    sum_recv,
    tail_send,
    tail_recv,
    gated_send,
    gated_recv,
):
    rows = hidden_ref.shape[0]
    _, depth, channels = planes.shape
    groups, taps, _ = bands.shape
    chunks, all_rows, chunk = gated.shape[1:]
    columns = out_ref.shape[1]
    tile = min(256, channels)
    me, place = lax.axis_index("ctx"), lax.axis_index("tensor")
    others = [lax.rem(me + 1 + k, parts) for k in range(parts - 1)]

    loads = [
        pltpu.make_async_copy(planes_ref.at[g], planes.at[g], load_sem.at[g]) for g in (1, 2, 0)
    ]
    for load in loads:
        load.start()
    last_load = pltpu.make_async_copy(weight_ref, weight, load_sem.at[3])
    last_load.start()
    neighbours = [
        ("tensor", jnp.maximum(place - 1, 0), place > 0),
        ("tensor", jnp.minimum(place + 1, shards - 1), place < shards - 1),
    ]
    greeted = greet([("ctx", other, me >= 0) for other in others] + neighbours)
    normalize_rows(hidden_ref, gain_ref, normed)
    own = pltpu.make_async_copy(
        normed.at[:, span(me, depth)], slots.at[place, span(me, rows)], own_sem
    )
    own.start()
    pl.semaphore_wait(pltpu.get_barrier_semaphore(), greeted)

    swaps = [
        pltpu.make_async_remote_copy(
            src_ref=normed.at[:, span(other, depth)],
            dst_ref=slots.at[place, span(me, rows)],
            send_sem=swap_send.at[k],
            recv_sem=swap_recv.at[parts - 2 - k],
            device_id={"ctx": other},
            device_id_type=MESH,
        )
        for k, other in enumerate(others)
    ]
    for swap in swaps:
        swap.start()
    line = Line(
        shards, parts, lambda origin, c: slots.at[origin, span(c, rows)], line_send, line_recv
    )
    own.wait()
    line.send(place, me, 0)
    line.send(place, me, 1)

    first[...] = first_rows(taps_ref, decay_ref)

    @pl.when(me == 0)
    def _():
        padding = jnp.zeros((taps - tail_ref.shape[0], channels), jnp.float32)
        before[...] = jnp.concatenate(
            [padding, tail_ref[...].astype(jnp.float32)], axis=0
        ).astype(jnp.bfloat16)

    for k in range(parts - 1):
        swaps[parts - 2 - k].wait_recv()
        line.send(place, others[k], 0)
        line.send(place, others[k], 1)

    def write_band(group, carry):
        row = jnp.broadcast_to(first[pl.ds(group, 1), :], (taps, 2 * taps))
        bands[group] = pltpu.roll(row, 0, 1, stride=1, stride_axis=0).astype(jnp.bfloat16)
        return carry

    lax.fori_loop(0, groups, write_band, 0)
    for load in loads:
        load.wait()

    tiles = channels // tile

    def project(origin, k):
        def step(index, carry):
            g, column = lax.rem(index // tiles + 1, 3), lax.rem(index, tiles)
            where = span(column, tile)
            partial[g, origin, :, where] = jnp.dot(
                slots[origin], planes[g, :, where], preferred_element_type=jnp.float32
            ).astype(jnp.bfloat16)

            @pl.when(column == tiles - 1)
            def _():
                for k, other in enumerate(others):
                    pltpu.make_async_remote_copy(
                        src_ref=partial.at[g, origin, span(other, rows)],
                        dst_ref=arrived.at[g, parts - 2 - k, span(origin, rows)],
                        send_sem=sum_send,
                        recv_sem=sum_recv.at[g],
                        device_id={"ctx": other},
                        device_id_type=MESH,
                    ).start()

            return carry

        steps = 3 * tiles
        lax.fori_loop(k * steps // parts, (k + 1) * steps // parts, step, 0)

    def project_from(distance, k):
        below, above = place - distance, place + distance

        @pl.when(line.inside(below))
        def _():
            project(jnp.maximum(below, 0), k)

        @pl.when(line.inside(above) & (distance > 0))
        def _():
            project(jnp.minimum(above, shards - 1), k)

    def project_piece(origin, piece):
        mine = span(piece, rows)

        def plane(step, carry):
            g = lax.rem(step + 1, 3)

            def columns(column, inner):
                where = span(column, tile)
                partial[g, origin, mine, where] = jnp.dot(
                    slots[origin, mine], planes[g, :, where], preferred_element_type=jnp.float32
                ).astype(jnp.bfloat16)
                return inner

            lax.fori_loop(0, tiles, columns, 0)

            @pl.when(piece != me)
            def _():
                slot = jnp.clip(lax.rem(me - piece - 1 + parts, parts), 0, parts - 2)
                pltpu.make_async_remote_copy(
                    src_ref=partial.at[g, origin, mine],
                    dst_ref=arrived.at[g, slot, span(origin, rows)],
                    send_sem=sum_send,
                    recv_sem=sum_recv.at[g],
                    device_id={"ctx": piece},
                    device_id_type=MESH,
                ).start()

            return carry

        lax.fori_loop(0, 3, plane, 0)

    def stage(index, carry):
        distance, k = index // parts, lax.rem(index, parts)
        project_from(distance, k)
        piece = lax.rem(me + k, parts)
        line.pass_on(distance + 1, piece, 1)
        line.pass_on(distance + 1, piece, 0)

        @pl.when((distance == shards - 2) & ((place == 0) | (place == shards - 1)))
        def _():
            project_piece(shards - 1 - place, piece)

        return carry

    lax.fori_loop(0, (shards - 1) * parts, stage, 0)

    def summed(g, origin, where=slice(None)):
        value = partial[g, origin, span(me, rows), where].astype(jnp.float32)
        for k in range(parts - 1):
            value = value + arrived[g, k, span(origin, rows), where].astype(jnp.float32)
        return value

    for g in (1, 2):
        pltpu.make_async_copy(arrived.at[g], arrived.at[g], sum_recv.at[g]).wait()

    def write_product(step, carry):
        origin = shards - 1 - step
        product[span(origin, rows), :] = (summed(1, origin) * summed(2, origin)).astype(
            jnp.bfloat16
        )
        return carry

    tail_steps = -(-taps // rows)
    lax.fori_loop(0, tail_steps, write_product, 0)
    tail = pltpu.make_async_remote_copy(
        src_ref=product.at[pl.ds(all_rows - taps, taps)],
        dst_ref=before,
        send_sem=tail_send,
        recv_sem=tail_recv,
        device_id={"ctx": jnp.minimum(me + 1, parts - 1)},
        device_id_type=MESH,
    )

    @pl.when(me + 1 < parts)
    def _():
        tail.start()

    lax.fori_loop(tail_steps, shards, write_product, 0)
    @pl.when(me > 0)
    def _():
        tail.wait_recv()

    per, windows_count = LANES // GROUP, all_rows // taps

    def filter_lanes(block, carry):
        where = span(block, LANES)
        extended = jnp.concatenate([before[:, where], product[:, where]], axis=0)
        windows = jnp.concatenate(
            [extended[b * taps : (b + 2) * taps] for b in range(windows_count)], axis=1
        )
        lane = lax.broadcasted_iota(jnp.int32, windows.shape, 1)
        owner = lax.rem(lane, LANES) // GROUP
        sums = jnp.zeros((taps, windows_count * LANES), jnp.float32)
        for group in range(per):
            mine = jnp.where(owner == group, windows, jnp.zeros_like(windows))
            sums = sums + jnp.dot(
                bands[block * per + group], mine, preferred_element_type=jnp.float32
            )
        for b in range(windows_count):
            inner = pl.ds(b * taps, taps)
            direct = skip_ref[:, where] * product[inner, where].astype(jnp.float32)
            filtered[inner, where] = sums[:, b * LANES : (b + 1) * LANES] + direct
        return carry

    lax.fori_loop(0, channels // LANES, filter_lanes, 0)
    pltpu.make_async_copy(arrived.at[0], arrived.at[0], sum_recv.at[0]).wait()

    gated_line = Line(
        shards, chunks, lambda origin, c: gated.at[origin, c], gated_send, gated_recv
    )

    def gate_chunk(c, carry):
        where = span(c, chunk)

        def gate(origin, inner):
            mine = span(origin, rows)
            gated[place, c, mine, :] = (
                summed(0, origin, where) * filtered[mine, where]
            ).astype(jnp.bfloat16)
            return inner

        lax.fori_loop(0, shards, gate, 0)
        gated_line.send(place, c, 0)
        gated_line.send(place, c, 1)
        return carry

    lax.fori_loop(0, chunks, gate_chunk, 0)
    last_load.wait()
    wide = min(512, columns)

    def multiply(origin, c, fresh):
        deep = span(origin * chunks + c, chunk)

        def column(index, carry):
            where = span(index, wide)
            value = jnp.dot(
                gated[origin, c], weight[deep, where], preferred_element_type=jnp.float32
            )
            total[:, where] = value if fresh else total[:, where] + value
            return carry

        lax.fori_loop(0, columns // wide, column, 0)

    multiply(place, 0, True)

    def multiply_own(c, carry):
        multiply(place, c, False)
        return carry

    lax.fori_loop(1, chunks, multiply_own, 0)
    first_up = jnp.where(2 * place >= shards, 1, 0)

    def collect(index, carry):
        distance, side = index // (2 * chunks) + 1, lax.rem(index // chunks, 2)
        c = lax.rem(index, chunks)
        up = lax.rem(first_up + side, 2)
        gated_line.pass_on(distance, c, up)
        origin = place - distance * (2 * up - 1)

        @pl.when(gated_line.inside(origin))
        def _():
            multiply(jnp.clip(origin, 0, shards - 1), c, False)

        return carry

    lax.fori_loop(0, 2 * chunks * (shards - 1), collect, 0)
    out_ref[...] = total[...].astype(jnp.bfloat16)

    for swap in swaps:
        swap.wait_send()

    @pl.when(me + 1 < parts)
    def _():
        tail.wait_send()

    line.sent()
    gated_line.sent()
    pltpu.make_async_copy(arrived, arrived, sum_send).wait()


def paired_kernel(
    shards,
    hidden_in,
    gain_in,
    planes_ref,
    taps_in,
    decay_in,
    skip_in,
    tail_in,
    weight_ref,
    total,
    hidden_ref,
    gain_ref,
    taps_ref,
    decay_ref,
    skip_ref,
    tail_ref,
    normed,
    first,
    planes,
    slots,
    mine,
    outgoing,
    arrived,
    extended,
    filtered,
    bands,
    weight,
    gated,
    handed,
    input_sem,
    load_sem,
    own_sem,
    planes_send,
    planes_recv,
    swap_send,
    line_send,
    line_recv,
    pair_send,
    pair_recv,
    sum_send,
    sum_recv,
    tail_send,
    tail_recv,
    hand_send,
    hand_recv,
    gated_send,
    gated_recv,
):
    rows = hidden_ref.shape[0]
    parts = slots.shape[1] // rows
    _, both_depths, half = planes.shape
    depth = both_depths // 2
    _, taps, _ = bands.shape
    chunks, all_rows, chunk = gated.shape[1:]
    columns = total.shape[1]
    tile = min(256, half)
    tiles = half // tile
    me, place = lax.axis_index("ctx"), lax.axis_index("tensor")
    pair, core = me // 2, lax.rem(me, 2)
    across = 1 - pair
    outward = jnp.where(2 * place >= shards, 1, 0)
    sibling, peer = 2 * pair + 1 - core, 2 * across + core

    others = [lax.rem(me + 1 + k, parts) for k in range(parts - 1)]
    neighbours = [
        ("tensor", jnp.maximum(place - 1, 0), place > 0),
        ("tensor", jnp.minimum(place + 1, shards - 1), place < shards - 1),
    ]
    greeted = greet([("ctx", other, me >= 0) for other in others] + neighbours)
    inputs = [
        pltpu.make_async_copy(source, target, input_sem.at[k])
        for k, (source, target) in enumerate(
            [
                (hidden_in, hidden_ref),
                (gain_in, gain_ref),
                (taps_in, taps_ref),
                (decay_in, decay_ref),
                (skip_in, skip_ref),
                (tail_in, tail_ref),
            ]
        )
    ]
    for load in inputs:
        load.start()
    loads = [
        pltpu.make_async_copy(
            planes_ref.at[g, :, span(core, half)], planes.at[g, span(core, depth)], load_sem.at[g]
        )
        for g in (1, 2, 0)
    ]
    for load in loads:
        load.start()
    last_load = pltpu.make_async_copy(weight_ref, weight, load_sem.at[3])
    for load in inputs[:2]:
        load.wait()
    normalize_rows(hidden_ref, gain_ref, normed)
    mine_in = normed.at[:, span(pair, both_depths)]
    own = pltpu.make_async_copy(mine_in, slots.at[place, span(me, rows)], own_sem)
    own.start()
    pl.semaphore_wait(pltpu.get_barrier_semaphore(), greeted)

    def remote(source, target, send, recv, **device):
        return pltpu.make_async_remote_copy(
            src_ref=source,
            dst_ref=target,
            send_sem=send,
            recv_sem=recv,
            device_id=device,
            device_id_type=MESH,
        )

    line = Line(
        shards,
        parts,
        lambda origin, c: slots.at[origin, span(c, rows), span(core, depth)],
        line_send,
        line_recv,
    )
    line.send(place, me, 0, normed.at[:, span(me, depth)])
    line.send(place, me, 1, normed.at[:, span(me, depth)])
    to_sibling = remote(
        mine_in, slots.at[place, span(me, rows)], pair_send, pair_recv.at[place, me], ctx=sibling
    )
    to_sibling.start()
    swaps = [
        remote(
            normed.at[:, span(2 * across + k, depth)],
            slots.at[place, span(me, rows), pl.ds(k * depth, depth)],
            swap_send.at[k],
            line_recv.at[place, me],
            ctx=2 * across + k,
        )
        for k in range(2)
    ]
    swaps[0].start()
    shares = [
        remote(
            planes_ref.at[g, :, span(1 - core, half)],
            planes.at[g, span(core, depth)],
            planes_send,
            planes_recv.at[g],
            ctx=sibling,
        )
        for g in (1, 2, 0)
    ]
    for share in shares:
        share.start()

    def share_piece(origin, c):
        ref = slots.at[origin, span(c, rows), span(core, depth)]
        return remote(ref, ref, pair_send, pair_recv.at[origin, c], ctx=sibling)

    def from_sibling(origin, c):
        ref = slots.at[origin, span(c, rows), span(1 - core, depth)]
        return remote(ref, ref, pair_send, pair_recv.at[origin, c], ctx=sibling)

    for load in inputs[2:]:
        load.wait()
    first[...] = first_rows(taps_ref, decay_ref)

    @pl.when(pair == 0)
    def _():
        padding = jnp.zeros((taps - tail_ref.shape[0], half), jnp.float32)
        extended[pl.ds(0, taps), :] = jnp.concatenate(
            [padding, tail_ref[:, span(core, half)].astype(jnp.float32)], axis=0
        ).astype(jnp.bfloat16)

    remote(
        mine_in,
        slots.at[place, span(sibling, rows)],
        pair_send,
        pair_recv.at[place, sibling],
        ctx=sibling,
    ).wait_recv()
    line.send(place, sibling, 0)
    line.send(place, sibling, 1)

    def write_band(group, carry):
        row = jnp.broadcast_to(first[pl.ds(core * (half // GROUP) + group, 1), :], (taps, 2 * taps))
        bands[group] = pltpu.roll(row, 0, 1, stride=1, stride_axis=0).astype(jnp.bfloat16)
        return carry

    lax.fori_loop(0, half // GROUP, write_band, 0)
    swaps[0].wait_send()
    swaps[1].start()
    for k in range(2):
        c = 2 * across + k
        line.hop(place, c, 1).wait_recv()
        line.send(place, c, 0)
        line.send(place, c, 1)
        share_piece(place, c).start()
    own.wait()
    for load in loads:
        load.wait()
    for share in shares:
        share.wait_recv()
    last_load.start()

    def sum_piece(g, origin):
        where = span(origin, rows)
        return remote(
            outgoing.at[g, :, where],
            arrived.at[g, :, where],
            sum_send,
            sum_recv.at[g, origin],
            ctx=peer,
        )

    def group_of(far):
        return jnp.where(far == 1, across, pair)

    def project(origin, far):
        tokens = span(group_of(far), 2 * rows)

        def step(index, carry):
            g, column = lax.rem(index // tiles + 1, 3), lax.rem(index, tiles)
            where = span(column, tile)
            value = jnp.dot(
                slots[origin, tokens], planes[g, :, where], preferred_element_type=jnp.float32
            )

            def keep(target):
                for k in range(2):
                    target[g, k, span(origin, rows), where] = value[
                        k * rows : (k + 1) * rows
                    ].astype(target.dtype)

            @pl.when(far == 0)
            def _():
                keep(mine)

            @pl.when(far == 1)
            def _():
                keep(outgoing)

            @pl.when((far == 1) & (column == tiles - 1))
            def _():
                sum_piece(g, origin).start()

            return carry

        lax.fori_loop(0, 3 * tiles, step, 0)

    def combine(origin):
        where = span(origin, rows)
        for g in (1, 2, 0):
            sum_piece(g, origin).wait_recv()
        for k in range(2):
            q, key, value = [
                mine[g, k, where] + arrived[g, k, where].astype(jnp.float32) for g in range(3)
            ]
            mine[0, k, where] = q
            start = pl.multiple_of(taps + k * all_rows + origin * rows, rows)
            extended[pl.ds(start, rows), :] = (key * value).astype(jnp.bfloat16)

    def beside(distance, work):
        for origin in (place - distance, place + distance):

            @pl.when(line.inside(origin))
            def _(origin=origin):
                work(jnp.clip(origin, 0, shards - 1))

    def project_own(far, carry):
        @pl.when(far == 1)
        def _():
            for k in range(2):
                from_sibling(place, 2 * across + k).wait_recv()

        project(place, far)
        return carry

    lax.fori_loop(0, 2, project_own, 0)

    def from_side(distance, up):
        origin = place - distance * (2 * up - 1)
        return line.inside(origin), jnp.clip(origin, 0, shards - 1), origin == (1 - up) * (shards - 1)

    def far_at(distance, turn, last):
        return jnp.where(last & (distance > 1), 1 - turn, turn)

    def flow(distance, turn, up):
        there, origin, last = from_side(distance, up)
        held = last & (distance == 1)

        @pl.when(there)
        def _():
            group = group_of(far_at(distance, turn, last))
            for k in range(2):
                line.hop(origin, 2 * group + k, up).wait_recv()

                @pl.when(~held | (turn == 1))
                def _(k=k):
                    usual = jnp.where(held, pair, group_of(turn))
                    line.follow(origin, 2 * group + k, up, 2 * usual + k)

                share_piece(origin, 2 * group + k).start()

            @pl.when(held & (turn == 1))
            def _():
                for k in range(2):
                    line.follow(origin, 2 * pair + k, up, 2 * across + k)

    def project_side(distance, turn, up):
        there, origin, last = from_side(distance, up)

        @pl.when(there)
        def _():
            far = far_at(distance, turn, last)
            for k in range(2):
                from_sibling(origin, 2 * group_of(far) + k).wait_recv()
            project(origin, far)

    def stage(distance, carry):
        def half_stage(turn, inner):
            flow(distance, turn, outward)
            flow(distance, turn, 1 - outward)

            def side(up, nothing):
                project_side(distance, turn, up)
                return nothing

            lax.fori_loop(0, 2, side, 0)
            return inner

        lax.fori_loop(0, 2, half_stage, 0)

        @pl.when(distance == 1)
        def _():
            combine(place)

        @pl.when(distance > 1)
        def _():
            beside(distance - 1, combine)

        return carry

    lax.fori_loop(1, shards, stage, 0)
    beside(shards - 1, combine)
    before = extended.at[pl.ds(0, taps)]
    tail = remote(
        extended.at[pl.ds(2 * all_rows, taps)], before, tail_send, tail_recv, ctx=peer
    )

    @pl.when(pair == 0)
    def _():
        tail.start()

    per, windows_count = LANES // GROUP, all_rows // taps

    def filter_lanes(k, block):
        where = span(block, LANES)
        values = extended[pl.ds(k * all_rows, taps + all_rows), where]
        windows = jnp.concatenate(
            [values[b * taps : (b + 2) * taps] for b in range(windows_count)], axis=1
        )
        lane = lax.broadcasted_iota(jnp.int32, windows.shape, 1)
        owner = lax.rem(lane, LANES) // GROUP
        sums = jnp.zeros((taps, windows_count * LANES), jnp.float32)
        for group in range(per):
            some = jnp.where(owner == group, windows, jnp.zeros_like(windows))
            sums = sums + jnp.dot(
                bands[block * per + group], some, preferred_element_type=jnp.float32
            )
        skip = skip_ref[:, pl.ds(pl.multiple_of(core * half + block * LANES, LANES), LANES)]
        for b in range(windows_count):
            direct = skip * values[(b + 1) * taps : (b + 2) * taps].astype(jnp.float32)
            filtered[pl.ds(b * taps, taps), where] = sums[:, b * LANES : (b + 1) * LANES] + direct

    gated_line = Line(
        shards, chunks, lambda origin, c: gated.at[origin, c], gated_send, gated_recv
    )
    mine_chunks = half // chunk

    def hand(i, owner):
        c = owner * mine_chunks + i
        return remote(handed.at[i], gated.at[place, c], hand_send, hand_recv.at[i], ctx=sibling)

    inner_place = (place > 0) & (place < shards - 1)


    def send_gated(c):
        gated_line.send(place, c, 1 - outward)

        @pl.when(~inner_place)
        def _():
            gated_line.send(place, c, outward)

    def gate_half(step, carry):
        k = 1 - step

        @pl.when((k == 0) & (pair == 1))
        def _():
            tail.wait_recv()

        def gate_chunk(i, inner):
            def lanes(block, nothing):
                filter_lanes(k, block)
                return nothing

            per_chunk = chunk // LANES
            lax.fori_loop(i * per_chunk, (i + 1) * per_chunk, lanes, 0)
            where, c = span(i, chunk), core * mine_chunks + i
            value = (mine[0, k, :, where] * filtered[:, where]).astype(jnp.bfloat16)

            @pl.when(k == core)
            def _():
                gated[place, c] = value
                send_gated(c)

            @pl.when(k != core)
            def _():
                handed[i] = value
                hand(i, core).start()

            return inner

        lax.fori_loop(0, mine_chunks, gate_chunk, 0)
        return carry

    lax.fori_loop(0, 2, gate_half, 0)

    def take(i, carry):
        hand(i, 1 - core).wait_recv()
        send_gated((1 - core) * mine_chunks + i)
        return carry

    lax.fori_loop(0, mine_chunks, take, 0)
    line.last_sent()

    @pl.when(inner_place)
    def _():
        for i in range(chunks):
            gated_line.send(place, lax.rem(core * mine_chunks + i, chunks), outward)

    last_load.wait()
    wide = min(512, columns)

    def multiply(origin, c, fresh=False):
        deep = span(origin * chunks + c, chunk)
        for start in range(0, columns, wide):
            where = pl.ds(start, wide)
            value = jnp.dot(
                gated[origin, c], weight[deep, where], preferred_element_type=jnp.float32
            )
            total[:, where] = value if fresh else total[:, where] + value

    multiply(place, 0, True)

    def multiply_own(c, carry):
        multiply(place, c)
        return carry

    lax.fori_loop(1, chunks, multiply_own, 0)
    def collect(index, carry):
        distance, side = index // (2 * chunks) + 1, lax.rem(index // chunks, 2)
        step = lax.rem(index, chunks)
        c = lax.rem(step + core * mine_chunks, chunks)
        up = lax.rem(outward + side, 2)
        origin = place - distance * (2 * up - 1)

        @pl.when(gated_line.inside(origin))
        def _():
            source = jnp.clip(origin, 0, shards - 1)
            gated_line.hop(source, c, up).wait_recv()
            gated_line.follow(source, c, up, c)


        @pl.when(gated_line.inside(origin))
        def _():
            multiply(jnp.clip(origin, 0, shards - 1), c)

        return carry

    lax.fori_loop(0, 2 * chunks * (shards - 1), collect, 0)

    swaps[1].wait_send()

    @pl.when(pair == 0)
    def _():
        tail.wait_send()

    gated_line.last_sent()
    slices = slots.at[:, :, pl.ds(0, depth)]
    pltpu.make_async_copy(slices, slices, pair_send).wait()
    pltpu.make_async_copy(handed, handed, hand_send).wait()
    pltpu.make_async_copy(outgoing, outgoing, sum_send).wait()
    sent_planes = planes.at[:, pl.ds(0, depth)]
    pltpu.make_async_copy(sent_planes, sent_planes, planes_send).wait()


def on_paired_device(
    hidden_in, norm_gain, weight_in, filter_taps, filter_decay, skip_gain, tail_cache, output_weight
):
    shards, parts = lax.axis_size("tensor"), lax.axis_size("ctx")
    rows = hidden_in.shape[0]
    depth, _, channels = weight_in.shape
    groups, taps = filter_taps.shape
    columns = output_weight.shape[1]
    all_rows = shards * rows
    half = channels // 2
    chunk = min(256, half)
    chunks = channels // chunk
    anywhere = pl.BlockSpec(memory_space=pl.ANY)
    dma = pltpu.SemaphoreType.DMA
    bf16, f32 = jnp.bfloat16, jnp.float32
    total = pl.pallas_call(
        functools.partial(paired_kernel, shards),
        out_shape=pltpu.VMEM((all_rows, columns), f32),
        in_specs=[anywhere] * 8,
        out_specs=pl.BlockSpec(memory_space=pltpu.VMEM),
        scratch_shapes=[
            pltpu.VMEM(hidden_in.shape, bf16),
            pltpu.VMEM((1, norm_gain.shape[0]), f32),
            pltpu.VMEM(filter_taps.shape, f32),
            pltpu.VMEM((1, groups), f32),
            pltpu.VMEM((1, channels), f32),
            pltpu.VMEM(tail_cache.shape, bf16),
            pltpu.VMEM((rows, hidden_in.shape[1]), bf16),
            pltpu.VMEM((groups, 2 * taps), f32),
            pltpu.VMEM((3, 2 * depth, half), bf16),
            pltpu.VMEM((shards, parts * rows, 2 * depth), bf16),
            pltpu.VMEM((3, 2, all_rows, half), f32),
            pltpu.VMEM((3, 2, all_rows, half), bf16),
            pltpu.VMEM((3, 2, all_rows, half), bf16),
            pltpu.VMEM((taps + 2 * all_rows, half), bf16),
            pltpu.VMEM((all_rows, half), f32),
            pltpu.VMEM((groups // 2, taps, 2 * taps), bf16),
            pltpu.VMEM(output_weight.shape, bf16),
            pltpu.VMEM((shards, chunks, all_rows, chunk), bf16),
            pltpu.VMEM((chunks // 2, all_rows, chunk), bf16),
            dma((6,)),
            dma((4,)),
            dma,
            dma,
            dma((3,)),
            dma((2,)),
            dma((2, shards, parts)),
            dma((shards, parts)),
            dma,
            dma((shards, parts)),
            dma,
            dma((3, shards)),
            dma,
            dma,
            dma,
            dma((chunks // 2,)),
            dma((2, shards, chunks)),
            dma((shards, chunks)),
        ],
        compiler_params=pltpu.CompilerParams(
            collective_id=0, has_side_effects=True, vmem_limit_bytes=54 << 20
        ),
    )(
        hidden_in,
        norm_gain.reshape(1, norm_gain.shape[0]),
        weight_in.transpose(1, 0, 2),
        filter_taps,
        filter_decay.reshape(1, groups),
        skip_gain.reshape(1, channels),
        tail_cache,
        output_weight,
    )
    return total.astype(bf16)


def on_device(
    hidden_in, norm_gain, weight_in, filter_taps, filter_decay, skip_gain, tail_cache, output_weight
):
    shards, parts = lax.axis_size("tensor"), lax.axis_size("ctx")
    rows = hidden_in.shape[0]
    depth, _, channels = weight_in.shape
    groups, taps = filter_taps.shape
    columns = output_weight.shape[1]
    all_rows = shards * rows
    chunk = min(256, channels)
    chunks = channels // chunk
    vmem, anywhere = pl.BlockSpec(memory_space=pltpu.VMEM), pl.BlockSpec(memory_space=pl.ANY)
    dma = pltpu.SemaphoreType.DMA
    bf16, f32 = jnp.bfloat16, jnp.float32
    return pl.pallas_call(
        functools.partial(mixer_kernel, shards, parts),
        out_shape=jax.ShapeDtypeStruct((all_rows, columns), bf16),
        in_specs=[vmem, vmem, anywhere, vmem, vmem, vmem, vmem, anywhere],
        out_specs=vmem,
        scratch_shapes=[
            pltpu.VMEM((rows, hidden_in.shape[1]), bf16),
            pltpu.VMEM((groups, 2 * taps), f32),
            pltpu.VMEM((3, depth, channels), bf16),
            pltpu.VMEM((shards, parts * rows, depth), bf16),
            pltpu.VMEM((3, shards, parts * rows, channels), bf16),
            pltpu.VMEM((3, parts - 1, all_rows, channels), bf16),
            pltpu.VMEM((all_rows, channels), f32),
            pltpu.VMEM((all_rows, channels), bf16),
            pltpu.VMEM((taps, channels), bf16),
            pltpu.VMEM((groups, taps, 2 * taps), bf16),
            pltpu.VMEM(output_weight.shape, bf16),
            pltpu.VMEM((shards, chunks, all_rows, chunk), bf16),
            pltpu.VMEM((all_rows, columns), f32),
            dma((4,)),
            dma,
            dma((parts - 1,)),
            dma((parts - 1,)),
            dma((2, shards, parts)),
            dma((shards, parts)),
            dma,
            dma((3,)),
            dma,
            dma,
            dma((2, shards, chunks)),
            dma((shards, chunks)),
        ],
        compiler_params=pltpu.CompilerParams(
            collective_id=0, has_side_effects=True, vmem_limit_bytes=56 << 20
        ),
    )(
        hidden_in,
        norm_gain.reshape(1, norm_gain.shape[0]),
        weight_in.transpose(1, 0, 2),
        filter_taps,
        filter_decay.reshape(1, groups),
        skip_gain.reshape(1, channels),
        tail_cache,
        output_weight,
    )


def solution(mesh):
    in_specs = (
        P(("prompt", "ctx", "tensor"), None),
        P(),
        P("ctx", None, "tensor"),
        P("tensor", None),
        P("tensor"),
        P("tensor"),
        P("prompt", "tensor"),
        P(None, "tensor"),
    )
    out_specs = P(("prompt", "ctx"), "tensor")
    paired = mesh.shape["ctx"] == 4 and mesh.shape["tensor"] > 1
    return jax.shard_map(
        on_paired_device if paired else on_device, mesh=mesh, in_specs=in_specs, out_specs=out_specs, check_vma=False
    )
```
